32 devices in a mesh: gx: 4 (over x, core), gy: 8 (over z, y).
Axes of the slice: x: 2, y: 2, z: 4, core: 2. Of those that a mesh axis runs over, the one named last changes fastest.
Arguments:
- farm_velocity: float32 [3, 64, 64, 192], P(None, 'gx', 'gy'), may hold values from -6 to 6
- precursor_velocity: float32 [3, 64, 64, 192], P(None, 'gx', 'gy'), may hold values from -6 to 6
- turb_cell: int32 [4, 8, 256], P('gx', 'gy'), may hold values from 0 to 24575
- turb_slot: int32 [4, 8, 256], P('gx', 'gy'), may hold values from 0 to 15
- disk_mask: int32 [4, 8, 256], P('gx', 'gy'), may hold values 0 or 1
Outputs:
- farm_new: float32 [3, 64, 64, 192], P(None, 'gx', 'gy')
- precursor_new: float32 [3, 64, 64, 192], P(None, 'gx', 'gy')
The draws below stay inside these ranges and needn't reach their ends.
Inputs may be any that keep to these rules, and one draw needn't show every extreme that they name: `turb_cell`: the cell is (x * 8 + y) * 192 + z within the device's tile of 16 x 8 x 192 cells.
All inputs are finite; a program needn't handle non-finite values. No bound on the sum of `disk_mask` on one device may be relied on, other than what follows from the above.
Results may differ from the reference program's by a relative error of at most 0.0003.
Values sent between devices are 32-bit elements; how exact they have to be, the bound alone decides.
A program may use at most 64 MiB of HBM per device.

```python
import math
import jax
import jax.numpy as jnp
from jax import lax

CX = 16
CY = 8
NZ = 192
NF = 48
TURB = 16
SLOTS = 256
NX = 64
NY = 64
N_GX = 4
N_GY = 8


def plant(values, own_key, smallest, top_value):
    longest = values.shape.index(max(values.shape))
    spots = []
    for shift in (0, 1):
        where = [jax.random.randint(jax.random.fold_in(own_key, axis), (), 0, length) for axis, length in enumerate(values.shape)]
        where[longest] = (where[longest] + shift) % values.shape[longest]
        spots.append(tuple(where))
    return values.at[spots[0]].set(smallest).at[spots[1]].set(top_value)


def levels(stream_key, shape, split, low, top_value):
    def one(position, parts):
        steps = jax.random.uniform(jax.random.fold_in(jax.random.fold_in(stream_key, 6), position), (parts,), jnp.float32, low / len(split), top_value / len(split))
        return jnp.repeat(jnp.exp(steps), shape[position] // parts).reshape((-1,) + (1,) * (len(shape) - position - 1))

    level = one(*split[0])
    for cut in split[1:]:
        level = level * one(*cut)
    return level


def noise(key, shape, spread, most, split=(), held_as=jnp.bfloat16):
    values = jax.random.normal(key, shape, jnp.float32) * spread
    if len(split) > 0:
        values = levels(key, shape, split, -0.22, 0.18) * values
    return jnp.clip(values, min=-most, max=most).astype(held_as)


def setup_inputs(seed: int = 0) -> dict:
    key_list = jax.random.split(jax.random.key(seed), 6)
    return {
        "farm_velocity": noise(key_list[0], (3, NX, NY, NZ), 1.0, 6.0, ((1, 4), (2, 8)), jnp.float32),
        "precursor_velocity": noise(key_list[1], (3, NX, NY, NZ), 1.0, 6.0, ((1, 4), (2, 8)), jnp.float32),
        "turb_cell": plant(jax.random.randint(key_list[2], (N_GX, N_GY, SLOTS), 0, CX * CY * NZ), jax.random.fold_in(key_list[2], 1), 0, (CX * CY * NZ) - 1).astype(jnp.int32),
        "turb_slot": plant(jax.random.randint(key_list[3], (N_GX, N_GY, SLOTS), 0, TURB), jax.random.fold_in(key_list[3], 1), 0, TURB - 1).astype(jnp.int32),
        "disk_mask": plant((jax.random.randint(key_list[4], (N_GX, N_GY, SLOTS), 0, 4) < 1).astype(jnp.int32), jax.random.fold_in(key_list[4], 1), 0, 1),
    }


WIND = 3.0
STEP = 0.1
SMAG = 0.0289
THRUST = 1.33
DIFFUSE = 0.05
HIGH = lax.Precision.HIGHEST

def inner(arr, axis, start, length):
    out = arr
    for dim in range(3):
        place = out.ndim - 3 + dim
        extent = arr.shape[arr.ndim - 3 + dim]
        if dim == axis:
            out = lax.slice_in_dim(out, start, start + length, axis=place)
        else:
            out = lax.slice_in_dim(out, 1, extent - 1, axis=place)
    return out

def farm_tendency(ext):
    padded = jnp.pad(ext, ((0, 0), (0, 0), (0, 0), (2, 2)))
    cycle = padded[:, 1:-1, 1:-1, 1:-1]
    grads = []
    for axis in range(3):
        extent = padded.shape[1 + axis]
        grads.append(0.5 * (inner(padded, axis, 2, extent - 2) - inner(padded, axis, 0, extent - 2)))
    square = jnp.zeros(cycle.shape[1:], jnp.float32)
    for first in range(3):
        for second in range(3):
            strain = 0.5 * (grads[second][first] + grads[first][second])
            square = square + strain * strain
    eddy = SMAG * jnp.sqrt(2.0 * square)
    advect = cycle + jnp.array([WIND, 0.0, 0.0], jnp.float32)[:, None, None, None]
    total = jnp.zeros((3,) + tuple((n - 2 for n in cycle.shape[1:])), jnp.float32)
    for axis in range(3):
        extent = cycle.shape[1 + axis]
        low_f = inner(cycle, axis, 0, extent - 1)
        high_f = inner(cycle, axis, 1, extent - 1)
        low_v = inner(advect[axis], axis, 0, extent - 1)
        high_v = inner(advect[axis], axis, 1, extent - 1)
        low_e = inner(eddy, axis, 0, extent - 1)
        high_e = inner(eddy, axis, 1, extent - 1)
        flux = 0.25 * (low_v + high_v) * (low_f + high_f) - 0.5 * (low_e + high_e) * (high_f - low_f)
        faces = extent - 1
        change = lax.slice_in_dim(flux, 1, faces, axis=1 + axis) - lax.slice_in_dim(flux, 0, faces - 1, axis=1 + axis)
        total = total - change
    return total

def drag_tile(flat, cells, slots, live):
    values = flat[cells] + WIND
    onehot = jnp.where((slots[:, None] == jnp.arange(TURB, dtype=jnp.int32)[None, :]) & (live[:, None] == 1), 1.0, 0.0).astype(jnp.float32)
    sums = jnp.dot(values, onehot, precision=HIGH)
    counts = lax.optimization_barrier(jnp.sum(onehot, axis=0))
    mean = sums / jnp.maximum(counts, 1.0)
    thrust = -0.5 * THRUST * mean * jnp.abs(mean)
    per_slot = jnp.dot(onehot, thrust, precision=HIGH)
    return jnp.zeros(flat.shape, jnp.float32).at[cells].add(per_slot)

def farm_rate(field, cells, slots, live):
    padded = jnp.pad(field, ((0, 0), (2, 2), (2, 2), (0, 0)), mode='wrap')

    def tile_rate(index):
        block = lax.dynamic_slice_in_dim(padded, index * CX, CX + 4, axis=1)
        return farm_tendency(block)
    rates = lax.map(tile_rate, jnp.arange(N_GX, dtype=jnp.int32))
    rates = jnp.moveaxis(rates, 0, 1).reshape(3, NX, NY, NZ)
    tiles = field[0].reshape(N_GX, CX, N_GY, CY, NZ).transpose(0, 2, 1, 3, 4).reshape(N_GX, N_GY, CX * CY * NZ)
    forces = jax.vmap(jax.vmap(drag_tile))(tiles, cells, slots, live)
    forces = forces.reshape(N_GX, N_GY, CX, CY, NZ).transpose(0, 2, 1, 3, 4).reshape(NX, NY, NZ)
    return rates.at[0].add(forces)

def precursor_step(field):
    component = jnp.arange(3)[:, None, None, None]
    height = jnp.arange(NZ)[None, None, None, :]
    field = jnp.where((component == 2) & (height == NZ - 1), 0.0, field)
    spec = jnp.fft.rfft(field, axis=1)[:, :NX // 2]
    spec = jnp.fft.fft(spec, axis=2)
    yindex = jnp.arange(NY)
    spec = jnp.where((yindex == NY // 2)[None, None, :, None], 0.0, spec)
    kx = 2.0 * math.pi / NX * jnp.arange(NX // 2).astype(jnp.float32)
    ky = 2.0 * math.pi / NY * jnp.where(yindex < NY // 2, yindex, yindex - NY).astype(jnp.float32)
    kx = kx[:, None, None]
    ky = ky[None, :, None]
    hor = kx * kx + ky * ky
    u_hat, v_hat, w_hat = (spec[0], spec[1], spec[2])
    below = w_hat - jnp.pad(w_hat, ((0, 0), (0, 0), (1, 0)))[:, :, :-1]
    div = 1j * kx * u_hat + 1j * ky * v_hat + below
    level = jnp.arange(NZ)
    ends = jnp.where((level == 0) | (level == NZ - 1), -1.0, -2.0).astype(jnp.float32)
    pin = jnp.where((hor == 0.0) & (level == 0)[None, None, :], -1.0, 0.0).astype(jnp.float32)
    diag = ends[None, None, :] - hor + pin
    lower = jnp.broadcast_to(jnp.where(level == 0, 0.0, 1.0).astype(jnp.float32), diag.shape)
    upper = jnp.broadcast_to(jnp.where(level == NZ - 1, 0.0, 1.0).astype(jnp.float32), diag.shape)
    rhs = jnp.stack([jnp.real(div), jnp.imag(div)], axis=-1)
    solved = lax.linalg.tridiagonal_solve(lower, diag, upper, rhs)
    press = solved[..., 0] + 1j * solved[..., 1]
    grad = jnp.pad(press, ((0, 0), (0, 0), (0, 1)))[:, :, 1:] - press
    grad = jnp.where((level == NZ - 1)[None, None, :], 0.0, grad)
    decay = jnp.exp(-DIFFUSE * hor)
    u_hat = (u_hat - 1j * kx * press) * decay
    v_hat = (v_hat - 1j * ky * press) * decay
    w_hat = (w_hat - grad) * decay
    spec = jnp.stack([u_hat, v_hat, w_hat])
    spec = jnp.fft.ifft(spec, axis=2)
    spec = jnp.pad(spec, ((0, 0), (0, 1), (0, 0), (0, 0)))
    return jnp.fft.irfft(spec, n=NX, axis=1).astype(jnp.float32)

def reference(farm_velocity, precursor_velocity, turb_cell, turb_slot, disk_mask):
    precursor_new = precursor_step(precursor_velocity)
    state = farm_velocity.at[:, :NF].set(precursor_new[:, NX - NF:])
    section_one = state + STEP * farm_rate(state, turb_cell, turb_slot, disk_mask)
    section_two = 0.75 * state + 0.25 * (section_one + STEP * farm_rate(section_one, turb_cell, turb_slot, disk_mask))
    farm_new = state / 3.0 + 2.0 / 3.0 * (section_two + STEP * farm_rate(section_two, turb_cell, turb_slot, disk_mask))
    return (farm_new, precursor_new)
```

```python
import functools
import math

import jax
import jax.numpy as jnp
import numpy as np
from jax import lax
from jax.experimental import pallas as pl
from jax.experimental.pallas import tpu as pltpu
from jax.sharding import PartitionSpec as P

NF = 48
TURB = 16
WIND = 3.0
STEP = 0.1
SMAG = 0.0289
THRUST = 1.33
DIFFUSE = 0.05
MESH = pl.DeviceIdType.MESH
CHUNKS = 2


def split_pair(table):
    table = np.asarray(table, np.float32)
    head = table.astype(jnp.bfloat16)
    tail = (table - head.astype(np.float32)).astype(jnp.bfloat16)
    return np.stack([head, tail])


def stacked(table):
    head, tail = split_pair(table)
    return np.concatenate([head, tail, head], axis=1)


def spectral_tables(across, spanwise, width, depth, levels, lanes):
    count = across * spanwise
    total_x, total_y = across * width, spanwise * depth
    groups = -(-levels // count)
    order = np.arange(groups * count)[:, None]
    height = np.arange(levels)[None, :]
    inside = order < levels
    scale = np.where(order == 0, math.sqrt(1.0 / levels), math.sqrt(2.0 / levels)) * inside
    centre = scale * np.cos(math.pi / (2 * levels) * (order * (2 * height + 1) % (4 * levels)))
    face = (
        math.sqrt(2.0 / levels)
        * np.sin(math.pi / levels * (order * (height + 1) % (2 * levels)))
        * ((height < levels - 1) & (order > 0) & inside)
    )
    pad = ((0, 0), (0, 0), (0, lanes - levels))
    vertical = np.stack([np.pad(split_pair(centre), pad), np.pad(split_pair(face), pad)])
    rise = 2.0 * np.sin(np.minimum(order, levels)[:, 0] * (math.pi / (2 * levels)))
    rise = np.pad(rise.reshape(groups, count).T, ((0, 0), (0, -groups % 8)))
    rise = np.broadcast_to(rise[:, :, None], rise.shape + (128,))
    tile = np.arange(count)
    tile_x, tile_y = tile // spanwise, tile % spanwise
    turn = 2.0 * math.pi * (np.outer(tile_x, tile_x) / across + np.outer(tile_y, tile_y) / spanwise)
    outer = np.concatenate([np.cos(turn), -np.sin(turn)], axis=0)
    outer_back = np.concatenate([np.cos(turn), -np.sin(turn)], axis=1)
    lane = np.arange(width * depth)
    lane_x, lane_y = lane // depth, lane % depth
    back = (lane % width) * depth + lane // width
    angle = 2.0 * math.pi * (np.outer(tile_x, lane_x) / total_x + np.outer(tile_y, lane_y) / total_y)
    twist = np.stack([np.cos(angle), -np.sin(angle), np.cos(angle)[:, back], -np.sin(angle)[:, back]])
    turn = 2.0 * math.pi * (np.outer(lane_x, lane_x) / width + np.outer(lane_y, lane_y) / depth)
    real, imag = np.cos(turn), np.sin(turn)
    inner_forward = np.block([[real, -imag], [imag, real]])
    real, imag = real[:, back], imag[:, back]
    inner_back = np.block([[real, imag], [-imag, real]])
    k = tile_x[:, None] + across * lane_x[None, :]
    q = tile_y[:, None] + spanwise * lane_y[None, :]
    kx = 2.0 * math.pi / total_x * np.where(k < total_x // 2, k, k - total_x)
    ky = 2.0 * math.pi / total_y * np.where(q < total_y // 2, q, q - total_y)
    hor = kx * kx + ky * ky
    kept = (k != total_x // 2) & (q != total_y // 2)
    decay = np.exp(-DIFFUSE * hor) * kept / (total_x * total_y)
    waves = np.stack([kx, ky, hor, decay])
    return (
        vertical,
        stacked(outer),
        stacked(outer_back),
        split_pair(inner_forward),
        split_pair(inner_back),
        twist.astype(np.float32),
        waves.astype(np.float32),
        rise.astype(np.float32),
    )


def halves(value):
    head = value.astype(jnp.bfloat16)
    return head, (value - head.astype(jnp.float32)).astype(jnp.bfloat16)


def dot(left, right, dims=((1,), (0,))):
    return lax.dot_general(
        left, right, dimension_numbers=(dims, ((), ())), preferred_element_type=jnp.float32
    )


def product(left, right, dims=((1,), (0,))):
    return dot(left[0], right[0], dims) + (dot(left[0], right[1], dims) + dot(left[1], right[0], dims))


def step_body(
    across, spanwise, pre, farm, cell, slot, live, vertical, outer, outer_back, inner_f, inner_b,
    twist, waves, rise, farm_new, pre_new,
    pre_v, farm_v, turb_v, vert_v, outer_v, outerb_v, innf_v, innb_v, twist_v, waves_v, rise_v,
    send, recv, send_two, recv_two, fringe, own, stage_one, stage_two, stage_three, eddy, force,
    where_row, where_lev, where_turb, load_sem, a2a_send, a2a_recv, shift_send, shift_recv,
    halo_send, halo_recv, out_sem,
):
    count = across * spanwise
    comps, width, depth, levels = farm.shape
    area = width * depth
    lanes = fringe.shape[-1]
    rows = width + 8
    groups = send.shape[0] // comps
    shift = across - NF // width
    filled = NF // width
    row, column = lax.axis_index("gx"), lax.axis_index("gy")
    position = row * spanwise + column
    barrier = pltpu.get_barrier_semaphore()

    @pl.loop(1, count)
    def _(step):
        peer = (position + step) % count
        pl.semaphore_signal(
            barrier, inc=1, device_id=(peer // spanwise, peer % spanwise), device_id_type=MESH
        )

    loads = [pltpu.make_async_copy(vertical, vert_v, load_sem.at[0])]
    for comp in range(comps):
        loads.append(pltpu.make_async_copy(pre.at[comp], pre_v.at[comp], load_sem.at[1 + comp]))
    early = len(loads)
    for index, (source, target) in enumerate((
        (outer, outer_v), (outer_back, outerb_v), (inner_f, innf_v), (inner_b, innb_v),
        (twist, twist_v), (waves, waves_v), (rise.at[position], rise_v),
        (cell, turb_v.at[0]), (slot, turb_v.at[1]), (live, turb_v.at[2]),
    )):
        loads.append(pltpu.make_async_copy(source, target, load_sem.at[early + index]))
    tables = len(loads)
    for y in range(depth):
        loads.append(pltpu.make_async_copy(farm.at[:, :, y], farm_v.at[:, y], load_sem.at[tables + y]))
    for copy in loads:
        copy.start()

    loads[0].wait()
    last = ((1,), (1,))
    for comp in range(comps):
        loads[1 + comp].wait()
        kind = comp // 2
        table = (vert_v[kind, 0][:, :levels], vert_v[kind, 1][:, :levels])
        modes = product(table, halves(pre_v[comp]), last)
        for group in range(groups):
            send[group * comps + comp] = modes[group * count : (group + 1) * count]

    chunks = []
    size = -(-groups // CHUNKS)
    for start in range(0, groups, size):
        chunks.append((start, min(groups, start + size)))

    def spread(leg, index, source, target):
        low, high = chunks[index]
        part = pl.ds(low * comps, (high - low) * comps)

        @pl.loop(1, count)
        def _(step):
            peer = (position + step) % count
            pltpu.make_async_remote_copy(
                src_ref=source.at[part, peer],
                dst_ref=target.at[part, position],
                send_sem=a2a_send.at[leg, index],
                recv_sem=a2a_recv.at[leg, index],
                device_id=(peer // spanwise, peer % spanwise),
                device_id_type=MESH,
            ).start()

        pltpu.make_async_copy(
            source.at[part, position], target.at[part, position], a2a_recv.at[leg, index]
        ).start()

    def gathered(leg, index, target):
        low, high = chunks[index]
        part = target.at[pl.ds(low * comps, (high - low) * comps)]
        pltpu.make_async_copy(part, part, a2a_recv.at[leg, index]).wait()

    def sent(leg, index, source):
        low, high = chunks[index]
        part = source.at[pl.ds(low * comps, (high - low) * comps), pl.ds(0, count - 1)]
        pltpu.make_async_copy(part, part, a2a_send.at[leg, index]).wait()

    pl.semaphore_wait(barrier, count - 1)
    for index in range(len(chunks)):
        spread(0, index, send, recv)

    pieces = [
        (0, 0, pl.ds(0, depth), pl.ds(0, width), pl.ds(2, depth), pl.ds(0, width)),
        (0, 1, pl.ds(depth - 2, 2), pl.ds(0, width), pl.ds(0, 2), pl.ds(0, width)),
        (0, -1, pl.ds(0, 2), pl.ds(0, width), pl.ds(depth + 2, 2), pl.ds(0, width)),
        (1, 1, depth - 1, pl.ds(width - 1, 1), 1, pl.ds(width + 7, 1)),
        (-1, 1, depth - 1, pl.ds(0, 1), 1, pl.ds(width, 1)),
        (1, -1, 0, pl.ds(width - 1, 1), depth + 2, pl.ds(width + 7, 1)),
        (-1, -1, 0, pl.ds(0, 1), depth + 2, pl.ds(width, 1)),
        (1, 0, pl.ds(0, depth), pl.ds(width - 2, 2), pl.ds(2, depth), pl.ds(width + 6, 2)),
        (-1, 0, pl.ds(0, depth), pl.ds(0, 2), pl.ds(2, depth), pl.ds(width, 2)),
    ]

    def moved(at):
        return at + 2 if isinstance(at, int) else pl.ds(at.start + 2, at.size)

    def transfer(source, target, step_row, step_col, send_sem, recv_sem):
        if step_row % across == 0 and step_col % spanwise == 0:
            return pltpu.make_async_copy(source, target, recv_sem), False
        copy = pltpu.make_async_remote_copy(
            src_ref=source, dst_ref=target, send_sem=send_sem, recv_sem=recv_sem,
            device_id=((row + step_row) % across, (column + step_col) % spanwise),
            device_id_type=MESH,
        )
        return copy, True

    def tile_copies(source, role, comp, offset, kinds):
        out = []
        for kind in kinds:
            step_row, step_col, sy, sx, ty, tx = pieces[kind]
            out.append(transfer(
                source.at[comp, sy, sx], stage_one.at[comp, ty, tx], step_row + offset, step_col,
                shift_send.at[role, kind, comp], shift_recv.at[kind, comp],
            ))
        return out

    for copy in loads[tables:]:
        copy.wait()
    blank = jnp.zeros((width, lanes - 128), jnp.float32)

    @pl.when(row >= filled)
    def _():
        for comp in range(comps):
            for y in range(depth):
                own[comp, y, :, 128:] = blank
                own[comp, y, :, :levels] = farm_v[comp, y]
                stage_one[comp, 2 + y, :width] = own[comp, y]
            for copy, _ in tile_copies(own, 1, comp, 0, range(1, 9)):
                copy.start()

    for copy in loads[early:tables]:
        copy.wait()
    index = turb_v[0].astype(jnp.float32)
    line = jnp.floor((index + 0.5) * (1.0 / levels))
    level = index - levels * line
    at_x = jnp.floor((line + 0.5) * (1.0 / depth))
    line = (line - depth * at_x) * width + at_x
    slots = index.shape[-1]

    def hot(size, value):
        steps = lax.broadcasted_iota(jnp.int32, (size, slots), 0).astype(jnp.float32)
        return jnp.where(steps == value, 1.0, 0.0)

    where_row[...] = hot(area, line)
    where_lev[...] = hot(lanes, level).astype(jnp.bfloat16)
    turbine = jnp.where(turb_v[2] == 1, turb_v[1], TURB).astype(jnp.float32)
    where_turb[...] = hot(TURB, turbine)

    kx, ky, hor, decay = waves_v[0], waves_v[1], waves_v[2], waves_v[3]

    def project(chunk):
        low, high = chunk
        table = outer_v[...]
        cos, sin = twist_v[0], twist_v[1]
        blocks = []
        for place in range(low * comps, high * comps):
            head, tail = halves(recv[place])
            spun = dot(table, jnp.concatenate([head, head, tail], axis=0))
            real, imag = spun[:count], spun[count:]
            blocks.append(jnp.concatenate([real * cos - imag * sin, real * sin + imag * cos], axis=1))
        spec = product(halves(jnp.concatenate(blocks, axis=0)), (innf_v[0], innf_v[1]))
        blocks = []
        for group in range(low, high):
            lift = rise_v[pl.ds(group, 1), :area]
            real, imag = [], []
            for comp in range(comps):
                start = ((group - low) * comps + comp) * count
                real.append(spec[start : start + count, :area])
                imag.append(spec[start : start + count, area:])
            bound = hor + lift * lift
            inverse = jnp.where(bound > 0.0, -1.0 / jnp.where(bound > 0.0, bound, 1.0), 0.0)
            press_re = (lift * real[2] - kx * imag[0] - ky * imag[1]) * inverse
            press_im = (kx * real[0] + ky * real[1] + lift * imag[2]) * inverse
            new_re = [real[0] + kx * press_im, real[1] + ky * press_im, real[2] + lift * press_re]
            new_im = [imag[0] - kx * press_re, imag[1] - ky * press_re, imag[2] + lift * press_im]
            for comp in range(comps):
                blocks.append(jnp.concatenate([new_re[comp] * decay, new_im[comp] * decay], axis=1))
        lines = product(halves(jnp.concatenate(blocks, axis=0)), (innb_v[0], innb_v[1]))
        table = outerb_v[...]
        cos, sin = twist_v[2], twist_v[3]
        for place in range((high - low) * comps):
            real = lines[place * count : (place + 1) * count, :area]
            imag = lines[place * count : (place + 1) * count, area:]
            spun = jnp.concatenate([real * cos + imag * sin, imag * cos - real * sin], axis=0)
            head, tail = halves(spun)
            send_two[low * comps + place] = dot(table, jnp.concatenate([head, head, tail], axis=0))

    for index, chunk in enumerate(chunks):
        gathered(0, index, recv)
        project(chunk)
        spread(1, index, send_two, recv_two)

    outs = []
    for index, (low, high) in enumerate(chunks):
        gathered(1, index, recv_two)
        for comp in range(comps):
            modes = jnp.concatenate([recv_two[g * comps + comp] for g in range(low, high)], axis=0)
            kind = comp // 2
            span = slice(low * count, high * count)
            value = product(halves(modes.T), (vert_v[kind, 0, span], vert_v[kind, 1, span]))
            value = value.reshape(depth, width, lanes)
            if index > 0:
                value = value + fringe[comp]
            fringe[comp] = value
            if index == len(chunks) - 1:
                @pl.when(row >= shift)
                def _():
                    for copy, _ in tile_copies(fringe, 0, comp, -shift, (1, 2, 3, 4, 5, 6, 0, 7, 8)):
                        copy.start()

                farm_v[comp] = value[:, :, :levels]
                for y in range(depth):
                    copy = pltpu.make_async_copy(
                        farm_v.at[comp, y], pre_new.at[comp, :, y], out_sem.at[0, comp, y]
                    )
                    copy.start()
                    outs.append(copy)

    inside = lax.broadcasted_iota(jnp.int32, (width, lanes), 1) < levels
    late = (1, 2, 3, 4, 5, 6)
    soon = (7, 8)

    def received(kinds, stage, target):
        for kind in kinds:
            _, _, _, _, ty, tx = pieces[kind]
            if stage == 0:
                for comp in range(comps):
                    part = target.at[comp, ty, tx]
                    pltpu.make_async_copy(part, part, shift_recv.at[kind, comp]).wait()
            else:
                part = target.at[:, ty, tx]
                pltpu.make_async_copy(part, part, halo_recv.at[stage - 1, kind]).wait()

    def drag(field):
        cells = field[0, 2 : depth + 2, :width].reshape(area, lanes)
        head, tail = halves(cells)
        table = where_lev[...]
        picked = (dot(head, table) + dot(tail, table)) * where_row[...]
        values = jnp.sum(picked, axis=0, keepdims=True) + WIND
        turbs = where_turb[...]
        sums = jnp.sum(turbs * values, axis=1, keepdims=True)
        counts = jnp.sum(turbs, axis=1, keepdims=True)
        mean = sums / jnp.maximum(counts, 1.0)
        thrust = (-0.5 * THRUST * STEP) * mean * jnp.abs(mean)
        per_slot = jnp.sum(turbs * thrust, axis=0, keepdims=True)
        head, tail = halves(where_row[...] * per_slot)
        last = ((1,), (1,))
        force[...] = (dot(head, table, last) + dot(tail, table, last)).reshape(depth, width, lanes)

    def ahead(value, axis):
        return pltpu.roll(value, value.shape[axis] - 1, axis)

    def behind(value, axis):
        return pltpu.roll(value, 1, axis)

    def eddy_slab(field, j):
        along, across_y, up = [], [], []
        for comp in range(comps):
            value = field[comp, j]
            along.append(ahead(value, 0) - behind(value, 0))
            across_y.append(field[comp, j + 1] - field[comp, j - 1])
            up.append(ahead(value, 1) - behind(value, 1))
        square = along[0] * along[0] + across_y[1] * across_y[1] + up[2] * up[2]
        for pair in (along[1] + across_y[0], along[2] + up[0], across_y[2] + up[1]):
            square = square + 0.5 * (pair * pair)
        eddy[j - 1] = (0.5 * STEP * SMAG * math.sqrt(0.5)) * jnp.sqrt(square)

    def flux(speed, low_f, high_f, low_h, high_h):
        return speed * (low_f + high_f) - (low_h + high_h) * (high_f - low_f)

    quarter = 0.25 * STEP

    def span_flux(field, j):
        speed = quarter * (field[1, j, :width] + field[1, j + 1, :width])
        return tuple(
            flux(speed, field[comp, j, :width], field[comp, j + 1, :width], eddy[j - 1, :width], eddy[j, :width])
            for comp in range(comps)
        )

    def rates(field, low, high, store):
        def slab(j, below):
            above = span_flux(field, j)
            viscous = eddy[j - 1]
            beyond = ahead(viscous, 0)
            whole = field[0, j]
            next_u = ahead(whole, 0)
            speed = quarter * (whole + next_u) + (2.0 * quarter * WIND)
            inner_h = viscous[:width]
            upper_h = ahead(inner_h, 1)
            lift = field[2, j, :width]
            rising = quarter * (lift + ahead(lift, 1))
            for comp in range(comps):
                value = field[comp, j]
                face = flux(speed, value, next_u if comp == 0 else ahead(value, 0), viscous, beyond)
                total = (face - behind(face, 0))[:width] + (above[comp] - below[comp])
                mid = value[:width]
                face = flux(rising, mid, ahead(mid, 1), inner_h, upper_h)
                total = total + (face - behind(face, 1))
                change = force[j - 2] - total if comp == 0 else -total
                store(comp, j, mid + change)
            return above

        lax.fori_loop(low + 2, high + 2, slab, span_flux(field, low + 1))

    def section(stage, field, store):
        if stage == 0:
            @pl.when(row < filled)
            def _():
                received((0,), 0, field)
        drag(field)
        received(soon, stage, field)

        @pl.loop(3, depth + 1)
        def _(j):
            eddy_slab(field, j)

        rates(field, 2, depth - 2, store)
        received(late, stage, field)
        for j in (1, 2, depth + 1, depth + 2):
            eddy_slab(field, j)
        rates(field, 0, 2, store)
        rates(field, depth - 2, depth, store)

    def to_next(target, share):
        def store(comp, j, value):
            if share < 1.0:
                value = (1.0 - share) * stage_one[comp, j, :width] + share * value
            target[comp, j, :width] = jnp.where(inside, value, 0.0)
        return store

    def halo_copies(field, stage):
        out = []
        for kind in range(1, 9):
            step_row, step_col, sy, sx, ty, tx = pieces[kind]
            out.append(transfer(
                field.at[:, moved(sy), sx], field.at[:, ty, tx], step_row, step_col,
                halo_send.at[stage - 1, kind], halo_recv.at[stage - 1, kind],
            ))
        return out

    def to_output(comp, j, value):
        value = stage_one[comp, j, :width] * (1.0 / 3.0) + (2.0 / 3.0) * value
        farm_v[comp, j - 2] = value[:, :levels]

    section(0, stage_one, to_next(stage_two, 1.0))
    first = halo_copies(stage_two, 1)
    for copy, _ in first:
        copy.start()
    section(1, stage_two, to_next(stage_three, 0.25))
    second = halo_copies(stage_three, 2)
    for copy, _ in second:
        copy.start()
    for copy in outs:
        copy.wait()
    section(2, stage_three, to_output)
    outs = []
    for y in range(depth):
        copy = pltpu.make_async_copy(farm_v.at[:, y], farm_new.at[:, :, y], out_sem.at[1, 0, y])
        copy.start()
        outs.append(copy)

    for index in range(len(chunks)):
        sent(0, index, send)
        sent(1, index, send_two)
    for copy, remote in first + second:
        if remote:
            copy.wait_send()

    @pl.when(row >= shift)
    def _():
        for comp in range(comps):
            for copy, remote in tile_copies(fringe, 0, comp, -shift, range(9)):
                if remote:
                    copy.wait_send()

    @pl.when(row >= filled)
    def _():
        for comp in range(comps):
            for copy, remote in tile_copies(own, 1, comp, 0, range(1, 9)):
                if remote:
                    copy.wait_send()

    for copy in outs:
        copy.wait()


def shards(across, spanwise, farm, pre, turb_cell, turb_slot, disk_mask):
    comps, width, depth, levels = pre.shape
    count = across * spanwise
    area = width * depth
    slots = turb_cell.shape[-1]
    lanes = -(-(levels + 2) // 128) * 128
    groups = -(-levels // count)
    tables = [jnp.asarray(t) for t in spectral_tables(across, spanwise, width, depth, levels, lanes)]
    anywhere = pl.BlockSpec(memory_space=pl.ANY)
    f32 = jnp.float32

    def vmem(*shape, dtype=f32):
        return pltpu.VMEM(shape, dtype)

    def sems(*shape):
        return pltpu.SemaphoreType.DMA(shape)

    modes = vmem(groups * comps, count, area)
    cells = vmem(comps, depth, width, lanes)
    padded = vmem(comps, depth + 4, width + 8, lanes)
    return pl.pallas_call(
        functools.partial(step_body, across, spanwise),
        out_shape=[jax.ShapeDtypeStruct(farm.shape, f32), jax.ShapeDtypeStruct(pre.shape, f32)],
        in_specs=[anywhere] * (5 + len(tables)),
        out_specs=[anywhere] * 2,
        scratch_shapes=[
            vmem(comps, area, levels),
            vmem(comps, depth, width, levels),
            vmem(3, 1, slots, dtype=jnp.int32),
            *[vmem(*t.shape, dtype=t.dtype) for t in tables[:-1]],
            vmem(*tables[-1].shape[1:]),
            modes, modes, modes, modes,
            cells, cells, padded, padded, padded,
            vmem(depth + 2, width + 8, lanes),
            vmem(depth, width, lanes),
            vmem(area, slots),
            vmem(lanes, slots, dtype=jnp.bfloat16),
            vmem(TURB, slots),
            sems(4 + 10 + depth),
            sems(2, CHUNKS),
            sems(2, CHUNKS),
            sems(2, 9, comps),
            sems(9, comps),
            sems(2, 9),
            sems(2, 9),
            sems(2, comps, depth),
        ],
        compiler_params=pltpu.CompilerParams(collective_id=0, has_side_effects=True),
        name="step",
    )(
        pre.reshape(comps, area, levels), farm,
        turb_cell.reshape(1, slots), turb_slot.reshape(1, slots), disk_mask.reshape(1, slots),
        *tables,
    )


def solution(mesh):
    across, spanwise = mesh.shape["gx"], mesh.shape["gy"]
    return jax.shard_map(
        functools.partial(shards, across, spanwise),
        mesh=mesh,
        in_specs=(
            P(None, "gx", "gy", None),
            P(None, "gx", "gy", None),
            P("gx", "gy", None),
            P("gx", "gy", None),
            P("gx", "gy", None),
        ),
        out_specs=(P(None, "gx", "gy", None), P(None, "gx", "gy", None)),
        check_vma=False,
    )
```

```python
import functools
import math

import jax
import jax.numpy as jnp
import numpy as np
from jax import lax
from jax.experimental import pallas as pl
from jax.experimental.pallas import tpu as pltpu
from jax.sharding import PartitionSpec as P

NF = 48
TURB = 16
WIND = 3.0
STEP = 0.1
SMAG = 0.0289
THRUST = 1.33
DIFFUSE = 0.05
MESH = pl.DeviceIdType.MESH
CHUNKS = 3


def split_pair(table):
    table = np.asarray(table, np.float32)
    head = table.astype(jnp.bfloat16)
    tail = (table - head.astype(np.float32)).astype(jnp.bfloat16)
    return np.stack([head, tail])


def stacked(table):
    head, tail = split_pair(table)
    return np.concatenate([head, tail, head], axis=1)


def spectral_tables(across, spanwise, width, depth, levels, lanes):
    count = across * spanwise
    total_x, total_y = across * width, spanwise * depth
    groups = -(-levels // count)
    order = np.arange(groups * count)[:, None]
    height = np.arange(levels)[None, :]
    inside = order < levels
    scale = np.where(order == 0, math.sqrt(1.0 / levels), math.sqrt(2.0 / levels)) * inside
    centre = scale * np.cos(math.pi / (2 * levels) * (order * (2 * height + 1) % (4 * levels)))
    face = (
        math.sqrt(2.0 / levels)
        * np.sin(math.pi / levels * (order * (height + 1) % (2 * levels)))
        * ((height < levels - 1) & (order > 0) & inside)
    )
    pad = ((0, 0), (0, 0), (0, lanes - levels))
    vertical = np.stack([np.pad(split_pair(centre), pad), np.pad(split_pair(face), pad)])
    rise = 2.0 * np.sin(np.minimum(order, levels)[:, 0] * (math.pi / (2 * levels)))
    rise = np.pad(rise.reshape(groups, count).T, ((0, 0), (0, -groups % 8)))
    rise = np.broadcast_to(rise[:, :, None], rise.shape + (128,))
    tile = np.arange(count)
    tile_x, tile_y = tile // spanwise, tile % spanwise
    turn = 2.0 * math.pi * (np.outer(tile_x, tile_x) / across + np.outer(tile_y, tile_y) / spanwise)
    outer = np.concatenate([np.cos(turn), -np.sin(turn)], axis=0)
    outer_back = np.concatenate([np.cos(turn), -np.sin(turn)], axis=1)
    lane = np.arange(width * depth)
    lane_x, lane_y = lane // depth, lane % depth
    back = (lane % width) * depth + lane // width
    angle = 2.0 * math.pi * (np.outer(tile_x, lane_x) / total_x + np.outer(tile_y, lane_y) / total_y)
    twist = np.stack([np.cos(angle), -np.sin(angle), np.cos(angle)[:, back], -np.sin(angle)[:, back]])
    turn = 2.0 * math.pi * (np.outer(lane_x, lane_x) / width + np.outer(lane_y, lane_y) / depth)
    real, imag = np.cos(turn), np.sin(turn)
    inner_forward = np.block([[real, -imag], [imag, real]])
    real, imag = real[:, back], imag[:, back]
    inner_back = np.block([[real, imag], [-imag, real]])
    k = tile_x[:, None] + across * lane_x[None, :]
    q = tile_y[:, None] + spanwise * lane_y[None, :]
    kx = 2.0 * math.pi / total_x * np.where(k < total_x // 2, k, k - total_x)
    ky = 2.0 * math.pi / total_y * np.where(q < total_y // 2, q, q - total_y)
    hor = kx * kx + ky * ky
    kept = (k != total_x // 2) & (q != total_y // 2)
    decay = np.exp(-DIFFUSE * hor) * kept / (total_x * total_y)
    waves = np.stack([kx, ky, hor, decay])
    return (
        vertical,
        stacked(outer),
        stacked(outer_back),
        split_pair(inner_forward),
        split_pair(inner_back),
        twist.astype(np.float32),
        waves.astype(np.float32),
        rise.astype(np.float32),
    )


def halves(value):
    head = value.astype(jnp.bfloat16)
    return head, (value - head.astype(jnp.float32)).astype(jnp.bfloat16)


def dot(left, right, dims=((1,), (0,))):
    return lax.dot_general(
        left, right, dimension_numbers=(dims, ((), ())), preferred_element_type=jnp.float32
    )


def product(left, right, dims=((1,), (0,))):
    return dot(left[0], right[0], dims) + (dot(left[0], right[1], dims) + dot(left[1], right[0], dims))


def step_body(
    across, spanwise, pre, farm, cell, slot, live, vertical, outer, outer_back, inner_f, inner_b,
    twist, waves, rise, farm_new, pre_new,
    pre_v, farm_v, turb_v, vert_v, outer_v, outerb_v, innf_v, innb_v, twist_v, waves_v, rise_v,
    send, recv, send_two, recv_two, relayed, fringe, own, stage_one, stage_two, stage_three, tails_out,
    tails_in, eddy, force, where_row, where_lev, where_turb, load_sem, a2a_send, a2a_recv, relay_send,
    relay_recv, halo_send, halo_recv, out_sem,
):
    count = across * spanwise
    comps, width, depth, levels = farm.shape
    area = width * depth
    lanes = fringe.shape[-1]
    base = lanes - 128
    tail = levels - base
    groups = send.shape[0] // comps
    filled = NF // width
    shift = across - filled
    row, column = lax.axis_index("gx"), lax.axis_index("gy")
    position = row * spanwise + column
    barrier = pltpu.get_barrier_semaphore()

    @pl.loop(1, count)
    def _(step):
        peer = (position + step) % count
        pl.semaphore_signal(
            barrier, inc=1, device_id=(peer // spanwise, peer % spanwise), device_id_type=MESH
        )

    loads = [pltpu.make_async_copy(vertical, vert_v, load_sem.at[0])]
    for comp in range(comps):
        loads.append(pltpu.make_async_copy(pre.at[comp], pre_v.at[comp], load_sem.at[1 + comp]))
    early = len(loads)
    for index, (source, target) in enumerate((
        (outer, outer_v), (outer_back, outerb_v), (inner_f, innf_v), (inner_b, innb_v),
        (twist, twist_v), (waves, waves_v), (rise.at[position], rise_v),
        (cell, turb_v.at[0]), (slot, turb_v.at[1]), (live, turb_v.at[2]),
    )):
        loads.append(pltpu.make_async_copy(source, target, load_sem.at[early + index]))
    tables = len(loads)
    for y in range(depth):
        loads.append(pltpu.make_async_copy(farm.at[:, :, y], farm_v.at[:, y], load_sem.at[tables + y]))
    for copy in loads:
        copy.start()

    loads[0].wait()
    last = ((1,), (1,))
    for comp in range(comps):
        loads[1 + comp].wait()
        kind = comp // 2
        table = (vert_v[kind, 0][:, :levels], vert_v[kind, 1][:, :levels])
        modes = product(table, halves(pre_v[comp]), last)
        for group in range(groups):
            send[group * comps + comp] = modes[group * count : (group + 1) * count]

    chunks = []
    size = -(-groups // CHUNKS)
    for start in range(0, groups, size):
        chunks.append((start, min(groups, start + size)))

    def part_of(index):
        low, high = chunks[index]
        return pl.ds(low * comps, (high - low) * comps)

    def spread(leg, index, source, target):
        part = part_of(index)

        @pl.loop(0, count - 1)
        def _(step):
            turn = step // across
            away = (spanwise // 2 + (turn % 2 * 2 - 1) * ((turn + 1) // 2)) % spanwise
            col = (column + away + spanwise) % spanwise
            peer_row = (row + step + 1) % across
            pltpu.make_async_remote_copy(
                src_ref=source.at[part, peer_row * spanwise + col],
                dst_ref=target.at[part, position],
                send_sem=a2a_send.at[leg, index],
                recv_sem=a2a_recv.at[leg, index],
                device_id=(peer_row, col),
                device_id_type=MESH,
            ).start()

        pltpu.make_async_copy(
            source.at[part, position], target.at[part, position], a2a_recv.at[leg, index]
        ).start()

    def gathered(leg, index, target):
        part = target.at[part_of(index)]
        pltpu.make_async_copy(part, part, a2a_recv.at[leg, index]).wait()

    def sent(leg, index, source):
        part = source.at[part_of(index), pl.ds(0, count - 1)]
        pltpu.make_async_copy(part, part, a2a_send.at[leg, index]).wait()

    pl.semaphore_wait(barrier, count - 1)
    for index in range(len(chunks)):
        spread(0, index, send, recv)

    def transfer(source, target, step_row, step_col, send_sem, recv_sem):
        if isinstance(step_col, int) and step_row % across == 0 and step_col % spanwise == 0:
            return pltpu.make_async_copy(source, target, recv_sem), False
        copy = pltpu.make_async_remote_copy(
            src_ref=source, dst_ref=target, send_sem=send_sem, recv_sem=recv_sem,
            device_id=((row + step_row) % across, (column + step_col) % spanwise),
            device_id_type=MESH,
        )
        return copy, True

    def side_copies(source, at, stage, role, target, offset, side):
        step = 1 - 2 * side
        near = at + (depth - 2) * (1 - side)
        edge = at + (depth - 1) * (1 - side)
        land = (depth + 2) * side
        ghost = 1 + (depth + 1) * side
        use = lambda place: (halo_send.at[role, place], halo_recv.at[stage, place])
        return [
            transfer(
                source.at[:, pl.ds(near, 2), pl.ds(0, width), pl.ds(0, base)],
                target.at[:, pl.ds(land, 2), pl.ds(0, width), pl.ds(0, base)],
                offset, step, *use(side),
            ),
            transfer(tails_out.at[role, side], tails_in.at[stage, side], offset, step, *use(2 + side)),
            transfer(
                source.at[:, edge, pl.ds(width - 1, 1)], target.at[:, ghost, pl.ds(width + 7, 1)],
                offset + 1, step, *use(4 + 2 * side),
            ),
            transfer(
                source.at[:, edge, pl.ds(0, 1)], target.at[:, ghost, pl.ds(width, 1)],
                offset - 1, step, *use(5 + 2 * side),
            ),
        ]

    def line_copies(source, at, stage, role, target, offset):
        rows = pl.ds(at, depth)
        use = lambda place: (halo_send.at[role, place], halo_recv.at[stage, place])
        return [
            transfer(
                source.at[:, rows, pl.ds(width - 2, 2)], target.at[:, pl.ds(2, depth), pl.ds(width + 6, 2)],
                offset + 1, 0, *use(8),
            ),
            transfer(
                source.at[:, rows, pl.ds(0, 2)], target.at[:, pl.ds(2, depth), pl.ds(width, 2)],
                offset - 1, 0, *use(9),
            ),
        ]

    def pack(source, at, role, side):
        near = at + (depth - 2) * (1 - side)
        for comp in range(comps):
            tails_out[role, side, comp] = source[comp, near, :width, base:] + pltpu.roll(
                source[comp, near + 1, :width, base:], tail, 1
            )

    def send_side(source, at, stage, role, target, offset, side):
        pack(source, at, role, side)
        copies = side_copies(source, at, stage, role, target, offset, side)
        for copy, _ in copies:
            copy.start()
        return copies

    def send_lines(source, at, stage, role, target, offset):
        copies = line_copies(source, at, stage, role, target, offset)
        for copy, _ in copies:
            copy.start()
        return copies

    def send_tile(source, role, offset):
        copies = []
        for side in (0, 1):
            copies += send_side(source, 0, 0, role, stage_one, offset, side)
        return copies + send_lines(source, 0, 0, role, stage_one, offset)

    def tile_sent(source, role, offset):
        copies = line_copies(source, 0, 0, role, stage_one, offset)
        for side in (0, 1):
            copies += side_copies(source, 0, 0, role, stage_one, offset, side)
        for copy, remote in copies:
            if remote:
                copy.wait_send()

    for copy in loads[tables:]:
        copy.wait()
    blank = jnp.zeros((width, lanes - base), jnp.float32)

    @pl.when(row >= filled)
    def _():
        for comp in range(comps):
            for y in range(depth):
                own[comp, y, :, base:] = blank
                own[comp, y, :, :levels] = farm_v[comp, y]
                stage_one[comp, 2 + y, :width] = own[comp, y]
        send_tile(own, 0, 0)

    for copy in loads[early:tables]:
        copy.wait()
    index = turb_v[0].astype(jnp.float32)
    line = jnp.floor((index + 0.5) * (1.0 / levels))
    level = index - levels * line
    at_x = jnp.floor((line + 0.5) * (1.0 / depth))
    line = (line - depth * at_x) * width + at_x
    slots = index.shape[-1]

    def hot(size, value):
        steps = lax.broadcasted_iota(jnp.int32, (size, slots), 0).astype(jnp.float32)
        return jnp.where(steps == value, 1.0, 0.0)

    where_row[...] = hot(area, line)
    where_lev[...] = hot(lanes, level).astype(jnp.bfloat16)
    turbine = jnp.where(turb_v[2] == 1, turb_v[1], TURB).astype(jnp.float32)
    where_turb[...] = hot(TURB, turbine)

    kx, ky, hor, decay = waves_v[0], waves_v[1], waves_v[2], waves_v[3]

    def project(chunk):
        low, high = chunk
        table = outer_v[...]
        cos, sin = twist_v[0], twist_v[1]
        blocks = []
        for place in range(low * comps, high * comps):
            head, rest = halves(recv[place])
            spun = dot(table, jnp.concatenate([head, head, rest], axis=0))
            real, imag = spun[:count], spun[count:]
            blocks.append(jnp.concatenate([real * cos - imag * sin, real * sin + imag * cos], axis=1))
        spec = product(halves(jnp.concatenate(blocks, axis=0)), (innf_v[0], innf_v[1]))
        blocks = []
        for group in range(low, high):
            lift = rise_v[pl.ds(group, 1), :area]
            real, imag = [], []
            for comp in range(comps):
                start = ((group - low) * comps + comp) * count
                real.append(spec[start : start + count, :area])
                imag.append(spec[start : start + count, area:])
            bound = hor + lift * lift
            inverse = jnp.where(bound > 0.0, -1.0 / jnp.where(bound > 0.0, bound, 1.0), 0.0)
            press_re = (lift * real[2] - kx * imag[0] - ky * imag[1]) * inverse
            press_im = (kx * real[0] + ky * real[1] + lift * imag[2]) * inverse
            new_re = [real[0] + kx * press_im, real[1] + ky * press_im, real[2] + lift * press_re]
            new_im = [imag[0] - kx * press_re, imag[1] - ky * press_re, imag[2] + lift * press_im]
            for comp in range(comps):
                blocks.append(jnp.concatenate([new_re[comp] * decay, new_im[comp] * decay], axis=1))
        lines = product(halves(jnp.concatenate(blocks, axis=0)), (innb_v[0], innb_v[1]))
        table = outerb_v[...]
        cos, sin = twist_v[2], twist_v[3]
        for place in range((high - low) * comps):
            real = lines[place * count : (place + 1) * count, :area]
            imag = lines[place * count : (place + 1) * count, area:]
            spun = jnp.concatenate([real * cos + imag * sin, imag * cos - real * sin], axis=0)
            head, rest = halves(spun)
            send_two[low * comps + place] = dot(table, jnp.concatenate([head, head, rest], axis=0))

    for index, chunk in enumerate(chunks):
        gathered(0, index, recv)
        project(chunk)
        spread(1, index, send_two, recv_two)

    def relay(index):
        return transfer(
            recv_two.at[part_of(index)], relayed.at[part_of(index)], -shift, 0,
            relay_send.at[index], relay_recv.at[index],
        )

    def levels_of(source, index, comp):
        low, high = chunks[index]
        modes = jnp.concatenate([source[g * comps + comp] for g in range(low, high)], axis=0)
        kind = comp // 2
        span = slice(low * count, high * count)
        value = product(halves(modes.T), (vert_v[kind, 0, span], vert_v[kind, 1, span]))
        return value.reshape(depth, width, lanes)

    for index in range(len(chunks)):
        gathered(1, index, recv_two)

        @pl.when(row >= shift)
        def _():
            relay(index)[0].start()

        for comp in range(comps):
            value = levels_of(recv_two, index, comp)
            fringe[comp] = value if index == 0 else fringe[comp] + value

    @pl.when(row >= shift)
    def _():
        send_tile(fringe, 1, -shift)

    outs = []
    for comp in range(comps):
        farm_v[comp] = fringe[comp][:, :, :levels]
    for y in range(depth):
        copy = pltpu.make_async_copy(farm_v.at[:, y], pre_new.at[:, :, y], out_sem.at[0, y])
        copy.start()
        outs.append(copy)

    @pl.when(row < filled)
    def _():
        for index in range(len(chunks)):
            part = relayed.at[part_of(index)]
            pltpu.make_async_copy(part, part, relay_recv.at[index]).wait()
            for comp in range(comps):
                value = levels_of(relayed, index, comp)
                if index > 0:
                    value = value + stage_one[comp, 2 : depth + 2, :width]
                stage_one[comp, 2 : depth + 2, :width] = value

    inside = lax.broadcasted_iota(jnp.int32, (width, lanes), 1) < levels
    kept = lax.broadcasted_iota(jnp.int32, (width, lanes - base), 1) < tail

    def arrived(part, stage, place):
        pltpu.make_async_copy(part, part, halo_recv.at[stage, place]).wait()

    def lines_in(field, stage):
        arrived(field.at[:, pl.ds(2, depth), pl.ds(width + 6, 2)], stage, 8)
        arrived(field.at[:, pl.ds(2, depth), pl.ds(width, 2)], stage, 9)

    def side_in(field, stage, side):
        land = (depth + 2) * side
        ghost = 1 + (depth + 1) * side
        arrived(field.at[:, pl.ds(land, 2), pl.ds(0, width), pl.ds(0, base)], stage, side)
        arrived(tails_in.at[stage, side], stage, 2 + side)
        arrived(field.at[:, ghost, pl.ds(width + 7, 1)], stage, 4 + 2 * side)
        arrived(field.at[:, ghost, pl.ds(width, 1)], stage, 5 + 2 * side)
        for comp in range(comps):
            packed = tails_in[stage, side, comp]
            field[comp, land, :width, base:] = jnp.where(kept, packed, 0.0)
            packed = pltpu.roll(packed, 128 - tail, 1)
            field[comp, land + 1, :width, base:] = jnp.where(kept, packed, 0.0)

    def drag(field):
        cells = field[0, 2 : depth + 2, :width].reshape(area, lanes)
        head, rest = halves(cells)
        table = where_lev[...]
        picked = (dot(head, table) + dot(rest, table)) * where_row[...]
        values = jnp.sum(picked, axis=0, keepdims=True) + WIND
        turbs = where_turb[...]
        sums = jnp.sum(turbs * values, axis=1, keepdims=True)
        counts = jnp.sum(turbs, axis=1, keepdims=True)
        mean = sums / jnp.maximum(counts, 1.0)
        thrust = (-0.5 * THRUST * STEP) * mean * jnp.abs(mean)
        per_slot = jnp.sum(turbs * thrust, axis=0, keepdims=True)
        head, rest = halves(where_row[...] * per_slot)
        last = ((1,), (1,))
        force[...] = (dot(head, table, last) + dot(rest, table, last)).reshape(depth, width, lanes)

    def ahead(value, axis):
        return pltpu.roll(value, value.shape[axis] - 1, axis)

    def behind(value, axis):
        return pltpu.roll(value, 1, axis)

    def eddy_slab(field, j):
        along, across_y, up = [], [], []
        for comp in range(comps):
            value = field[comp, j]
            along.append(ahead(value, 0) - behind(value, 0))
            across_y.append(field[comp, j + 1] - field[comp, j - 1])
            up.append(ahead(value, 1) - behind(value, 1))
        square = along[0] * along[0] + across_y[1] * across_y[1] + up[2] * up[2]
        for pair in (along[1] + across_y[0], along[2] + up[0], across_y[2] + up[1]):
            square = square + 0.5 * (pair * pair)
        eddy[j - 1] = (0.5 * STEP * SMAG * math.sqrt(0.5)) * jnp.sqrt(square)

    def flux(speed, low_f, high_f, low_h, high_h):
        return speed * (low_f + high_f) - (low_h + high_h) * (high_f - low_f)

    quarter = 0.25 * STEP

    def span_flux(field, j):
        speed = quarter * (field[1, j, :width] + field[1, j + 1, :width])
        return tuple(
            flux(speed, field[comp, j, :width], field[comp, j + 1, :width], eddy[j - 1, :width], eddy[j, :width])
            for comp in range(comps)
        )

    def rates(field, start, size, store):
        def slab(step, below):
            j = start + step
            above = span_flux(field, j)
            viscous = eddy[j - 1]
            beyond = ahead(viscous, 0)
            whole = field[0, j]
            next_u = ahead(whole, 0)
            speed = quarter * (whole + next_u) + (2.0 * quarter * WIND)
            inner_h = viscous[:width]
            upper_h = ahead(inner_h, 1)
            lift = field[2, j, :width]
            rising = quarter * (lift + ahead(lift, 1))
            for comp in range(comps):
                value = field[comp, j]
                face = flux(speed, value, next_u if comp == 0 else ahead(value, 0), viscous, beyond)
                total = (face - behind(face, 0))[:width] + (above[comp] - below[comp])
                mid = value[:width]
                face = flux(rising, mid, ahead(mid, 1), inner_h, upper_h)
                total = total + (face - behind(face, 1))
                change = force[j - 2] - total if comp == 0 else -total
                store(comp, j, mid + change)
            return above

        lax.fori_loop(0, size, slab, span_flux(field, start - 1))

    first = 1 - (column + spanwise - 1) // spanwise

    def section(stage, field, store, leave):
        drag(field)
        lines_in(field, stage)

        @pl.loop(3, depth + 1)
        def _(j):
            eddy_slab(field, j)

        rates(field, 4, depth - 4, store)

        @pl.loop(0, 2)
        def _(turn):
            side = (turn + first) % 2
            side_in(field, stage, side)

            @pl.loop(0, 2)
            def _(half):
                eddy_slab(field, 1 + depth * side + half)

            rates(field, 2 + (depth - 2) * side, 2, store)
            leave(1 - side)

    def to_next(target, share):
        def store(comp, j, value):
            if share < 1.0:
                value = (1.0 - share) * stage_one[comp, j, :width] + share * value
            target[comp, j, :width] = jnp.where(inside, value, 0.0)
        return store

    def to_output(comp, j, value):
        value = stage_one[comp, j, :width] * (1.0 / 3.0) + (2.0 / 3.0) * value
        farm_v[comp, j - 2] = value[:, :levels]

    section(0, stage_one, to_next(stage_two, 1.0), lambda side: send_side(stage_two, 2, 1, 2, stage_two, 0, side))
    send_lines(stage_two, 2, 1, 2, stage_two, 0)
    section(1, stage_two, to_next(stage_three, 0.25), lambda side: send_side(stage_three, 2, 2, 3, stage_three, 0, side))
    send_lines(stage_three, 2, 2, 3, stage_three, 0)
    for copy in outs:
        copy.wait()
    section(2, stage_three, to_output, lambda side: None)
    outs = []
    for y in range(depth):
        copy = pltpu.make_async_copy(farm_v.at[:, y], farm_new.at[:, :, y], out_sem.at[1, y])
        copy.start()
        outs.append(copy)

    for index in range(len(chunks)):
        sent(0, index, send)
        sent(1, index, send_two)
    for stage, field in ((1, stage_two), (2, stage_three)):
        copies = line_copies(field, 2, stage, stage + 1, field, 0)
        for side in (0, 1):
            copies += side_copies(field, 2, stage, stage + 1, field, 0, side)
        for copy, remote in copies:
            if remote:
                copy.wait_send()

    @pl.when(row >= shift)
    def _():
        tile_sent(fringe, 1, -shift)
        for index in range(len(chunks)):
            copy, remote = relay(index)
            if remote:
                copy.wait_send()

    @pl.when(row >= filled)
    def _():
        tile_sent(own, 0, 0)

    for copy in outs:
        copy.wait()


def shards(across, spanwise, farm, pre, turb_cell, turb_slot, disk_mask):
    comps, width, depth, levels = pre.shape
    count = across * spanwise
    area = width * depth
    slots = turb_cell.shape[-1]
    lanes = -(-(levels + 2) // 128) * 128
    groups = -(-levels // count)
    tables = [jnp.asarray(t) for t in spectral_tables(across, spanwise, width, depth, levels, lanes)]
    anywhere = pl.BlockSpec(memory_space=pl.ANY)
    f32 = jnp.float32

    def vmem(*shape, dtype=f32):
        return pltpu.VMEM(shape, dtype)

    def sems(*shape):
        return pltpu.SemaphoreType.DMA(shape)

    modes = vmem(groups * comps, count, area)
    cells = vmem(comps, depth, width, lanes)
    padded = vmem(comps, depth + 4, width + 8, lanes)
    return pl.pallas_call(
        functools.partial(step_body, across, spanwise),
        out_shape=[jax.ShapeDtypeStruct(farm.shape, f32), jax.ShapeDtypeStruct(pre.shape, f32)],
        in_specs=[anywhere] * (5 + len(tables)),
        out_specs=[anywhere] * 2,
        scratch_shapes=[
            vmem(comps, area, levels),
            vmem(comps, depth, width, levels),
            vmem(3, 1, slots, dtype=jnp.int32),
            *[vmem(*t.shape, dtype=t.dtype) for t in tables[:-1]],
            vmem(*tables[-1].shape[1:]),
            modes, modes, modes, modes, modes,
            cells, cells, padded, padded, padded,
            vmem(4, 2, comps, width, 128),
            vmem(3, 2, comps, width, 128),
            vmem(depth + 2, width + 8, lanes),
            vmem(depth, width, lanes),
            vmem(area, slots),
            vmem(lanes, slots, dtype=jnp.bfloat16),
            vmem(TURB, slots),
            sems(4 + 10 + depth),
            sems(2, CHUNKS),
            sems(2, CHUNKS),
            sems(CHUNKS),
            sems(CHUNKS),
            sems(4, 10),
            sems(3, 10),
            sems(2, depth),
        ],
        compiler_params=pltpu.CompilerParams(collective_id=0, has_side_effects=True),
        name="step",
    )(
        pre.reshape(comps, area, levels), farm,
        turb_cell.reshape(1, slots), turb_slot.reshape(1, slots), disk_mask.reshape(1, slots),
        *tables,
    )


def solution(mesh):
    across, spanwise = mesh.shape["gx"], mesh.shape["gy"]
    return jax.shard_map(
        functools.partial(shards, across, spanwise),
        mesh=mesh,
        in_specs=(
            P(None, "gx", "gy", None),
            P(None, "gx", "gy", None),
            P("gx", "gy", None),
            P("gx", "gy", None),
            P("gx", "gy", None),
        ),
        out_specs=(P(None, "gx", "gy", None), P(None, "gx", "gy", None)),
        check_vma=False,
    )
```

```python
import functools
import math

import jax
import jax.numpy as jnp
import numpy as np
from jax import lax
from jax.experimental import pallas as pl
from jax.experimental.pallas import tpu as pltpu
from jax.sharding import PartitionSpec as P

NF = 48
TURB = 16
WIND = 3.0
STEP = 0.1
SMAG = 0.0289
THRUST = 1.33
DIFFUSE = 0.05
MESH = pl.DeviceIdType.MESH
CHUNKS = 3


def split_pair(table):
    table = np.asarray(table, np.float32)
    head = table.astype(jnp.bfloat16)
    tail = (table - head.astype(np.float32)).astype(jnp.bfloat16)
    return np.stack([head, tail])


def stacked(table):
    head, tail = split_pair(table)
    return np.concatenate([head, tail, head], axis=1)


def spectral_tables(across, spanwise, width, depth, levels, lanes):
    count = across * spanwise
    total_x, total_y = across * width, spanwise * depth
    groups = -(-levels // count)
    order = np.arange(groups * count)[:, None]
    height = np.arange(levels)[None, :]
    inside = order < levels
    scale = np.where(order == 0, math.sqrt(1.0 / levels), math.sqrt(2.0 / levels)) * inside
    centre = scale * np.cos(math.pi / (2 * levels) * (order * (2 * height + 1) % (4 * levels)))
    face = (
        math.sqrt(2.0 / levels)
        * np.sin(math.pi / levels * (order * (height + 1) % (2 * levels)))
        * ((height < levels - 1) & (order > 0) & inside)
    )
    pad = ((0, 0), (0, 0), (0, lanes - levels))
    vertical = np.stack([np.pad(split_pair(centre), pad), np.pad(split_pair(face), pad)])
    rise = 2.0 * np.sin(np.minimum(order, levels)[:, 0] * (math.pi / (2 * levels)))
    rise = np.pad(rise.reshape(groups, count).T, ((0, 0), (0, -groups % 8)))
    rise = np.broadcast_to(rise[:, :, None], rise.shape + (128,))
    tile = np.arange(count)
    tile_x, tile_y = tile // spanwise, tile % spanwise
    turn = 2.0 * math.pi * (np.outer(tile_x, tile_x) / across + np.outer(tile_y, tile_y) / spanwise)
    outer = np.concatenate([np.cos(turn), -np.sin(turn)], axis=0)
    outer_back = np.concatenate([np.cos(turn), -np.sin(turn)], axis=1)
    lane = np.arange(width * depth)
    lane_x, lane_y = lane // depth, lane % depth
    back = (lane % width) * depth + lane // width
    angle = 2.0 * math.pi * (np.outer(tile_x, lane_x) / total_x + np.outer(tile_y, lane_y) / total_y)
    twist = np.stack([np.cos(angle), -np.sin(angle), np.cos(angle)[:, back], -np.sin(angle)[:, back]])
    turn = 2.0 * math.pi * (np.outer(lane_x, lane_x) / width + np.outer(lane_y, lane_y) / depth)
    real, imag = np.cos(turn), np.sin(turn)
    inner_forward = np.block([[real, -imag], [imag, real]])
    real, imag = real[:, back], imag[:, back]
    inner_back = np.block([[real, imag], [-imag, real]])
    k = tile_x[:, None] + across * lane_x[None, :]
    q = tile_y[:, None] + spanwise * lane_y[None, :]
    kx = 2.0 * math.pi / total_x * np.where(k < total_x // 2, k, k - total_x)
    ky = 2.0 * math.pi / total_y * np.where(q < total_y // 2, q, q - total_y)
    hor = kx * kx + ky * ky
    kept = (k != total_x // 2) & (q != total_y // 2)
    decay = np.exp(-DIFFUSE * hor) * kept / (total_x * total_y)
    waves = np.stack([kx, ky, hor, decay])
    return (
        vertical,
        stacked(outer),
        stacked(outer_back),
        split_pair(inner_forward),
        split_pair(inner_back),
        twist.astype(np.float32),
        waves.astype(np.float32),
        rise.astype(np.float32),
    )


def halves(value):
    head = value.astype(jnp.bfloat16)
    return head, (value - head.astype(jnp.float32)).astype(jnp.bfloat16)


def dot(left, right, dims=((1,), (0,))):
    return lax.dot_general(
        left, right, dimension_numbers=(dims, ((), ())), preferred_element_type=jnp.float32
    )


def product(left, right, dims=((1,), (0,))):
    return dot(left[0], right[0], dims) + (dot(left[0], right[1], dims) + dot(left[1], right[0], dims))


def step_body(
    across, spanwise, pre, farm, cell, slot, live, vertical, outer, outer_back, inner_f, inner_b,
    twist, waves, rise, farm_new, pre_new,
    pre_v, farm_v, turb_v, vert_v, outer_v, outerb_v, innf_v, innb_v, twist_v, waves_v, rise_v,
    send, recv, send_two, recv_two, relayed, fringe, own, stage_one, stage_two, stage_three, tails_out,
    tails_in, eddy, force, where_row, where_lev, where_turb, load_sem, a2a_send, a2a_recv, relay_send,
    relay_recv, halo_send, halo_recv, known,
):
    count = across * spanwise
    comps, width, depth, levels = farm.shape
    area = width * depth
    lanes = fringe.shape[-1]
    base = lanes - 128
    tail = levels - base
    groups = send.shape[0] // comps
    filled = NF // width
    shift = across - filled
    row, column = lax.axis_index("gx"), lax.axis_index("gy")
    position = row * spanwise + column
    barrier = pltpu.get_barrier_semaphore()

    loads = []
    for comp in range(comps):
        loads.append(pltpu.make_async_copy(pre.at[comp], pre_v.at[comp], load_sem.at[comp]))
    for kind in range(2):
        loads.append(pltpu.make_async_copy(vertical.at[kind], vert_v.at[kind], load_sem.at[comps + kind]))
    early = len(loads)
    for copy in loads:
        copy.start()

    bands = 4 if spanwise % 4 == 0 else 1
    deep = spanwise // bands
    band = column // deep
    crowd = deep * across
    seat = row * deep + column % deep

    def each_in(delta, action):
        def all_of(start):
            @pl.loop(start, crowd)
            def _(step):
                other = (seat + step) % crowd
                action(other // deep, (band + delta) * deep + other % deep)

        if delta == 0:
            all_of(1)
        elif delta > 0:
            pl.when(band < bands - delta)(lambda: all_of(0))
        else:
            pl.when(band >= -delta)(lambda: all_of(0))

    def greet(peer_row, peer_col):
        pl.semaphore_signal(barrier, inc=1, device_id=(peer_row, peer_col), device_id_type=MESH)

    def tell(semaphore, delta):
        pl.semaphore_signal(
            semaphore, inc=1, device_id=(row, column + delta * deep), device_id_type=MESH
        )

    near = (0,) if bands == 1 else (1, -1, 0)
    for delta in near[::-1]:
        each_in(delta, greet)

    for index, (source, target) in enumerate((
        (outer, outer_v), (outer_back, outerb_v), (inner_f, innf_v), (inner_b, innb_v),
        (twist, twist_v), (waves, waves_v), (rise.at[position], rise_v),
        (cell, turb_v.at[0]), (slot, turb_v.at[1]), (live, turb_v.at[2]),
    )):
        loads.append(pltpu.make_async_copy(source, target, load_sem.at[early + index]))
    tables = len(loads)
    for y in range(depth):
        loads.append(pltpu.make_async_copy(farm.at[:, :, y], farm_v.at[:, y], load_sem.at[tables + y]))
    for copy in loads[early:]:
        copy.start()

    chunks = []
    size = -(-groups // CHUNKS)
    for start in range(0, groups, size):
        chunks.append((start, min(groups, start + size)))

    def part_of(index):
        low, high = chunks[index]
        return pl.ds(low * comps, (high - low) * comps)

    def spread(leg, index, source, target, deltas):
        part = part_of(index)

        def post(peer_row, peer_col):
            pltpu.make_async_remote_copy(
                src_ref=source.at[part, peer_row * spanwise + peer_col],
                dst_ref=target.at[part, position],
                send_sem=a2a_send.at[leg, index],
                recv_sem=a2a_recv.at[leg, index],
                device_id=(peer_row, peer_col),
                device_id_type=MESH,
            ).start()

        for delta in deltas:
            each_in(delta, post)

    def keep(leg, index, source, target):
        part = part_of(index)
        pltpu.make_async_copy(
            source.at[part, position], target.at[part, position], a2a_recv.at[leg, index]
        ).start()

    def gathered(leg, index, target):
        part = target.at[part_of(index)]
        pltpu.make_async_copy(part, part, a2a_recv.at[leg, index]).wait()

    def sent(leg, index, source):
        part = source.at[part_of(index), pl.ds(0, count - 1)]
        pltpu.make_async_copy(part, part, a2a_send.at[leg, index]).wait()

    for copy in loads[:early]:
        copy.wait()
    columns = [halves(pre_v[comp]) for comp in range(comps)]

    def transform(index):
        low, high = chunks[index]
        span = slice(low * count, high * count)
        for comp in range(comps):
            kind = comp // 2
            table = (vert_v[kind, 0, span][:, :levels], vert_v[kind, 1, span][:, :levels])
            modes = product(table, columns[comp], ((1,), (1,)))
            for group in range(low, high):
                send[group * comps + comp] = modes[(group - low) * count : (group - low + 1) * count]

    far = () if bands == 1 else (2, -2, 3, -3)
    middle = ((band + 1) // 2) % 2
    for index in range(len(chunks)):
        transform(index)
        if index == 0:
            if bands == 1:
                pl.semaphore_wait(barrier, count - 1)
            else:
                pl.semaphore_wait(barrier, (2 + middle) * crowd - 1)

                @pl.when(middle == 1)
                def _():
                    tell(known.at[0], 1)
                    tell(known.at[0], -1)

            spread(0, index, send, recv, near)
            if bands > 1:
                pl.semaphore_wait(known.at[0], 1)

                @pl.when(band == 1)
                def _():
                    tell(known.at[1], -1)

                @pl.when(band == 2)
                def _():
                    tell(known.at[1], 1)

                spread(0, index, send, recv, far[:2])

                @pl.when(middle == 0)
                def _():
                    pl.semaphore_wait(known.at[1], 1)

                spread(0, index, send, recv, far[2:])
        else:
            spread(0, index, send, recv, far + near)
        keep(0, index, send, recv)

    def transfer(source, target, step_row, step_col, send_sem, recv_sem):
        if isinstance(step_col, int) and step_row % across == 0 and step_col % spanwise == 0:
            return pltpu.make_async_copy(source, target, recv_sem), False
        copy = pltpu.make_async_remote_copy(
            src_ref=source, dst_ref=target, send_sem=send_sem, recv_sem=recv_sem,
            device_id=((row + step_row) % across, (column + step_col) % spanwise),
            device_id_type=MESH,
        )
        return copy, True

    def side_copies(source, at, stage, role, target, offset, side):
        step = 1 - 2 * side
        near = at + (depth - 2) * (1 - side)
        edge = at + (depth - 1) * (1 - side)
        land = (depth + 2) * side
        ghost = 1 + (depth + 1) * side
        use = lambda place: (halo_send.at[role, place], halo_recv.at[stage, place])
        return [
            transfer(
                source.at[:, pl.ds(near, 2), pl.ds(0, width), pl.ds(0, base)],
                target.at[:, pl.ds(land, 2), pl.ds(0, width), pl.ds(0, base)],
                offset, step, *use(side),
            ),
            transfer(tails_out.at[role, side], tails_in.at[stage, side], offset, step, *use(2 + side)),
            transfer(
                source.at[:, edge, pl.ds(width - 1, 1)], target.at[:, ghost, pl.ds(width + 7, 1)],
                offset + 1, step, *use(4 + 2 * side),
            ),
            transfer(
                source.at[:, edge, pl.ds(0, 1)], target.at[:, ghost, pl.ds(width, 1)],
                offset - 1, step, *use(5 + 2 * side),
            ),
        ]

    def line_copies(source, at, stage, role, target, offset):
        rows = pl.ds(at, depth)
        use = lambda place: (halo_send.at[role, place], halo_recv.at[stage, place])
        return [
            transfer(
                source.at[:, rows, pl.ds(width - 2, 2)], target.at[:, pl.ds(2, depth), pl.ds(width + 6, 2)],
                offset + 1, 0, *use(8),
            ),
            transfer(
                source.at[:, rows, pl.ds(0, 2)], target.at[:, pl.ds(2, depth), pl.ds(width, 2)],
                offset - 1, 0, *use(9),
            ),
        ]

    def pack(source, at, role, side):
        near = at + (depth - 2) * (1 - side)
        for comp in range(comps):
            tails_out[role, side, comp] = source[comp, near, :width, base:] + pltpu.roll(
                source[comp, near + 1, :width, base:], tail, 1
            )

    def send_side(source, at, stage, role, target, offset, side):
        pack(source, at, role, side)
        copies = side_copies(source, at, stage, role, target, offset, side)
        for copy, _ in copies:
            copy.start()
        return copies

    def send_lines(source, at, stage, role, target, offset):
        copies = line_copies(source, at, stage, role, target, offset)
        for copy, _ in copies:
            copy.start()
        return copies

    def send_tile(source, role, offset):
        copies = send_lines(source, 0, 0, role, stage_one, offset)
        for side in (0, 1):
            copies += send_side(source, 0, 0, role, stage_one, offset, side)
        return copies

    def tile_sent(source, role, offset):
        copies = line_copies(source, 0, 0, role, stage_one, offset)
        for side in (0, 1):
            copies += side_copies(source, 0, 0, role, stage_one, offset, side)
        for copy, remote in copies:
            if remote:
                copy.wait_send()

    for copy in loads[tables:]:
        copy.wait()
    blank = jnp.zeros((width, lanes - base), jnp.float32)

    @pl.when(row >= filled)
    def _():
        for comp in range(comps):
            for y in range(depth):
                own[comp, y, :, base:] = blank
                own[comp, y, :, :levels] = farm_v[comp, y]
                stage_one[comp, 2 + y, :width] = own[comp, y]
        send_tile(own, 0, 0)

    for copy in loads[early:tables]:
        copy.wait()
    index = turb_v[0].astype(jnp.float32)
    line = jnp.floor((index + 0.5) * (1.0 / levels))
    level = index - levels * line
    at_x = jnp.floor((line + 0.5) * (1.0 / depth))
    line = (line - depth * at_x) * width + at_x
    slots = index.shape[-1]

    def hot(size, value):
        steps = lax.broadcasted_iota(jnp.int32, (size, slots), 0).astype(jnp.float32)
        return jnp.where(steps == value, 1.0, 0.0)

    where_row[...] = hot(area, line)
    where_lev[...] = hot(lanes, level).astype(jnp.bfloat16)
    turbine = jnp.where(turb_v[2] == 1, turb_v[1], TURB).astype(jnp.float32)
    where_turb[...] = hot(TURB, turbine)

    kx, ky, hor, decay = waves_v[0], waves_v[1], waves_v[2], waves_v[3]

    def project(chunk):
        low, high = chunk
        table = outer_v[...]
        cos, sin = twist_v[0], twist_v[1]
        blocks = []
        for place in range(low * comps, high * comps):
            head, rest = halves(recv[place])
            spun = dot(table, jnp.concatenate([head, head, rest], axis=0))
            real, imag = spun[:count], spun[count:]
            blocks.append(jnp.concatenate([real * cos - imag * sin, real * sin + imag * cos], axis=1))
        spec = product(halves(jnp.concatenate(blocks, axis=0)), (innf_v[0], innf_v[1]))
        blocks = []
        for group in range(low, high):
            lift = rise_v[pl.ds(group, 1), :area]
            real, imag = [], []
            for comp in range(comps):
                start = ((group - low) * comps + comp) * count
                real.append(spec[start : start + count, :area])
                imag.append(spec[start : start + count, area:])
            bound = hor + lift * lift
            inverse = jnp.where(bound > 0.0, -1.0 / jnp.where(bound > 0.0, bound, 1.0), 0.0)
            press_re = (lift * real[2] - kx * imag[0] - ky * imag[1]) * inverse
            press_im = (kx * real[0] + ky * real[1] + lift * imag[2]) * inverse
            new_re = [real[0] + kx * press_im, real[1] + ky * press_im, real[2] + lift * press_re]
            new_im = [imag[0] - kx * press_re, imag[1] - ky * press_re, imag[2] + lift * press_im]
            for comp in range(comps):
                blocks.append(jnp.concatenate([new_re[comp] * decay, new_im[comp] * decay], axis=1))
        lines = product(halves(jnp.concatenate(blocks, axis=0)), (innb_v[0], innb_v[1]))
        table = outerb_v[...]
        cos, sin = twist_v[2], twist_v[3]
        for place in range((high - low) * comps):
            real = lines[place * count : (place + 1) * count, :area]
            imag = lines[place * count : (place + 1) * count, area:]
            spun = jnp.concatenate([real * cos + imag * sin, imag * cos - real * sin], axis=0)
            head, rest = halves(spun)
            send_two[low * comps + place] = dot(table, jnp.concatenate([head, head, rest], axis=0))

    for index, chunk in enumerate(chunks):
        gathered(0, index, recv)
        project(chunk)
        keep(1, index, send_two, recv_two)
        spread(1, index, send_two, recv_two, far + near)

    def relay(index):
        return transfer(
            recv_two.at[part_of(index)], relayed.at[part_of(index)], -shift, 0,
            relay_send.at[index], relay_recv.at[index],
        )

    def levels_of(source, index, comp):
        low, high = chunks[index]
        modes = jnp.concatenate([source[g * comps + comp] for g in range(low, high)], axis=0)
        kind = comp // 2
        span = slice(low * count, high * count)
        value = product(halves(modes.T), (vert_v[kind, 0, span], vert_v[kind, 1, span]))
        return value.reshape(depth, width, lanes)

    for index in range(len(chunks)):
        gathered(1, index, recv_two)

        @pl.when(row >= shift)
        def _():
            relay(index)[0].start()

        for comp in range(comps):
            value = levels_of(recv_two, index, comp)
            fringe[comp] = value if index == 0 else fringe[comp] + value

    @pl.when(row >= shift)
    def _():
        send_tile(fringe, 1, -shift)


    @pl.when(row < filled)
    def _():
        for index in range(len(chunks)):
            part = relayed.at[part_of(index)]
            pltpu.make_async_copy(part, part, relay_recv.at[index]).wait()
            for comp in range(comps):
                value = levels_of(relayed, index, comp)
                if index > 0:
                    value = value + stage_one[comp, 2 : depth + 2, :width]
                stage_one[comp, 2 : depth + 2, :width] = value

    inside = lax.broadcasted_iota(jnp.int32, (width, lanes), 1) < levels
    kept = lax.broadcasted_iota(jnp.int32, (width, lanes - base), 1) < tail

    def arrived(part, stage, place):
        pltpu.make_async_copy(part, part, halo_recv.at[stage, place]).wait()

    def lines_in(field, stage):
        arrived(field.at[:, pl.ds(2, depth), pl.ds(width + 6, 2)], stage, 8)
        arrived(field.at[:, pl.ds(2, depth), pl.ds(width, 2)], stage, 9)

    def side_in(field, stage, side):
        land = (depth + 2) * side
        ghost = 1 + (depth + 1) * side
        arrived(field.at[:, pl.ds(land, 2), pl.ds(0, width), pl.ds(0, base)], stage, side)
        arrived(tails_in.at[stage, side], stage, 2 + side)
        arrived(field.at[:, ghost, pl.ds(width + 7, 1)], stage, 4 + 2 * side)
        arrived(field.at[:, ghost, pl.ds(width, 1)], stage, 5 + 2 * side)
        for comp in range(comps):
            packed = tails_in[stage, side, comp]
            field[comp, land, :width, base:] = jnp.where(kept, packed, 0.0)
            packed = pltpu.roll(packed, 128 - tail, 1)
            field[comp, land + 1, :width, base:] = jnp.where(kept, packed, 0.0)

    def drag(field):
        cells = field[0, 2 : depth + 2, :width].reshape(area, lanes)
        head, rest = halves(cells)
        table = where_lev[...]
        picked = (dot(head, table) + dot(rest, table)) * where_row[...]
        values = jnp.sum(picked, axis=0, keepdims=True) + WIND
        turbs = where_turb[...]
        sums = jnp.sum(turbs * values, axis=1, keepdims=True)
        counts = jnp.sum(turbs, axis=1, keepdims=True)
        mean = sums / jnp.maximum(counts, 1.0)
        thrust = (-0.5 * THRUST * STEP) * mean * jnp.abs(mean)
        per_slot = jnp.sum(turbs * thrust, axis=0, keepdims=True)
        head, rest = halves(where_row[...] * per_slot)
        last = ((1,), (1,))
        force[...] = (dot(head, table, last) + dot(rest, table, last)).reshape(depth, width, lanes)

    def ahead(value, axis):
        return pltpu.roll(value, value.shape[axis] - 1, axis)

    def behind(value, axis):
        return pltpu.roll(value, 1, axis)

    def eddy_slab(field, j):
        along, across_y, up = [], [], []
        for comp in range(comps):
            value = field[comp, j]
            along.append(ahead(value, 0) - behind(value, 0))
            across_y.append(field[comp, j + 1] - field[comp, j - 1])
            up.append(ahead(value, 1) - behind(value, 1))
        square = along[0] * along[0] + across_y[1] * across_y[1] + up[2] * up[2]
        for pair in (along[1] + across_y[0], along[2] + up[0], across_y[2] + up[1]):
            square = square + 0.5 * (pair * pair)
        eddy[j - 1] = (0.5 * STEP * SMAG * math.sqrt(0.5)) * jnp.sqrt(square)

    def flux(speed, low_f, high_f, low_h, high_h):
        return speed * (low_f + high_f) - (low_h + high_h) * (high_f - low_f)

    quarter = 0.25 * STEP

    def span_flux(field, j):
        speed = quarter * (field[1, j, :width] + field[1, j + 1, :width])
        return tuple(
            flux(speed, field[comp, j, :width], field[comp, j + 1, :width], eddy[j - 1, :width], eddy[j, :width])
            for comp in range(comps)
        )

    def rates(field, start, size, store):
        def slab(step, below):
            j = start + step
            above = span_flux(field, j)
            viscous = eddy[j - 1]
            beyond = ahead(viscous, 0)
            whole = field[0, j]
            next_u = ahead(whole, 0)
            speed = quarter * (whole + next_u) + (2.0 * quarter * WIND)
            inner_h = viscous[:width]
            upper_h = ahead(inner_h, 1)
            lift = field[2, j, :width]
            rising = quarter * (lift + ahead(lift, 1))
            for comp in range(comps):
                value = field[comp, j]
                face = flux(speed, value, next_u if comp == 0 else ahead(value, 0), viscous, beyond)
                total = (face - behind(face, 0))[:width] + (above[comp] - below[comp])
                mid = value[:width]
                face = flux(rising, mid, ahead(mid, 1), inner_h, upper_h)
                total = total + (face - behind(face, 1))
                change = force[j - 2] - total if comp == 0 else -total
                store(comp, j, mid + change)
            return above

        lax.fori_loop(0, size, slab, span_flux(field, start - 1))

    first = 1 - (column + spanwise - 1) // spanwise

    def section(stage, field, store, leave):
        drag(field)
        lines_in(field, stage)

        @pl.loop(3, depth + 1)
        def _(j):
            eddy_slab(field, j)

        rates(field, 4, depth - 4, store)

        @pl.loop(0, 2)
        def _(turn):
            side = (turn + first) % 2
            side_in(field, stage, side)

            @pl.loop(0, 2)
            def _(half):
                eddy_slab(field, 1 + depth * side + half)

            rates(field, 2 + (depth - 2) * side, 2, store)
            leave(1 - side)

    def to_next(target, share):
        def store(comp, j, value):
            if share < 1.0:
                value = (1.0 - share) * stage_one[comp, j, :width] + share * value
            target[comp, j, :width] = jnp.where(inside, value, 0.0)
        return store

    def to_output(comp, j, value):
        value = stage_one[comp, j, :width] * (1.0 / 3.0) + (2.0 / 3.0) * value
        farm_new[comp, j - 2] = value[:, :levels]

    section(0, stage_one, to_next(stage_two, 1.0), lambda side: send_side(stage_two, 2, 1, 2, stage_two, 0, side))
    send_lines(stage_two, 2, 1, 2, stage_two, 0)
    for comp in range(comps):
        pre_new[comp] = fringe[comp][:, :, :levels]
    section(1, stage_two, to_next(stage_three, 0.25), lambda side: send_side(stage_three, 2, 2, 3, stage_three, 0, side))
    send_lines(stage_three, 2, 2, 3, stage_three, 0)
    section(2, stage_three, to_output, lambda side: None)
    for index in range(len(chunks)):
        sent(0, index, send)
        sent(1, index, send_two)
    for stage, field in ((1, stage_two), (2, stage_three)):
        copies = line_copies(field, 2, stage, stage + 1, field, 0)
        for side in (0, 1):
            copies += side_copies(field, 2, stage, stage + 1, field, 0, side)
        for copy, remote in copies:
            if remote:
                copy.wait_send()

    @pl.when(row >= shift)
    def _():
        tile_sent(fringe, 1, -shift)
        for index in range(len(chunks)):
            copy, remote = relay(index)
            if remote:
                copy.wait_send()

    @pl.when(row >= filled)
    def _():
        tile_sent(own, 0, 0)


def write_out(farm, pre, farm_new, pre_new, sem):
    copies = []
    for place, (source, target) in enumerate(((farm, farm_new), (pre, pre_new))):
        for y in range(source.shape[1]):
            copies.append(pltpu.make_async_copy(source.at[:, y], target.at[:, :, y], sem.at[place, y]))
    for copy in copies:
        copy.start()
    for copy in copies:
        copy.wait()


def shards(across, spanwise, farm, pre, turb_cell, turb_slot, disk_mask):
    comps, width, depth, levels = pre.shape
    count = across * spanwise
    area = width * depth
    slots = turb_cell.shape[-1]
    lanes = -(-(levels + 2) // 128) * 128
    groups = -(-levels // count)
    tables = [jnp.asarray(t) for t in spectral_tables(across, spanwise, width, depth, levels, lanes)]
    anywhere = pl.BlockSpec(memory_space=pl.ANY)
    f32 = jnp.float32

    def vmem(*shape, dtype=f32):
        return pltpu.VMEM(shape, dtype)

    def sems(*shape):
        return pltpu.SemaphoreType.DMA(shape)

    modes = vmem(groups * comps, count, area)
    cells = vmem(comps, depth, width, lanes)
    padded = vmem(comps, depth + 4, width + 8, lanes)
    turned = jax.ShapeDtypeStruct((comps, depth, width, levels), f32)
    farm_new, pre_new = pl.pallas_call(
        functools.partial(step_body, across, spanwise),
        out_shape=[turned, turned],
        in_specs=[anywhere] * (5 + len(tables)),
        out_specs=[pl.BlockSpec(memory_space=pltpu.VMEM)] * 2,
        scratch_shapes=[
            vmem(comps, area, levels),
            vmem(comps, depth, width, levels),
            vmem(3, 1, slots, dtype=jnp.int32),
            *[vmem(*t.shape, dtype=t.dtype) for t in tables[:-1]],
            vmem(*tables[-1].shape[1:]),
            modes, modes, modes, modes, modes,
            cells, cells, padded, padded, padded,
            vmem(4, 2, comps, width, 128),
            vmem(3, 2, comps, width, 128),
            vmem(depth + 2, width + 8, lanes),
            vmem(depth, width, lanes),
            vmem(area, slots),
            vmem(lanes, slots, dtype=jnp.bfloat16),
            vmem(TURB, slots),
            sems(comps + 2 + 10 + depth),
            sems(2, CHUNKS),
            sems(2, CHUNKS),
            sems(CHUNKS),
            sems(CHUNKS),
            sems(4, 10),
            sems(3, 10),
            pltpu.SemaphoreType.REGULAR((2,)),
        ],
        compiler_params=pltpu.CompilerParams(collective_id=0, has_side_effects=True),
        name="step",
    )(
        pre.reshape(comps, area, levels), farm,
        turb_cell.reshape(1, slots), turb_slot.reshape(1, slots), disk_mask.reshape(1, slots),
        *tables,
    )
    return pl.pallas_call(
        write_out,
        out_shape=[jax.ShapeDtypeStruct(farm.shape, f32), jax.ShapeDtypeStruct(pre.shape, f32)],
        in_specs=[pl.BlockSpec(memory_space=pltpu.VMEM)] * 2,
        out_specs=[anywhere] * 2,
        scratch_shapes=[sems(2, depth)],
        name="write_out",
    )(farm_new, pre_new)


def solution(mesh):
    across, spanwise = mesh.shape["gx"], mesh.shape["gy"]
    return jax.shard_map(
        functools.partial(shards, across, spanwise),
        mesh=mesh,
        in_specs=(
            P(None, "gx", "gy", None),
            P(None, "gx", "gy", None),
            P("gx", "gy", None),
            P("gx", "gy", None),
            P("gx", "gy", None),
        ),
        out_specs=(P(None, "gx", "gy", None), P(None, "gx", "gy", None)),
        check_vma=False,
    )
```

```python
import functools
import math

import jax
import jax.numpy as jnp
import numpy as np
from jax import lax
from jax.experimental import pallas as pl
from jax.experimental.pallas import tpu as pltpu
from jax.sharding import PartitionSpec as P

NF = 48
TURB = 16
WIND = 3.0
STEP = 0.1
SMAG = 0.0289
THRUST = 1.33
DIFFUSE = 0.05
MESH = pl.DeviceIdType.MESH
SHARES = (1 / 3, 1 / 3, 1 / 6, 1 / 6)


def split_pair(table):
    table = np.asarray(table, np.float32)
    head = table.astype(jnp.bfloat16)
    tail = (table - head.astype(np.float32)).astype(jnp.bfloat16)
    return np.stack([head, tail])


def shared(left, right):
    rows = left[0].shape[0]
    both = dot(jnp.concatenate(left, axis=0), right[0])
    return both[:rows] + (both[rows:] + dot(left[0], right[1]))


def stacked(table):
    head, tail = split_pair(table)
    return np.concatenate([head, tail, head], axis=1)


def spectral_tables(across, spanwise, width, depth, levels, lanes):
    count = across * spanwise
    total_x, total_y = across * width, spanwise * depth
    groups = -(-levels // count)
    order = np.arange(groups * count)[:, None]
    height = np.arange(levels)[None, :]
    inside = order < levels
    scale = np.where(order == 0, math.sqrt(1.0 / levels), math.sqrt(2.0 / levels)) * inside
    centre = scale * np.cos(math.pi / (2 * levels) * (order * (2 * height + 1) % (4 * levels)))
    face = (
        math.sqrt(2.0 / levels)
        * np.sin(math.pi / levels * (order * (height + 1) % (2 * levels)))
        * ((height < levels - 1) & (order > 0) & inside)
    )
    pad = ((0, 0), (0, 0), (0, lanes - levels))
    vertical = np.stack([np.pad(split_pair(centre), pad), np.pad(split_pair(face), pad)])
    rise = 2.0 * np.sin(np.minimum(order, levels)[:, 0] * (math.pi / (2 * levels)))
    rise = np.pad(rise.reshape(groups, count).T, ((0, 0), (0, -groups % 8)))
    rise = np.broadcast_to(rise[:, :, None], rise.shape + (128,))
    tile = np.arange(count)
    tile_x, tile_y = tile // spanwise, tile % spanwise
    turn = 2.0 * math.pi * (np.outer(tile_x, tile_x) / across + np.outer(tile_y, tile_y) / spanwise)
    outer = np.concatenate([np.cos(turn), -np.sin(turn)], axis=0)
    outer_back = np.concatenate([np.cos(turn), -np.sin(turn)], axis=1)
    lane = np.arange(width * depth)
    lane_x, lane_y = lane // depth, lane % depth
    back = (lane % width) * depth + lane // width
    angle = 2.0 * math.pi * (np.outer(tile_x, lane_x) / total_x + np.outer(tile_y, lane_y) / total_y)
    twist = np.stack([np.cos(angle), -np.sin(angle), np.cos(angle)[:, back], -np.sin(angle)[:, back]])
    turn = 2.0 * math.pi * (np.outer(lane_x, lane_x) / width + np.outer(lane_y, lane_y) / depth)
    real, imag = np.cos(turn), np.sin(turn)
    inner_forward = np.block([[real, -imag], [imag, real]])
    real, imag = real[:, back], imag[:, back]
    inner_back = np.block([[real, imag], [-imag, real]])
    k = tile_x[:, None] + across * lane_x[None, :]
    q = tile_y[:, None] + spanwise * lane_y[None, :]
    kx = 2.0 * math.pi / total_x * np.where(k < total_x // 2, k, k - total_x)
    ky = 2.0 * math.pi / total_y * np.where(q < total_y // 2, q, q - total_y)
    hor = kx * kx + ky * ky
    kept = (k != total_x // 2) & (q != total_y // 2)
    decay = np.exp(-DIFFUSE * hor) * kept / (total_x * total_y)
    waves = np.stack([kx, ky, hor, decay])
    return (
        vertical,
        stacked(outer),
        stacked(outer_back),
        split_pair(inner_forward),
        split_pair(inner_back),
        twist.astype(np.float32),
        waves.astype(np.float32),
        rise.astype(np.float32),
    )


def halves(value):
    head = value.astype(jnp.bfloat16)
    return head, (value - head.astype(jnp.float32)).astype(jnp.bfloat16)


def dot(left, right, dims=((1,), (0,))):
    return lax.dot_general(
        left, right, dimension_numbers=(dims, ((), ())), preferred_element_type=jnp.float32
    )


def product(left, right, dims=((1,), (0,))):
    return dot(left[0], right[0], dims) + (dot(left[0], right[1], dims) + dot(left[1], right[0], dims))


def step_body(
    across, spanwise, pre, farm, cell, slot, live, vertical, outer, outer_back, inner_f, inner_b,
    twist, waves, rise, farm_new, pre_new,
    pre_v, farm_v, turb_v, vert_v, outer_v, outerb_v, innf_v, innb_v, twist_v, waves_v, rise_v,
    send, recv, send_two, recv_two, relayed, fringe, own, stage_one, stage_two, stage_three, tails_out,
    tails_in, eddy, force, where_row, where_lev, where_turb, load_sem, a2a_send, a2a_recv, relay_send,
    relay_recv, halo_send, halo_recv, known, out_sem,
):
    count = across * spanwise
    comps, width, depth, levels = farm.shape
    area = width * depth
    lanes = fringe.shape[-1]
    base = lanes - 128
    tail = levels - base
    groups = send.shape[0] // comps
    filled = NF // width
    shift = across - filled
    row, column = lax.axis_index("gx"), lax.axis_index("gy")
    position = row * spanwise + column
    barrier = pltpu.get_barrier_semaphore()

    loads = []
    for comp in range(comps):
        loads.append(pltpu.make_async_copy(pre.at[comp], pre_v.at[comp], load_sem.at[comp]))
    for kind in range(2):
        loads.append(pltpu.make_async_copy(vertical.at[kind], vert_v.at[kind], load_sem.at[comps + kind]))
    early = len(loads)
    for copy in loads:
        copy.start()

    bands = 4 if spanwise % 4 == 0 else 1
    deep = spanwise // bands
    band = column // deep
    crowd = deep * across
    seat = row * deep + column % deep

    def each_in(delta, action):
        def all_of(start):
            @pl.loop(start, crowd)
            def _(step):
                other = (seat + step) % crowd
                action(other // deep, (band + delta) * deep + other % deep)

        if delta == 0:
            all_of(1)
        elif delta > 0:
            pl.when(band < bands - delta)(lambda: all_of(0))
        else:
            pl.when(band >= -delta)(lambda: all_of(0))

    def greet(peer_row, peer_col):
        pl.semaphore_signal(barrier, inc=1, device_id=(peer_row, peer_col), device_id_type=MESH)

    def tell(semaphore, delta):
        pl.semaphore_signal(
            semaphore, inc=1, device_id=(row, column + delta * deep), device_id_type=MESH
        )

    near = (0,) if bands == 1 else (1, -1, 0)
    for delta in near[::-1]:
        each_in(delta, greet)

    for index, (source, target) in enumerate((
        (outer, outer_v), (outer_back, outerb_v), (inner_f, innf_v), (inner_b, innb_v),
        (twist, twist_v), (waves, waves_v), (rise.at[position], rise_v),
        (cell, turb_v.at[0]), (slot, turb_v.at[1]), (live, turb_v.at[2]),
    )):
        loads.append(pltpu.make_async_copy(source, target, load_sem.at[early + index]))
    tables = len(loads)
    for y in range(depth):
        loads.append(pltpu.make_async_copy(farm.at[:, :, y], farm_v.at[:, y], load_sem.at[tables + y]))
    for copy in loads[early:]:
        copy.start()

    chunks = []
    start = 0
    for share in SHARES:
        stop = min(groups, start + max(1, round(share * groups)))
        if start < stop:
            chunks.append((start, stop))
        start = stop
    chunks[-1] = (chunks[-1][0], groups)

    def part_of(index):
        low, high = chunks[index]
        return pl.ds(low * comps, (high - low) * comps)

    def spread(leg, index, source, target, deltas):
        part = part_of(index)

        def post(peer_row, peer_col):
            pltpu.make_async_remote_copy(
                src_ref=source.at[part, peer_row * spanwise + peer_col],
                dst_ref=target.at[part, position],
                send_sem=a2a_send.at[leg, index],
                recv_sem=a2a_recv.at[leg, index],
                device_id=(peer_row, peer_col),
                device_id_type=MESH,
            ).start()

        for delta in deltas:
            each_in(delta, post)

    def keep(leg, index, source, target):
        part = part_of(index)
        pltpu.make_async_copy(
            source.at[part, position], target.at[part, position], a2a_recv.at[leg, index]
        ).start()

    def gathered(leg, index, target):
        part = target.at[part_of(index)]
        pltpu.make_async_copy(part, part, a2a_recv.at[leg, index]).wait()

    def sent(leg, index, source):
        part = source.at[part_of(index), pl.ds(0, count - 1)]
        pltpu.make_async_copy(part, part, a2a_send.at[leg, index]).wait()

    for copy in loads[:early]:
        copy.wait()
    columns = [halves(pre_v[comp]) for comp in range(comps)]

    def transform(index):
        low, high = chunks[index]
        span = slice(low * count, high * count)
        for comp in range(comps):
            kind = comp // 2
            table = (vert_v[kind, 0, span][:, :levels], vert_v[kind, 1, span][:, :levels])
            modes = product(table, columns[comp], ((1,), (1,)))
            for group in range(low, high):
                send[group * comps + comp] = modes[(group - low) * count : (group - low + 1) * count]

    far = () if bands == 1 else (2, -2, 3, -3)
    middle = ((band + 1) // 2) % 2
    for index in range(len(chunks)):
        transform(index)
        if index == 0:
            if bands == 1:
                pl.semaphore_wait(barrier, count - 1)
            else:
                pl.semaphore_wait(barrier, (2 + middle) * crowd - 1)

                @pl.when(middle == 1)
                def _():
                    tell(known.at[0], 1)
                    tell(known.at[0], -1)

            spread(0, index, send, recv, near)
            if bands > 1:
                pl.semaphore_wait(known.at[0], 1)

                @pl.when(band == 1)
                def _():
                    tell(known.at[1], -1)

                @pl.when(band == 2)
                def _():
                    tell(known.at[1], 1)

                spread(0, index, send, recv, far[:2])

                @pl.when(middle == 0)
                def _():
                    pl.semaphore_wait(known.at[1], 1)

                spread(0, index, send, recv, far[2:])
        else:
            spread(0, index, send, recv, far + near)
        keep(0, index, send, recv)

    def transfer(source, target, step_row, step_col, send_sem, recv_sem):
        if isinstance(step_col, int) and step_row % across == 0 and step_col % spanwise == 0:
            return pltpu.make_async_copy(source, target, recv_sem), False
        copy = pltpu.make_async_remote_copy(
            src_ref=source, dst_ref=target, send_sem=send_sem, recv_sem=recv_sem,
            device_id=((row + step_row) % across, (column + step_col) % spanwise),
            device_id_type=MESH,
        )
        return copy, True

    def side_copies(source, at, stage, role, target, offset, side):
        step = 1 - 2 * side
        near = at + (depth - 2) * (1 - side)
        edge = at + (depth - 1) * (1 - side)
        land = (depth + 2) * side
        ghost = 1 + (depth + 1) * side
        use = lambda place: (halo_send.at[role, place], halo_recv.at[stage, place])
        return [
            transfer(
                source.at[:, pl.ds(near, 2), pl.ds(0, width), pl.ds(0, base)],
                target.at[:, pl.ds(land, 2), pl.ds(0, width), pl.ds(0, base)],
                offset, step, *use(side),
            ),
            transfer(tails_out.at[role, side], tails_in.at[stage, side], offset, step, *use(2 + side)),
            transfer(
                source.at[:, edge, pl.ds(width - 1, 1)], target.at[:, ghost, pl.ds(width + 7, 1)],
                offset + 1, step, *use(4 + 2 * side),
            ),
            transfer(
                source.at[:, edge, pl.ds(0, 1)], target.at[:, ghost, pl.ds(width, 1)],
                offset - 1, step, *use(5 + 2 * side),
            ),
        ]

    def line_copies(source, at, stage, role, target, offset):
        rows = pl.ds(at, depth)
        use = lambda place: (halo_send.at[role, place], halo_recv.at[stage, place])
        return [
            transfer(
                source.at[:, rows, pl.ds(width - 2, 2)], target.at[:, pl.ds(2, depth), pl.ds(width + 6, 2)],
                offset + 1, 0, *use(8),
            ),
            transfer(
                source.at[:, rows, pl.ds(0, 2)], target.at[:, pl.ds(2, depth), pl.ds(width, 2)],
                offset - 1, 0, *use(9),
            ),
        ]

    def pack(source, at, role, side):
        near = at + (depth - 2) * (1 - side)
        for comp in range(comps):
            tails_out[role, side, comp] = source[comp, near, :width, base:] + pltpu.roll(
                source[comp, near + 1, :width, base:], tail, 1
            )

    def send_side(source, at, stage, role, target, offset, side):
        pack(source, at, role, side)
        copies = side_copies(source, at, stage, role, target, offset, side)
        for copy, _ in copies:
            copy.start()
        return copies

    def send_lines(source, at, stage, role, target, offset):
        copies = line_copies(source, at, stage, role, target, offset)
        for copy, _ in copies:
            copy.start()
        return copies

    def send_tile(source, role, offset):
        copies = send_lines(source, 0, 0, role, stage_one, offset)
        for side in (0, 1):
            copies += send_side(source, 0, 0, role, stage_one, offset, side)
        return copies

    def tile_sent(source, role, offset):
        copies = line_copies(source, 0, 0, role, stage_one, offset)
        for side in (0, 1):
            copies += side_copies(source, 0, 0, role, stage_one, offset, side)
        for copy, remote in copies:
            if remote:
                copy.wait_send()

    for copy in loads[tables:]:
        copy.wait()
    blank = jnp.zeros((width, lanes - base), jnp.float32)

    @pl.when(row >= filled)
    def _():
        for comp in range(comps):
            for y in range(depth):
                own[comp, y, :, base:] = blank
                own[comp, y, :, :levels] = farm_v[comp, y]
                stage_one[comp, 2 + y, :width] = own[comp, y]
        send_tile(own, 0, 0)

    for copy in loads[early:tables]:
        copy.wait()
    index = turb_v[0].astype(jnp.float32)
    line = jnp.floor((index + 0.5) * (1.0 / levels))
    level = index - levels * line
    at_x = jnp.floor((line + 0.5) * (1.0 / depth))
    line = (line - depth * at_x) * width + at_x
    slots = index.shape[-1]

    def hot(size, value):
        steps = lax.broadcasted_iota(jnp.int32, (size, slots), 0).astype(jnp.float32)
        return jnp.where(steps == value, 1.0, 0.0)

    where_row[...] = hot(area, line)
    where_lev[...] = hot(lanes, level).astype(jnp.bfloat16)
    turbine = jnp.where(turb_v[2] == 1, turb_v[1], TURB).astype(jnp.float32)
    where_turb[...] = hot(TURB, turbine)

    kx, ky, hor, decay = waves_v[0], waves_v[1], waves_v[2], waves_v[3]

    def project(chunk):
        low, high = chunk
        table = outer_v[...]
        cos, sin = twist_v[0], twist_v[1]
        blocks = []
        for place in range(low * comps, high * comps):
            head, rest = halves(recv[place])
            spun = dot(table, jnp.concatenate([head, head, rest], axis=0))
            real, imag = spun[:count], spun[count:]
            blocks.append(jnp.concatenate([real * cos - imag * sin, real * sin + imag * cos], axis=1))
        spec = shared(halves(jnp.concatenate(blocks, axis=0)), (innf_v[0], innf_v[1]))
        blocks = []
        for group in range(low, high):
            lift = rise_v[pl.ds(group, 1), :area]
            real, imag = [], []
            for comp in range(comps):
                start = ((group - low) * comps + comp) * count
                real.append(spec[start : start + count, :area])
                imag.append(spec[start : start + count, area:])
            bound = hor + lift * lift
            inverse = jnp.where(bound > 0.0, -1.0 / jnp.where(bound > 0.0, bound, 1.0), 0.0)
            press_re = (lift * real[2] - kx * imag[0] - ky * imag[1]) * inverse
            press_im = (kx * real[0] + ky * real[1] + lift * imag[2]) * inverse
            new_re = [real[0] + kx * press_im, real[1] + ky * press_im, real[2] + lift * press_re]
            new_im = [imag[0] - kx * press_re, imag[1] - ky * press_re, imag[2] + lift * press_im]
            for comp in range(comps):
                blocks.append(jnp.concatenate([new_re[comp] * decay, new_im[comp] * decay], axis=1))
        lines = shared(halves(jnp.concatenate(blocks, axis=0)), (innb_v[0], innb_v[1]))
        table = outerb_v[...]
        cos, sin = twist_v[2], twist_v[3]
        for place in range((high - low) * comps):
            real = lines[place * count : (place + 1) * count, :area]
            imag = lines[place * count : (place + 1) * count, area:]
            spun = jnp.concatenate([real * cos + imag * sin, imag * cos - real * sin], axis=0)
            head, rest = halves(spun)
            send_two[low * comps + place] = dot(table, jnp.concatenate([head, head, rest], axis=0))

    for index, chunk in enumerate(chunks):
        gathered(0, index, recv)
        project(chunk)
        keep(1, index, send_two, recv_two)
        spread(1, index, send_two, recv_two, far + near)

    def relay(index):
        return transfer(
            recv_two.at[part_of(index)], relayed.at[part_of(index)], -shift, 0,
            relay_send.at[index], relay_recv.at[index],
        )

    def levels_of(source, index, comp):
        low, high = chunks[index]
        modes = jnp.concatenate([source[g * comps + comp] for g in range(low, high)], axis=0)
        kind = comp // 2
        span = slice(low * count, high * count)
        value = shared(halves(modes.T), (vert_v[kind, 0, span], vert_v[kind, 1, span]))
        return value.reshape(depth, width, lanes)

    for index in range(len(chunks)):
        gathered(1, index, recv_two)

        @pl.when(row >= shift)
        def _():
            relay(index)[0].start()

        for comp in range(comps):
            value = levels_of(recv_two, index, comp)
            fringe[comp] = value if index == 0 else fringe[comp] + value

    @pl.when(row >= shift)
    def _():
        send_tile(fringe, 1, -shift)


    @pl.when(row < filled)
    def _():
        for index in range(len(chunks)):
            part = relayed.at[part_of(index)]
            pltpu.make_async_copy(part, part, relay_recv.at[index]).wait()
            for comp in range(comps):
                value = levels_of(relayed, index, comp)
                if index > 0:
                    value = value + stage_one[comp, 2 : depth + 2, :width]
                stage_one[comp, 2 : depth + 2, :width] = value

    inside = lax.broadcasted_iota(jnp.int32, (width, lanes), 1) < levels
    kept = lax.broadcasted_iota(jnp.int32, (width, lanes - base), 1) < tail

    def arrived(part, stage, place):
        pltpu.make_async_copy(part, part, halo_recv.at[stage, place]).wait()

    def lines_in(field, stage):
        arrived(field.at[:, pl.ds(2, depth), pl.ds(width + 6, 2)], stage, 8)
        arrived(field.at[:, pl.ds(2, depth), pl.ds(width, 2)], stage, 9)

    def side_in(field, stage, side):
        land = (depth + 2) * side
        ghost = 1 + (depth + 1) * side
        arrived(field.at[:, pl.ds(land, 2), pl.ds(0, width), pl.ds(0, base)], stage, side)
        arrived(tails_in.at[stage, side], stage, 2 + side)
        arrived(field.at[:, ghost, pl.ds(width + 7, 1)], stage, 4 + 2 * side)
        arrived(field.at[:, ghost, pl.ds(width, 1)], stage, 5 + 2 * side)
        for comp in range(comps):
            packed = tails_in[stage, side, comp]
            field[comp, land, :width, base:] = jnp.where(kept, packed, 0.0)
            packed = pltpu.roll(packed, 128 - tail, 1)
            field[comp, land + 1, :width, base:] = jnp.where(kept, packed, 0.0)

    def drag(field):
        cells = field[0, 2 : depth + 2, :width].reshape(area, lanes)
        head, rest = halves(cells)
        table = where_lev[...]
        picked = (dot(head, table) + dot(rest, table)) * where_row[...]
        values = jnp.sum(picked, axis=0, keepdims=True) + WIND
        turbs = where_turb[...]
        sums = jnp.sum(turbs * values, axis=1, keepdims=True)
        counts = jnp.sum(turbs, axis=1, keepdims=True)
        mean = sums / jnp.maximum(counts, 1.0)
        thrust = (-0.5 * THRUST * STEP) * mean * jnp.abs(mean)
        per_slot = jnp.sum(turbs * thrust, axis=0, keepdims=True)
        head, rest = halves(where_row[...] * per_slot)
        last = ((1,), (1,))
        force[...] = (dot(head, table, last) + dot(rest, table, last)).reshape(depth, width, lanes)

    def ahead(value, axis):
        return pltpu.roll(value, value.shape[axis] - 1, axis)

    def behind(value, axis):
        return pltpu.roll(value, 1, axis)

    def eddy_slab(field, j, size):
        along, across_y, up = [], [], []
        for comp in range(comps):
            value = field[comp, j]
            along.append((ahead(value, 0) - behind(value, 0))[:size])
            across_y.append(field[comp, j + 1, :size] - field[comp, j - 1, :size])
            up.append(ahead(value[:size], 1) - behind(value[:size], 1))
        shear = 0.0
        for pair in (along[1] + across_y[0], along[2] + up[0], across_y[2] + up[1]):
            shear = shear + pair * pair
        square = along[0] * along[0] + across_y[1] * across_y[1] + up[2] * up[2] + 0.5 * shear
        eddy[j - 1, :size] = (0.5 * STEP * SMAG * math.sqrt(0.5)) * jnp.sqrt(square)

    def factors(speed, viscous):
        return speed + viscous, speed - viscous

    def flux(pair, low_f, high_f):
        return pair[0] * low_f + pair[1] * high_f

    quarter = 0.25 * STEP

    def span_flux(field, j):
        speed = quarter * (field[1, j, :width] + field[1, j + 1, :width])
        pair = factors(speed, eddy[j - 1, :width] + eddy[j, :width])
        return tuple(
            flux(pair, field[comp, j, :width], field[comp, j + 1, :width]) for comp in range(comps)
        )

    def rates(field, start, size, store):
        def slab(step, below):
            j = start + step
            above = span_flux(field, j)
            viscous = eddy[j - 1]
            whole = field[0, j]
            next_u = ahead(whole, 0)
            along = factors(
                quarter * (whole + next_u) + (2.0 * quarter * WIND), viscous + ahead(viscous, 0)
            )
            inner_h = viscous[:width]
            lift = field[2, j, :width]
            next_w = ahead(lift, 1)
            rising = factors(quarter * (lift + next_w), inner_h + ahead(inner_h, 1))
            for comp in range(comps):
                value = field[comp, j]
                face = flux(along, value, next_u if comp == 0 else ahead(value, 0))
                total = (face - behind(face, 0))[:width] + (above[comp] - below[comp])
                mid = value[:width]
                face = flux(rising, mid, next_w if comp == 2 else ahead(mid, 1))
                total = total + (face - behind(face, 1))
                change = force[j - 2] - total if comp == 0 else -total
                store(comp, j, mid + change)
            return above

        lax.fori_loop(0, size, slab, span_flux(field, start - 1), unroll=2)

    first = 1 - (column + spanwise - 1) // spanwise

    def section(stage, field, store, leave, settled=lambda: None):
        drag(field)
        lines_in(field, stage)

        @pl.loop(3, depth + 1, unroll=2)
        def _(j):
            eddy_slab(field, j, width + 8)

        rates(field, 4, depth - 4, store)
        settled()

        @pl.loop(0, 2)
        def _(turn):
            side = (turn + first) % 2
            side_in(field, stage, side)

            eddy_slab(field, 1 + (depth + 1) * side, width)
            eddy_slab(field, 2 + (depth - 1) * side, width + 8)

            rates(field, 2 + (depth - 2) * side, 2, store)
            leave(side)

    def to_next(target, share):
        def store(comp, j, value):
            if share < 1.0:
                value = (1.0 - share) * stage_one[comp, j, :width] + share * value
            target[comp, j, :width] = jnp.where(inside, value, 0.0)
        return store

    def to_output(comp, j, value):
        value = stage_one[comp, j, :width] * (1.0 / 3.0) + (2.0 / 3.0) * value
        farm_v[comp, j - 2] = value[:, :levels]

    section(0, stage_one, to_next(stage_two, 1.0), lambda side: send_side(stage_two, 2, 1, 2, stage_two, 0, 1 - side))
    send_lines(stage_two, 2, 1, 2, stage_two, 0)
    outs = []
    for comp in range(comps):
        farm_v[comp] = fringe[comp][:, :, :levels]
    for y in range(depth):
        outs.append(pltpu.make_async_copy(farm_v.at[:, y], pre_new.at[:, :, y], out_sem.at[0, y]))
        outs[-1].start()
    section(1, stage_two, to_next(stage_three, 0.25), lambda side: send_side(stage_three, 2, 2, 3, stage_three, 0, 1 - side))
    send_lines(stage_three, 2, 2, 3, stage_three, 0)

    def result(y):
        return pltpu.make_async_copy(farm_v.at[:, y], farm_new.at[:, :, y], out_sem.at[1, y])

    def inner_rows():
        for y in range(2, depth - 2):
            result(y).start()

    def outer_rows(side):
        for half in (0, 1):
            result((depth - 2) * side + half).start()

    for copy in outs:
        copy.wait()
    section(2, stage_three, to_output, outer_rows, inner_rows)
    for index in range(len(chunks)):
        sent(0, index, send)
        sent(1, index, send_two)
    for stage, field in ((1, stage_two), (2, stage_three)):
        copies = line_copies(field, 2, stage, stage + 1, field, 0)
        for side in (0, 1):
            copies += side_copies(field, 2, stage, stage + 1, field, 0, side)
        for copy, remote in copies:
            if remote:
                copy.wait_send()

    @pl.when(row >= shift)
    def _():
        tile_sent(fringe, 1, -shift)
        for index in range(len(chunks)):
            copy, remote = relay(index)
            if remote:
                copy.wait_send()

    @pl.when(row >= filled)
    def _():
        tile_sent(own, 0, 0)

    for y in range(depth):
        result(y).wait()


def write_out(farm, pre, farm_new, pre_new, hold, in_sem, out_sem):
    pieces = []
    for place, (source, target) in enumerate(((pre, pre_new), (farm, farm_new))):
        for comp in range(source.shape[0]):
            seat = hold.at[place, comp]
            pieces.append((
                pltpu.make_async_copy(source.at[comp], seat, in_sem.at[place, comp]),
                pltpu.make_async_copy(seat, target.at[comp], out_sem.at[place, comp]),
            ))
    for copy, _ in pieces:
        copy.start()
    for copy, onward in pieces:
        copy.wait()
        onward.start()
    for _, onward in pieces:
        onward.wait()


def shards(across, spanwise, farm, pre, turb_cell, turb_slot, disk_mask):
    comps, width, depth, levels = pre.shape
    count = across * spanwise
    area = width * depth
    slots = turb_cell.shape[-1]
    lanes = -(-(levels + 2) // 128) * 128
    groups = -(-levels // count)
    tables = [jnp.asarray(t) for t in spectral_tables(across, spanwise, width, depth, levels, lanes)]
    anywhere = pl.BlockSpec(memory_space=pl.ANY)
    f32 = jnp.float32

    def vmem(*shape, dtype=f32):
        return pltpu.VMEM(shape, dtype)

    def sems(*shape):
        return pltpu.SemaphoreType.DMA(shape)

    modes = vmem(groups * comps, count, area)
    cells = vmem(comps, depth, width, lanes)
    padded = vmem(comps, depth + 4, width + 8, lanes)
    results = [jax.ShapeDtypeStruct(farm.shape, f32), jax.ShapeDtypeStruct(pre.shape, f32)]
    farm_new, pre_new = pl.pallas_call(
        functools.partial(step_body, across, spanwise),
        out_shape=results,
        in_specs=[anywhere] * (5 + len(tables)),
        out_specs=[anywhere] * 2,
        scratch_shapes=[
            vmem(comps, area, levels),
            vmem(comps, depth, width, levels),
            vmem(3, 1, slots, dtype=jnp.int32),
            *[vmem(*t.shape, dtype=t.dtype) for t in tables[:-1]],
            vmem(*tables[-1].shape[1:]),
            modes, modes, modes, modes, modes,
            cells, cells, padded, padded, padded,
            vmem(4, 2, comps, width, 128),
            vmem(3, 2, comps, width, 128),
            vmem(depth + 2, width + 8, lanes),
            vmem(depth, width, lanes),
            vmem(area, slots),
            vmem(lanes, slots, dtype=jnp.bfloat16),
            vmem(TURB, slots),
            sems(comps + 2 + 10 + depth),
            sems(2, len(SHARES)),
            sems(2, len(SHARES)),
            sems(len(SHARES)),
            sems(len(SHARES)),
            sems(4, 10),
            sems(3, 10),
            pltpu.SemaphoreType.REGULAR((2,)),
            sems(2, depth),
        ],
        compiler_params=pltpu.CompilerParams(collective_id=0, has_side_effects=True),
        name="step",
    )(
        pre.reshape(comps, area, levels), farm,
        turb_cell.reshape(1, slots), turb_slot.reshape(1, slots), disk_mask.reshape(1, slots),
        *tables,
    )
    return pl.pallas_call(
        write_out,
        out_shape=results,
        in_specs=[anywhere] * 2,
        out_specs=[anywhere] * 2,
        scratch_shapes=[vmem(2, comps, width, depth, levels), sems(2, comps), sems(2, comps)],
        name="write_out",
    )(farm_new, pre_new)


def solution(mesh):
    across, spanwise = mesh.shape["gx"], mesh.shape["gy"]
    return jax.shard_map(
        functools.partial(shards, across, spanwise),
        mesh=mesh,
        in_specs=(
            P(None, "gx", "gy", None),
            P(None, "gx", "gy", None),
            P("gx", "gy", None),
            P("gx", "gy", None),
            P("gx", "gy", None),
        ),
        out_specs=(P(None, "gx", "gy", None), P(None, "gx", "gy", None)),
        check_vma=False,
    )
```

```python
import functools
import math

import jax
import jax.numpy as jnp
import numpy as np
from jax import lax
from jax.experimental import pallas as pl
from jax.experimental.pallas import tpu as pltpu
from jax.sharding import PartitionSpec as P

NF = 48
TURB = 16
WIND = 3.0
STEP = 0.1
SMAG = 0.0289
THRUST = 1.33
DIFFUSE = 0.05
MESH = pl.DeviceIdType.MESH
UNROLL = 1
SHARES = (1 / 3, 1 / 6, 1 / 3, 1 / 6)


def split_pair(table):
    table = np.asarray(table, np.float32)
    head = table.astype(jnp.bfloat16)
    tail = (table - head.astype(np.float32)).astype(jnp.bfloat16)
    return np.stack([head, tail])


def shared(left, right):
    rows = left[0].shape[0]
    both = dot(jnp.concatenate(left, axis=0), right[0])
    return both[:rows] + (both[rows:] + dot(left[0], right[1]))


def stacked(table):
    head, tail = split_pair(table)
    return np.concatenate([head, tail, head], axis=1)


def spectral_tables(across, spanwise, width, depth, levels, lanes):
    count = across * spanwise
    total_x, total_y = across * width, spanwise * depth
    groups = -(-levels // count)
    order = np.arange(groups * count)[:, None]
    height = np.arange(levels)[None, :]
    inside = order < levels
    scale = np.where(order == 0, math.sqrt(1.0 / levels), math.sqrt(2.0 / levels)) * inside
    centre = scale * np.cos(math.pi / (2 * levels) * (order * (2 * height + 1) % (4 * levels)))
    face = (
        math.sqrt(2.0 / levels)
        * np.sin(math.pi / levels * (order * (height + 1) % (2 * levels)))
        * ((height < levels - 1) & (order > 0) & inside)
    )
    pad = ((0, 0), (0, 0), (0, lanes - levels))
    vertical = np.stack([np.pad(split_pair(centre), pad), np.pad(split_pair(face), pad)])
    rise = 2.0 * np.sin(np.minimum(order, levels)[:, 0] * (math.pi / (2 * levels)))
    rise = np.pad(rise.reshape(groups, count).T, ((0, 0), (0, -groups % 8)))
    rise = np.broadcast_to(rise[:, :, None], rise.shape + (128,))
    tile = np.arange(count)
    tile_x, tile_y = tile // spanwise, tile % spanwise
    turn = 2.0 * math.pi * (np.outer(tile_x, tile_x) / across + np.outer(tile_y, tile_y) / spanwise)
    outer = np.concatenate([np.cos(turn), -np.sin(turn)], axis=0)
    outer_back = np.concatenate([np.cos(turn), -np.sin(turn)], axis=1)
    lane = np.arange(width * depth)
    lane_x, lane_y = lane // depth, lane % depth
    back = (lane % width) * depth + lane // width
    angle = 2.0 * math.pi * (np.outer(tile_x, lane_x) / total_x + np.outer(tile_y, lane_y) / total_y)
    twist = np.stack([np.cos(angle), -np.sin(angle), np.cos(angle)[:, back], -np.sin(angle)[:, back]])
    turn = 2.0 * math.pi * (np.outer(lane_x, lane_x) / width + np.outer(lane_y, lane_y) / depth)
    real, imag = np.cos(turn), np.sin(turn)
    inner_forward = np.block([[real, -imag], [imag, real]])
    real, imag = real[:, back], imag[:, back]
    inner_back = np.block([[real, imag], [-imag, real]])
    k = tile_x[:, None] + across * lane_x[None, :]
    q = tile_y[:, None] + spanwise * lane_y[None, :]
    kx = 2.0 * math.pi / total_x * np.where(k < total_x // 2, k, k - total_x)
    ky = 2.0 * math.pi / total_y * np.where(q < total_y // 2, q, q - total_y)
    hor = kx * kx + ky * ky
    kept = (k != total_x // 2) & (q != total_y // 2)
    decay = np.exp(-DIFFUSE * hor) * kept / (total_x * total_y)
    waves = np.stack([kx, ky, hor, decay])
    return (
        vertical,
        stacked(outer),
        stacked(outer_back),
        split_pair(inner_forward),
        split_pair(inner_back),
        twist.astype(np.float32),
        waves.astype(np.float32),
        rise.astype(np.float32),
    )


def halves(value):
    head = value.astype(jnp.bfloat16)
    return head, (value - head.astype(jnp.float32)).astype(jnp.bfloat16)


def dot(left, right, dims=((1,), (0,))):
    return lax.dot_general(
        left, right, dimension_numbers=(dims, ((), ())), preferred_element_type=jnp.float32
    )


def product(left, right, dims=((1,), (0,))):
    return dot(left[0], right[0], dims) + (dot(left[0], right[1], dims) + dot(left[1], right[0], dims))


def step_body(
    across, spanwise, pre, farm, cell, slot, live, vertical, outer, outer_back, inner_f, inner_b,
    twist, waves, rise, farm_new, pre_new,
    pre_v, farm_v, turb_v, vert_v, outer_v, outerb_v, innf_v, innb_v, twist_v, waves_v, rise_v,
    send, recv, send_two, recv_two, relayed, fringe, own, stage_one, stage_two, stage_three, tails_out,
    tails_in, eddy, force, where_row, where_lev, where_turb, load_sem, a2a_send, a2a_recv, relay_send,
    relay_recv, halo_send, halo_recv, known, out_sem,
):
    count = across * spanwise
    comps, width, depth, levels = farm.shape
    area = width * depth
    lanes = fringe.shape[-1]
    base = lanes - 128
    tail = levels - base
    groups = send.shape[0] // comps
    filled = NF // width
    shift = across - filled
    row, column = lax.axis_index("gx"), lax.axis_index("gy")
    position = row * spanwise + column
    barrier = pltpu.get_barrier_semaphore()

    loads = []
    for comp in range(comps):
        loads.append(pltpu.make_async_copy(pre.at[comp], pre_v.at[comp], load_sem.at[comp]))
    for kind in range(2):
        loads.append(pltpu.make_async_copy(vertical.at[kind], vert_v.at[kind], load_sem.at[comps + kind]))
    early = len(loads)
    for copy in loads:
        copy.start()

    bands = 4 if spanwise % 4 == 0 else 1
    deep = spanwise // bands
    band = column // deep
    crowd = deep * across
    seat = lax.rem(column, deep)

    def each_in(delta, action):
        def all_of():
            cols = [(band + delta) * deep + lax.rem(seat + step, deep) for step in range(deep)]

            @pl.loop(1, across + (delta != 0), unroll=UNROLL)
            def _(step):
                peer_row = lax.rem(row + step, across)
                for col in cols:
                    action(peer_row, col)

            if delta == 0:
                for col in cols[1:]:
                    action(row, col)

        if delta == 0:
            all_of()
        elif delta > 0:
            pl.when(band < bands - delta)(all_of)
        else:
            pl.when(band >= -delta)(all_of)

    def greet(peer_row, peer_col):
        pl.semaphore_signal(barrier, inc=1, device_id=(peer_row, peer_col), device_id_type=MESH)

    def tell(semaphore, delta):
        pl.semaphore_signal(
            semaphore, inc=1, device_id=(row, column + delta * deep), device_id_type=MESH
        )

    near = (0,) if bands == 1 else (1, -1, 0)
    for delta in near[::-1]:
        each_in(delta, greet)

    for index, (source, target) in enumerate((
        (outer, outer_v), (outer_back, outerb_v), (inner_f, innf_v), (inner_b, innb_v),
        (twist, twist_v), (waves, waves_v), (rise.at[position], rise_v),
        (cell, turb_v.at[0]), (slot, turb_v.at[1]), (live, turb_v.at[2]),
    )):
        loads.append(pltpu.make_async_copy(source, target, load_sem.at[early + index]))
    tables = len(loads)
    for y in range(depth):
        loads.append(pltpu.make_async_copy(farm.at[:, :, y], farm_v.at[:, y], load_sem.at[tables + y]))
    for copy in loads[early:]:
        copy.start()

    chunks = []
    start = 0
    for share in SHARES:
        stop = min(groups, start + max(1, round(share * groups)))
        if start < stop:
            chunks.append((start, stop))
        start = stop
    chunks[-1] = (chunks[-1][0], groups)

    def part_of(index):
        low, high = chunks[index]
        return pl.ds(low * comps, (high - low) * comps)

    def spread(leg, index, source, target, deltas):
        part = part_of(index)

        def post(peer_row, peer_col):
            pltpu.make_async_remote_copy(
                src_ref=source.at[part, peer_row * spanwise + peer_col],
                dst_ref=target.at[part, position],
                send_sem=a2a_send.at[leg, index],
                recv_sem=a2a_recv.at[leg, index],
                device_id=(peer_row, peer_col),
                device_id_type=MESH,
            ).start()

        for delta in deltas:
            each_in(delta, post)

    def keep(leg, index, source, target):
        part = part_of(index)
        pltpu.make_async_copy(
            source.at[part, position], target.at[part, position], a2a_recv.at[leg, index]
        ).start()

    def gathered(leg, index, target):
        part = target.at[part_of(index)]
        pltpu.make_async_copy(part, part, a2a_recv.at[leg, index]).wait()

    def sent(leg, index, source):
        part = source.at[part_of(index), pl.ds(0, count - 1)]
        pltpu.make_async_copy(part, part, a2a_send.at[leg, index]).wait()

    for copy in loads[:early]:
        copy.wait()
    columns = [halves(pre_v[comp]) for comp in range(comps)]

    def transform(index):
        low, high = chunks[index]
        span = slice(low * count, high * count)
        for comp in range(comps):
            kind = comp // 2
            table = (vert_v[kind, 0, span][:, :levels], vert_v[kind, 1, span][:, :levels])
            modes = product(table, columns[comp], ((1,), (1,)))
            for group in range(low, high):
                send[group * comps + comp] = modes[(group - low) * count : (group - low + 1) * count]

    far = () if bands == 1 else (2, -2, 3, -3)
    middle = ((band + 1) // 2) % 2
    for index in range(len(chunks)):
        transform(index)
        if index == 0:
            if bands == 1:
                pl.semaphore_wait(barrier, count - 1)
            else:
                pl.semaphore_wait(barrier, (2 + middle) * crowd - 1)

                @pl.when(middle == 1)
                def _():
                    tell(known.at[0], 1)
                    tell(known.at[0], -1)

            spread(0, index, send, recv, near)
            if bands > 1:
                pl.semaphore_wait(known.at[0], 1)

                @pl.when(band == 1)
                def _():
                    tell(known.at[1], -1)

                @pl.when(band == 2)
                def _():
                    tell(known.at[1], 1)

                spread(0, index, send, recv, far[:2])

                @pl.when(middle == 0)
                def _():
                    pl.semaphore_wait(known.at[1], 1)

                spread(0, index, send, recv, far[2:])
        else:
            spread(0, index, send, recv, far + near)
        keep(0, index, send, recv)

    def transfer(source, target, step_row, step_col, send_sem, recv_sem):
        if isinstance(step_col, int) and step_row % across == 0 and step_col % spanwise == 0:
            return pltpu.make_async_copy(source, target, recv_sem), False
        copy = pltpu.make_async_remote_copy(
            src_ref=source, dst_ref=target, send_sem=send_sem, recv_sem=recv_sem,
            device_id=((row + step_row) % across, (column + step_col) % spanwise),
            device_id_type=MESH,
        )
        return copy, True

    def side_copies(source, at, stage, role, target, offset, side):
        step = 1 - 2 * side
        near = at + (depth - 2) * (1 - side)
        edge = at + (depth - 1) * (1 - side)
        land = (depth + 2) * side
        ghost = 1 + (depth + 1) * side
        use = lambda place: (halo_send.at[role, place], halo_recv.at[stage, place])
        return [
            transfer(
                source.at[:, pl.ds(near, 2), pl.ds(0, width), pl.ds(0, base)],
                target.at[:, pl.ds(land, 2), pl.ds(0, width), pl.ds(0, base)],
                offset, step, *use(side),
            ),
            transfer(tails_out.at[role, side], tails_in.at[stage, side], offset, step, *use(2 + side)),
            transfer(
                source.at[:, edge, pl.ds(width - 1, 1)], target.at[:, ghost, pl.ds(width + 7, 1)],
                offset + 1, step, *use(4 + 2 * side),
            ),
            transfer(
                source.at[:, edge, pl.ds(0, 1)], target.at[:, ghost, pl.ds(width, 1)],
                offset - 1, step, *use(5 + 2 * side),
            ),
        ]

    def line_copies(source, at, stage, role, target, offset):
        rows = pl.ds(at, depth)
        use = lambda place: (halo_send.at[role, place], halo_recv.at[stage, place])
        return [
            transfer(
                source.at[:, rows, pl.ds(width - 2, 2)], target.at[:, pl.ds(2, depth), pl.ds(width + 6, 2)],
                offset + 1, 0, *use(8),
            ),
            transfer(
                source.at[:, rows, pl.ds(0, 2)], target.at[:, pl.ds(2, depth), pl.ds(width, 2)],
                offset - 1, 0, *use(9),
            ),
        ]

    def pack(source, at, role, side):
        near = at + (depth - 2) * (1 - side)
        for comp in range(comps):
            tails_out[role, side, comp] = source[comp, near, :width, base:] + pltpu.roll(
                source[comp, near + 1, :width, base:], tail, 1
            )

    def send_side(source, at, stage, role, target, offset, side):
        pack(source, at, role, side)
        copies = side_copies(source, at, stage, role, target, offset, side)
        for copy, _ in copies:
            copy.start()
        return copies

    def send_lines(source, at, stage, role, target, offset):
        copies = line_copies(source, at, stage, role, target, offset)
        for copy, _ in copies:
            copy.start()
        return copies

    def send_tile(source, role, offset):
        copies = send_lines(source, 0, 0, role, stage_one, offset)
        for side in (0, 1):
            copies += send_side(source, 0, 0, role, stage_one, offset, side)
        return copies

    def tile_sent(source, role, offset):
        copies = line_copies(source, 0, 0, role, stage_one, offset)
        for side in (0, 1):
            copies += side_copies(source, 0, 0, role, stage_one, offset, side)
        for copy, remote in copies:
            if remote:
                copy.wait_send()

    for copy in loads[tables:]:
        copy.wait()
    blank = jnp.zeros((width, lanes - base), jnp.float32)

    @pl.when(row >= filled)
    def _():
        for comp in range(comps):
            for y in range(depth):
                own[comp, y, :, base:] = blank
                own[comp, y, :, :levels] = farm_v[comp, y]
                stage_one[comp, 2 + y, :width] = own[comp, y]
        send_tile(own, 0, 0)

    for copy in loads[early:tables]:
        copy.wait()
    index = turb_v[0].astype(jnp.float32)
    line = jnp.floor((index + 0.5) * (1.0 / levels))
    level = index - levels * line
    at_x = jnp.floor((line + 0.5) * (1.0 / depth))
    line = (line - depth * at_x) * width + at_x
    slots = index.shape[-1]

    def hot(size, value):
        steps = lax.broadcasted_iota(jnp.int32, (size, slots), 0).astype(jnp.float32)
        return jnp.where(steps == value, 1.0, 0.0)

    where_row[...] = hot(area, line)
    where_lev[...] = hot(lanes, level).astype(jnp.bfloat16)
    turbine = jnp.where(turb_v[2] == 1, turb_v[1], TURB).astype(jnp.float32)
    where_turb[...] = hot(TURB, turbine)

    kx, ky, hor, decay = waves_v[0], waves_v[1], waves_v[2], waves_v[3]

    def project(chunk):
        low, high = chunk
        table = outer_v[...]
        cos, sin = twist_v[0], twist_v[1]
        blocks = []
        for place in range(low * comps, high * comps):
            head, rest = halves(recv[place])
            spun = dot(table, jnp.concatenate([head, head, rest], axis=0))
            real, imag = spun[:count], spun[count:]
            blocks.append(jnp.concatenate([real * cos - imag * sin, real * sin + imag * cos], axis=1))
        spec = shared(halves(jnp.concatenate(blocks, axis=0)), (innf_v[0], innf_v[1]))
        blocks = []
        for group in range(low, high):
            lift = rise_v[pl.ds(group, 1), :area]
            real, imag = [], []
            for comp in range(comps):
                start = ((group - low) * comps + comp) * count
                real.append(spec[start : start + count, :area])
                imag.append(spec[start : start + count, area:])
            bound = hor + lift * lift
            inverse = jnp.where(bound > 0.0, -1.0 / jnp.where(bound > 0.0, bound, 1.0), 0.0)
            press_re = (lift * real[2] - kx * imag[0] - ky * imag[1]) * inverse
            press_im = (kx * real[0] + ky * real[1] + lift * imag[2]) * inverse
            new_re = [real[0] + kx * press_im, real[1] + ky * press_im, real[2] + lift * press_re]
            new_im = [imag[0] - kx * press_re, imag[1] - ky * press_re, imag[2] + lift * press_im]
            for comp in range(comps):
                blocks.append(jnp.concatenate([new_re[comp] * decay, new_im[comp] * decay], axis=1))
        lines = shared(halves(jnp.concatenate(blocks, axis=0)), (innb_v[0], innb_v[1]))
        table = outerb_v[...]
        cos, sin = twist_v[2], twist_v[3]
        for place in range((high - low) * comps):
            real = lines[place * count : (place + 1) * count, :area]
            imag = lines[place * count : (place + 1) * count, area:]
            spun = jnp.concatenate([real * cos + imag * sin, imag * cos - real * sin], axis=0)
            head, rest = halves(spun)
            send_two[low * comps + place] = dot(table, jnp.concatenate([head, head, rest], axis=0))

    for index, chunk in enumerate(chunks):
        gathered(0, index, recv)
        project(chunk)
        keep(1, index, send_two, recv_two)
        spread(1, index, send_two, recv_two, far + near)

    def relay(index):
        return transfer(
            recv_two.at[part_of(index)], relayed.at[part_of(index)], -shift, 0,
            relay_send.at[index], relay_recv.at[index],
        )

    def levels_of(source, index, comp):
        low, high = chunks[index]
        modes = jnp.concatenate([source[g * comps + comp] for g in range(low, high)], axis=0)
        kind = comp // 2
        span = slice(low * count, high * count)
        value = shared(halves(modes.T), (vert_v[kind, 0, span], vert_v[kind, 1, span]))
        return value.reshape(depth, width, lanes)

    for index in range(len(chunks)):
        gathered(1, index, recv_two)

        @pl.when(row >= shift)
        def _():
            relay(index)[0].start()

        for comp in range(comps):
            value = levels_of(recv_two, index, comp)
            fringe[comp] = value if index == 0 else fringe[comp] + value

    @pl.when(row >= shift)
    def _():
        send_tile(fringe, 1, -shift)


    @pl.when(row < filled)
    def _():
        for index in range(len(chunks)):
            part = relayed.at[part_of(index)]
            pltpu.make_async_copy(part, part, relay_recv.at[index]).wait()
            for comp in range(comps):
                value = levels_of(relayed, index, comp)
                if index > 0:
                    value = value + stage_one[comp, 2 : depth + 2, :width]
                stage_one[comp, 2 : depth + 2, :width] = value

    inside = lax.broadcasted_iota(jnp.int32, (width, lanes), 1) < levels
    kept = lax.broadcasted_iota(jnp.int32, (width, lanes - base), 1) < tail

    def arrived(part, stage, place):
        pltpu.make_async_copy(part, part, halo_recv.at[stage, place]).wait()

    def lines_in(field, stage):
        arrived(field.at[:, pl.ds(2, depth), pl.ds(width + 6, 2)], stage, 8)
        arrived(field.at[:, pl.ds(2, depth), pl.ds(width, 2)], stage, 9)

    def side_in(field, stage, side):
        land = (depth + 2) * side
        ghost = 1 + (depth + 1) * side
        arrived(field.at[:, pl.ds(land, 2), pl.ds(0, width), pl.ds(0, base)], stage, side)
        arrived(tails_in.at[stage, side], stage, 2 + side)
        arrived(field.at[:, ghost, pl.ds(width + 7, 1)], stage, 4 + 2 * side)
        arrived(field.at[:, ghost, pl.ds(width, 1)], stage, 5 + 2 * side)
        for comp in range(comps):
            packed = tails_in[stage, side, comp]
            field[comp, land, :width, base:] = jnp.where(kept, packed, 0.0)
            packed = pltpu.roll(packed, 128 - tail, 1)
            field[comp, land + 1, :width, base:] = jnp.where(kept, packed, 0.0)

    def drag(field):
        cells = field[0, 2 : depth + 2, :width].reshape(area, lanes)
        head, rest = halves(cells)
        table = where_lev[...]
        picked = (dot(head, table) + dot(rest, table)) * where_row[...]
        values = jnp.sum(picked, axis=0, keepdims=True) + WIND
        turbs = where_turb[...]
        sums = jnp.sum(turbs * values, axis=1, keepdims=True)
        counts = jnp.sum(turbs, axis=1, keepdims=True)
        mean = sums / jnp.maximum(counts, 1.0)
        thrust = (-0.5 * THRUST * STEP) * mean * jnp.abs(mean)
        per_slot = jnp.sum(turbs * thrust, axis=0, keepdims=True)
        head, rest = halves(where_row[...] * per_slot)
        last = ((1,), (1,))
        force[...] = (dot(head, table, last) + dot(rest, table, last)).reshape(depth, width, lanes)

    def ahead(value, axis):
        return pltpu.roll(value, value.shape[axis] - 1, axis)

    def behind(value, axis):
        return pltpu.roll(value, 1, axis)

    def eddy_slab(field, j, size):
        along, across_y, up = [], [], []
        for comp in range(comps):
            value = field[comp, j]
            along.append((ahead(value, 0) - behind(value, 0))[:size])
            across_y.append(field[comp, j + 1, :size] - field[comp, j - 1, :size])
            up.append(ahead(value[:size], 1) - behind(value[:size], 1))
        shear = 0.0
        for pair in (along[1] + across_y[0], along[2] + up[0], across_y[2] + up[1]):
            shear = shear + pair * pair
        square = along[0] * along[0] + across_y[1] * across_y[1] + up[2] * up[2] + 0.5 * shear
        eddy[j - 1, :size] = (0.5 * STEP * SMAG * math.sqrt(0.5)) * jnp.sqrt(square)

    def factors(speed, viscous):
        return speed + viscous, speed - viscous

    def flux(pair, low_f, high_f):
        return pair[0] * low_f + pair[1] * high_f

    quarter = 0.25 * STEP

    def span_flux(field, j):
        speed = quarter * (field[1, j, :width] + field[1, j + 1, :width])
        pair = factors(speed, eddy[j - 1, :width] + eddy[j, :width])
        return tuple(
            flux(pair, field[comp, j, :width], field[comp, j + 1, :width]) for comp in range(comps)
        )

    def rates(field, start, size, store):
        def slab(step, below):
            j = start + step
            above = span_flux(field, j)
            viscous = eddy[j - 1]
            whole = field[0, j]
            next_u = ahead(whole, 0)
            along = factors(
                quarter * (whole + next_u) + (2.0 * quarter * WIND), viscous + ahead(viscous, 0)
            )
            inner_h = viscous[:width]
            lift = field[2, j, :width]
            next_w = ahead(lift, 1)
            rising = factors(quarter * (lift + next_w), inner_h + ahead(inner_h, 1))
            for comp in range(comps):
                value = field[comp, j]
                face = flux(along, value, next_u if comp == 0 else ahead(value, 0))
                total = (face - behind(face, 0))[:width] + (above[comp] - below[comp])
                mid = value[:width]
                face = flux(rising, mid, next_w if comp == 2 else ahead(mid, 1))
                total = total + (face - behind(face, 1))
                change = force[j - 2] - total if comp == 0 else -total
                store(comp, j, mid + change)
            return above

        lax.fori_loop(0, size, slab, span_flux(field, start - 1), unroll=2)

    first = 1 - column % 2

    def section(stage, field, store, leave, settled=lambda: None):
        drag(field)
        lines_in(field, stage)

        @pl.loop(3, depth + 1, unroll=2)
        def _(j):
            eddy_slab(field, j, width + 8)

        rates(field, 4, depth - 4, store)
        settled()

        @pl.loop(0, 2)
        def _(turn):
            side = (turn + first) % 2
            side_in(field, stage, side)

            eddy_slab(field, 1 + (depth + 1) * side, width)
            eddy_slab(field, 2 + (depth - 1) * side, width + 8)

            rates(field, 2 + (depth - 2) * side, 2, store)
            leave(side)

    def to_next(target, share):
        def store(comp, j, value):
            if share < 1.0:
                value = (1.0 - share) * stage_one[comp, j, :width] + share * value
            target[comp, j, :width] = jnp.where(inside, value, 0.0)
        return store

    def to_output(comp, j, value):
        value = stage_one[comp, j, :width] * (1.0 / 3.0) + (2.0 / 3.0) * value
        farm_v[comp, j - 2] = value[:, :levels]

    section(0, stage_one, to_next(stage_two, 1.0), lambda side: send_side(stage_two, 2, 1, 2, stage_two, 0, 1 - side))
    send_lines(stage_two, 2, 1, 2, stage_two, 0)
    outs = []
    for comp in range(comps):
        farm_v[comp] = fringe[comp][:, :, :levels]
    for y in range(depth):
        outs.append(pltpu.make_async_copy(farm_v.at[:, y], pre_new.at[:, :, y], out_sem.at[0, y]))
        outs[-1].start()
    section(1, stage_two, to_next(stage_three, 0.25), lambda side: send_side(stage_three, 2, 2, 3, stage_three, 0, 1 - side))
    send_lines(stage_three, 2, 2, 3, stage_three, 0)

    def result(y):
        return pltpu.make_async_copy(farm_v.at[:, y], farm_new.at[:, :, y], out_sem.at[1, y])

    def inner_rows():
        for y in range(2, depth - 2):
            result(y).start()

    def outer_rows(side):
        for half in (0, 1):
            result((depth - 2) * side + half).start()

    for copy in outs:
        copy.wait()
    section(2, stage_three, to_output, outer_rows, inner_rows)
    for index in range(len(chunks)):
        sent(0, index, send)
        sent(1, index, send_two)
    for stage, field in ((1, stage_two), (2, stage_three)):
        copies = line_copies(field, 2, stage, stage + 1, field, 0)
        for side in (0, 1):
            copies += side_copies(field, 2, stage, stage + 1, field, 0, side)
        for copy, remote in copies:
            if remote:
                copy.wait_send()

    @pl.when(row >= shift)
    def _():
        tile_sent(fringe, 1, -shift)
        for index in range(len(chunks)):
            copy, remote = relay(index)
            if remote:
                copy.wait_send()

    @pl.when(row >= filled)
    def _():
        tile_sent(own, 0, 0)

    for y in range(depth):
        result(y).wait()


def write_out(farm, pre, farm_new, pre_new, hold, in_sem, out_sem):
    pieces = []
    for place, (source, target) in enumerate(((pre, pre_new), (farm, farm_new))):
        for comp in range(source.shape[0]):
            seat = hold.at[place, comp]
            pieces.append((
                pltpu.make_async_copy(source.at[comp], seat, in_sem.at[place, comp]),
                pltpu.make_async_copy(seat, target.at[comp], out_sem.at[place, comp]),
            ))
    for copy, _ in pieces:
        copy.start()
    for copy, onward in pieces:
        copy.wait()
        onward.start()
    for _, onward in pieces:
        onward.wait()


def shards(across, spanwise, farm, pre, turb_cell, turb_slot, disk_mask):
    comps, width, depth, levels = pre.shape
    count = across * spanwise
    area = width * depth
    slots = turb_cell.shape[-1]
    lanes = -(-(levels + 2) // 128) * 128
    groups = -(-levels // count)
    tables = [jnp.asarray(t) for t in spectral_tables(across, spanwise, width, depth, levels, lanes)]
    anywhere = pl.BlockSpec(memory_space=pl.ANY)
    f32 = jnp.float32

    def vmem(*shape, dtype=f32):
        return pltpu.VMEM(shape, dtype)

    def sems(*shape):
        return pltpu.SemaphoreType.DMA(shape)

    modes = vmem(groups * comps, count, area)
    cells = vmem(comps, depth, width, lanes)
    padded = vmem(comps, depth + 4, width + 8, lanes)
    results = [jax.ShapeDtypeStruct(farm.shape, f32), jax.ShapeDtypeStruct(pre.shape, f32)]
    farm_new, pre_new = pl.pallas_call(
        functools.partial(step_body, across, spanwise),
        out_shape=results,
        in_specs=[anywhere] * (5 + len(tables)),
        out_specs=[anywhere] * 2,
        scratch_shapes=[
            vmem(comps, area, levels),
            vmem(comps, depth, width, levels),
            vmem(3, 1, slots, dtype=jnp.int32),
            *[vmem(*t.shape, dtype=t.dtype) for t in tables[:-1]],
            vmem(*tables[-1].shape[1:]),
            modes, modes, modes, modes, modes,
            cells, cells, padded, padded, padded,
            vmem(4, 2, comps, width, 128),
            vmem(3, 2, comps, width, 128),
            vmem(depth + 2, width + 8, lanes),
            vmem(depth, width, lanes),
            vmem(area, slots),
            vmem(lanes, slots, dtype=jnp.bfloat16),
            vmem(TURB, slots),
            sems(comps + 2 + 10 + depth),
            sems(2, len(SHARES)),
            sems(2, len(SHARES)),
            sems(len(SHARES)),
            sems(len(SHARES)),
            sems(4, 10),
            sems(3, 10),
            pltpu.SemaphoreType.REGULAR((2,)),
            sems(2, depth),
        ],
        compiler_params=pltpu.CompilerParams(collective_id=0, has_side_effects=True),
        name="step",
    )(
        pre.reshape(comps, area, levels), farm,
        turb_cell.reshape(1, slots), turb_slot.reshape(1, slots), disk_mask.reshape(1, slots),
        *tables,
    )
    return pl.pallas_call(
        write_out,
        out_shape=results,
        in_specs=[anywhere] * 2,
        out_specs=[anywhere] * 2,
        scratch_shapes=[vmem(2, comps, width, depth, levels), sems(2, comps), sems(2, comps)],
        name="write_out",
    )(farm_new, pre_new)


def solution(mesh):
    across, spanwise = mesh.shape["gx"], mesh.shape["gy"]
    return jax.shard_map(
        functools.partial(shards, across, spanwise),
        mesh=mesh,
        in_specs=(
            P(None, "gx", "gy", None),
            P(None, "gx", "gy", None),
            P("gx", "gy", None),
            P("gx", "gy", None),
            P("gx", "gy", None),
        ),
        out_specs=(P(None, "gx", "gy", None), P(None, "gx", "gy", None)),
        check_vma=False,
    )
```

```python
import functools
import math

import jax
import jax.numpy as jnp
import numpy as np
from jax import lax
from jax.experimental import pallas as pl
from jax.experimental.pallas import tpu as pltpu
from jax.sharding import PartitionSpec as P

NF = 48
TURB = 16
WIND = 3.0
STEP = 0.1
SMAG = 0.0289
THRUST = 1.33
DIFFUSE = 0.05
MESH = pl.DeviceIdType.MESH
UNROLL = 1
SHARES = (1 / 3, 1 / 6, 1 / 3, 1 / 6)


def split_pair(table):
    table = np.asarray(table, np.float32)
    head = table.astype(jnp.bfloat16)
    tail = (table - head.astype(np.float32)).astype(jnp.bfloat16)
    return np.stack([head, tail])


def shared(left, right):
    rows = left[0].shape[0]
    both = dot(jnp.concatenate(left, axis=0), right[0])
    return both[:rows] + (both[rows:] + dot(left[0], right[1]))


def stacked(table):
    head, tail = split_pair(table)
    return np.concatenate([head, tail, head], axis=1)


def spectral_tables(across, spanwise, width, depth, levels, lanes):
    count = across * spanwise
    total_x, total_y = across * width, spanwise * depth
    groups = -(-levels // count)
    order = np.arange(groups * count)[:, None]
    height = np.arange(levels)[None, :]
    inside = order < levels
    scale = np.where(order == 0, math.sqrt(1.0 / levels), math.sqrt(2.0 / levels)) * inside
    centre = scale * np.cos(math.pi / (2 * levels) * (order * (2 * height + 1) % (4 * levels)))
    face = (
        math.sqrt(2.0 / levels)
        * np.sin(math.pi / levels * (order * (height + 1) % (2 * levels)))
        * ((height < levels - 1) & (order > 0) & inside)
    )
    pad = ((0, 0), (0, 0), (0, lanes - levels))
    vertical = np.stack([np.pad(split_pair(centre), pad), np.pad(split_pair(face), pad)])
    rise = 2.0 * np.sin(np.minimum(order, levels)[:, 0] * (math.pi / (2 * levels)))
    rise = np.pad(rise.reshape(groups, count).T, ((0, 0), (0, -groups % 8)))
    rise = np.broadcast_to(rise[:, :, None], rise.shape + (128,))
    tile = np.arange(count)
    tile_x, tile_y = tile // spanwise, tile % spanwise
    turn = 2.0 * math.pi * (np.outer(tile_x, tile_x) / across + np.outer(tile_y, tile_y) / spanwise)
    outer = np.concatenate([np.cos(turn), -np.sin(turn)], axis=0)
    outer_back = np.concatenate([np.cos(turn), -np.sin(turn)], axis=1)
    lane = np.arange(width * depth)
    lane_x, lane_y = lane // depth, lane % depth
    back = (lane % width) * depth + lane // width
    angle = 2.0 * math.pi * (np.outer(tile_x, lane_x) / total_x + np.outer(tile_y, lane_y) / total_y)
    twist = np.stack([np.cos(angle), -np.sin(angle), np.cos(angle)[:, back], -np.sin(angle)[:, back]])
    turn = 2.0 * math.pi * (np.outer(lane_x, lane_x) / width + np.outer(lane_y, lane_y) / depth)
    real, imag = np.cos(turn), np.sin(turn)
    inner_forward = np.block([[real, -imag], [imag, real]])
    real, imag = real[:, back], imag[:, back]
    inner_back = np.block([[real, imag], [-imag, real]])
    k = tile_x[:, None] + across * lane_x[None, :]
    q = tile_y[:, None] + spanwise * lane_y[None, :]
    kx = 2.0 * math.pi / total_x * np.where(k < total_x // 2, k, k - total_x)
    ky = 2.0 * math.pi / total_y * np.where(q < total_y // 2, q, q - total_y)
    hor = kx * kx + ky * ky
    kept = (k != total_x // 2) & (q != total_y // 2)
    decay = np.exp(-DIFFUSE * hor) * kept / (total_x * total_y)
    waves = np.stack([kx, ky, hor, decay])
    return (
        vertical,
        stacked(outer),
        stacked(outer_back),
        split_pair(inner_forward),
        split_pair(inner_back),
        twist.astype(np.float32),
        waves.astype(np.float32),
        rise.astype(np.float32),
    )


def halves(value):
    head = value.astype(jnp.bfloat16)
    return head, (value - head.astype(jnp.float32)).astype(jnp.bfloat16)


def dot(left, right, dims=((1,), (0,))):
    return lax.dot_general(
        left, right, dimension_numbers=(dims, ((), ())), preferred_element_type=jnp.float32
    )


def product(left, right, dims=((1,), (0,))):
    return dot(left[0], right[0], dims) + (dot(left[0], right[1], dims) + dot(left[1], right[0], dims))


def step_body(
    across, spanwise, pre, farm, cell, slot, live, vertical, outer, outer_back, inner_f, inner_b,
    twist, waves, rise, farm_new, pre_new,
    pre_v, farm_v, turb_v, vert_v, outer_v, outerb_v, innf_v, innb_v, twist_v, waves_v, rise_v,
    send, recv, send_two, recv_two, relayed, fringe, own, stage_one, stage_two, stage_three, rows_out,
    rows_in, eddy, force, where_row, where_lev, where_turb, load_sem, a2a_send, a2a_recv, relay_send,
    relay_recv, halo_send, halo_recv, known, out_sem,
):
    count = across * spanwise
    comps, width, depth, levels = farm.shape
    area = width * depth
    lanes = fringe.shape[-1]
    base = lanes - 128
    tail = levels - base
    groups = send.shape[0] // comps
    filled = NF // width
    shift = across - filled
    row, column = lax.axis_index("gx"), lax.axis_index("gy")
    position = row * spanwise + column
    barrier = pltpu.get_barrier_semaphore()

    chunks = []
    start = 0
    for share in SHARES:
        stop = min(groups, start + max(1, round(share * groups)))
        if start < stop:
            chunks.append((start, stop))
        start = stop
    chunks[-1] = (chunks[-1][0], groups)

    loads = []
    for comp in range(comps):
        loads.append(pltpu.make_async_copy(pre.at[comp], pre_v.at[comp], load_sem.at[comp]))
    cut = chunks[0][1] * count
    modes = groups * count
    loads.append(pltpu.make_async_copy(
        vertical.at[:, :, pl.ds(0, cut)], vert_v.at[:, :, pl.ds(0, cut)], load_sem.at[comps]
    ))
    early = len(loads)
    others = []
    if cut < modes:
        others.append(pltpu.make_async_copy(
            vertical.at[:, :, pl.ds(cut, modes - cut)], vert_v.at[:, :, pl.ds(cut, modes - cut)],
            load_sem.at[comps + 1],
        ))
    for copy in loads + others:
        copy.start()

    bands = 4 if spanwise % 4 == 0 else 1
    deep = spanwise // bands
    band = column // deep
    crowd = deep * across
    seat = lax.rem(column, deep)

    def each_in(delta, action):
        def all_of():
            cols = [(band + delta) * deep + lax.rem(seat + step, deep) for step in range(deep)]

            @pl.loop(1, across + (delta != 0), unroll=UNROLL)
            def _(step):
                peer_row = lax.rem(row + step, across)
                for col in cols:
                    action(peer_row, col)

            if delta == 0:
                for col in cols[1:]:
                    action(row, col)

        if delta == 0:
            all_of()
        elif delta > 0:
            pl.when(band < bands - delta)(all_of)
        else:
            pl.when(band >= -delta)(all_of)

    def greet(peer_row, peer_col):
        pl.semaphore_signal(barrier, inc=1, device_id=(peer_row, peer_col), device_id_type=MESH)

    def tell(semaphore, delta):
        pl.semaphore_signal(
            semaphore, inc=1, device_id=(row, column + delta * deep), device_id_type=MESH
        )

    near = (0,) if bands == 1 else (1, -1, 0)
    for delta in near[::-1]:
        each_in(delta, greet)

    for index, (source, target) in enumerate((
        (outer, outer_v), (outer_back, outerb_v), (inner_f, innf_v), (inner_b, innb_v),
        (twist, twist_v), (waves, waves_v), (rise.at[position], rise_v),
        (cell, turb_v.at[0]), (slot, turb_v.at[1]), (live, turb_v.at[2]),
    )):
        loads.append(pltpu.make_async_copy(source, target, load_sem.at[comps + 2 + index]))
    tables = len(loads)
    for y in range(depth):
        loads.append(pltpu.make_async_copy(farm.at[:, :, y], farm_v.at[:, y], load_sem.at[comps + 12 + y]))
    for copy in loads[early:]:
        copy.start()

    def part_of(index):
        low, high = chunks[index]
        return pl.ds(low * comps, (high - low) * comps)

    def spread(leg, index, source, target, deltas):
        part = part_of(index)

        def post(peer_row, peer_col):
            pltpu.make_async_remote_copy(
                src_ref=source.at[part, peer_row * spanwise + peer_col],
                dst_ref=target.at[part, position],
                send_sem=a2a_send.at[leg, index],
                recv_sem=a2a_recv.at[leg, index],
                device_id=(peer_row, peer_col),
                device_id_type=MESH,
            ).start()

        for delta in deltas:
            each_in(delta, post)

    def keep(leg, index, source, target):
        part = part_of(index)
        pltpu.make_async_copy(
            source.at[part, position], target.at[part, position], a2a_recv.at[leg, index]
        ).start()

    def gathered(leg, index, target):
        part = target.at[part_of(index)]
        pltpu.make_async_copy(part, part, a2a_recv.at[leg, index]).wait()

    def sent(leg, index, source):
        part = source.at[part_of(index), pl.ds(0, count - 1)]
        pltpu.make_async_copy(part, part, a2a_send.at[leg, index]).wait()

    for copy in loads[:early]:
        copy.wait()
    columns = [halves(pre_v[comp]) for comp in range(comps)]

    def transform(index):
        low, high = chunks[index]
        span = slice(low * count, high * count)
        for comp in range(comps):
            kind = comp // 2
            table = (vert_v[kind, 0, span][:, :levels], vert_v[kind, 1, span][:, :levels])
            modes = product(table, columns[comp], ((1,), (1,)))
            for group in range(low, high):
                send[group * comps + comp] = modes[(group - low) * count : (group - low + 1) * count]

    far = () if bands == 1 else (2, -2, 3, -3)
    middle = ((band + 1) // 2) % 2
    for index in range(len(chunks)):
        if index == 1:
            for copy in others:
                copy.wait()
        transform(index)
        if index == 0:
            if bands == 1:
                pl.semaphore_wait(barrier, count - 1)
            else:
                pl.semaphore_wait(barrier, (2 + middle) * crowd - 1)

                @pl.when(middle == 1)
                def _():
                    tell(known.at[0], 1)
                    tell(known.at[0], -1)

            spread(0, index, send, recv, near)
            if bands > 1:
                pl.semaphore_wait(known.at[0], 1)

                @pl.when(band == 1)
                def _():
                    tell(known.at[1], -1)

                @pl.when(band == 2)
                def _():
                    tell(known.at[1], 1)

                spread(0, index, send, recv, far[:2])

                @pl.when(middle == 0)
                def _():
                    pl.semaphore_wait(known.at[1], 1)

                spread(0, index, send, recv, far[2:])
        else:
            spread(0, index, send, recv, far + near)
        keep(0, index, send, recv)

    def transfer(source, target, step_row, step_col, send_sem, recv_sem):
        if isinstance(step_col, int) and step_row % across == 0 and step_col % spanwise == 0:
            return pltpu.make_async_copy(source, target, recv_sem), False
        copy = pltpu.make_async_remote_copy(
            src_ref=source, dst_ref=target, send_sem=send_sem, recv_sem=recv_sem,
            device_id=((row + step_row) % across, (column + step_col) % spanwise),
            device_id_type=MESH,
        )
        return copy, True

    def side_copies(source, at, stage, role, target, offset, side):
        step = 1 - 2 * side
        edge = at + (depth - 1) * (1 - side)
        ghost = 1 + (depth + 1) * side
        use = lambda place: (halo_send.at[role, place], halo_recv.at[stage, place])
        return [
            transfer(rows_out.at[role, side], rows_in.at[stage, side], offset, step, *use(side)),
            transfer(
                source.at[:, edge, pl.ds(width - 1, 1)], target.at[:, ghost, pl.ds(width + 7, 1)],
                offset + 1, step, *use(4 + 2 * side),
            ),
            transfer(
                source.at[:, edge, pl.ds(0, 1)], target.at[:, ghost, pl.ds(width, 1)],
                offset - 1, step, *use(5 + 2 * side),
            ),
        ]

    def line_copies(source, at, stage, role, target, offset):
        rows = pl.ds(at, depth)
        use = lambda place: (halo_send.at[role, place], halo_recv.at[stage, place])
        return [
            transfer(
                source.at[:, rows, pl.ds(width - 2, 2)], target.at[:, pl.ds(2, depth), pl.ds(width + 6, 2)],
                offset + 1, 0, *use(8),
            ),
            transfer(
                source.at[:, rows, pl.ds(0, 2)], target.at[:, pl.ds(2, depth), pl.ds(width, 2)],
                offset - 1, 0, *use(9),
            ),
        ]

    def pack(source, at, role, side):
        near = at + (depth - 2) * (1 - side)
        for comp in range(comps):
            for half in (0, 1):
                for block in range(base // 128):
                    rows_out[role, side, comp, half * (base // 128) + block] = source[
                        comp, near + half, :width, block * 128 : block * 128 + 128
                    ]
            rows_out[role, side, comp, 2 * (base // 128)] = source[comp, near, :width, base:] + pltpu.roll(
                source[comp, near + 1, :width, base:], tail, 1
            )

    def send_side(source, at, stage, role, target, offset, side):
        pack(source, at, role, side)
        copies = side_copies(source, at, stage, role, target, offset, side)
        for copy, _ in copies:
            copy.start()
        return copies

    def send_lines(source, at, stage, role, target, offset):
        copies = line_copies(source, at, stage, role, target, offset)
        for copy, _ in copies:
            copy.start()
        return copies

    def send_tile(source, role, offset):
        copies = send_lines(source, 0, 0, role, stage_one, offset)
        for side in (0, 1):
            copies += send_side(source, 0, 0, role, stage_one, offset, side)
        return copies

    def tile_sent(source, role, offset):
        copies = line_copies(source, 0, 0, role, stage_one, offset)
        for side in (0, 1):
            copies += side_copies(source, 0, 0, role, stage_one, offset, side)
        for copy, remote in copies:
            if remote:
                copy.wait_send()

    for copy in loads[tables:]:
        copy.wait()
    blank = jnp.zeros((width, lanes - base), jnp.float32)

    @pl.when(row >= filled)
    def _():
        for comp in range(comps):
            for y in range(depth):
                own[comp, y, :, base:] = blank
                own[comp, y, :, :levels] = farm_v[comp, y]
                stage_one[comp, 2 + y, :width] = own[comp, y]
        send_tile(own, 0, 0)

    for copy in loads[early:tables]:
        copy.wait()
    index = turb_v[0].astype(jnp.float32)
    line = jnp.floor((index + 0.5) * (1.0 / levels))
    level = index - levels * line
    at_x = jnp.floor((line + 0.5) * (1.0 / depth))
    line = (line - depth * at_x) * width + at_x
    slots = index.shape[-1]

    def hot(size, value):
        steps = lax.broadcasted_iota(jnp.int32, (size, slots), 0).astype(jnp.float32)
        return jnp.where(steps == value, 1.0, 0.0)

    where_row[...] = hot(area, line)
    where_lev[...] = hot(lanes, level).astype(jnp.bfloat16)
    turbine = jnp.where(turb_v[2] == 1, turb_v[1], TURB).astype(jnp.float32)
    where_turb[...] = hot(TURB, turbine)

    kx, ky, hor, decay = waves_v[0], waves_v[1], waves_v[2], waves_v[3]

    def project(chunk):
        low, high = chunk
        table = outer_v[...]
        cos, sin = twist_v[0], twist_v[1]
        blocks = []
        for place in range(low * comps, high * comps):
            head, rest = halves(recv[place])
            spun = dot(table, jnp.concatenate([head, head, rest], axis=0))
            real, imag = spun[:count], spun[count:]
            blocks.append(jnp.concatenate([real * cos - imag * sin, real * sin + imag * cos], axis=1))
        spec = shared(halves(jnp.concatenate(blocks, axis=0)), (innf_v[0], innf_v[1]))
        blocks = []
        for group in range(low, high):
            lift = rise_v[pl.ds(group, 1), :area]
            real, imag = [], []
            for comp in range(comps):
                start = ((group - low) * comps + comp) * count
                real.append(spec[start : start + count, :area])
                imag.append(spec[start : start + count, area:])
            bound = hor + lift * lift
            inverse = jnp.where(bound > 0.0, -1.0 / jnp.where(bound > 0.0, bound, 1.0), 0.0)
            press_re = (lift * real[2] - kx * imag[0] - ky * imag[1]) * inverse
            press_im = (kx * real[0] + ky * real[1] + lift * imag[2]) * inverse
            new_re = [real[0] + kx * press_im, real[1] + ky * press_im, real[2] + lift * press_re]
            new_im = [imag[0] - kx * press_re, imag[1] - ky * press_re, imag[2] + lift * press_im]
            for comp in range(comps):
                blocks.append(jnp.concatenate([new_re[comp] * decay, new_im[comp] * decay], axis=1))
        lines = shared(halves(jnp.concatenate(blocks, axis=0)), (innb_v[0], innb_v[1]))
        table = outerb_v[...]
        cos, sin = twist_v[2], twist_v[3]
        for place in range((high - low) * comps):
            real = lines[place * count : (place + 1) * count, :area]
            imag = lines[place * count : (place + 1) * count, area:]
            spun = jnp.concatenate([real * cos + imag * sin, imag * cos - real * sin], axis=0)
            head, rest = halves(spun)
            send_two[low * comps + place] = dot(table, jnp.concatenate([head, head, rest], axis=0))

    for index, chunk in enumerate(chunks):
        gathered(0, index, recv)
        project(chunk)
        keep(1, index, send_two, recv_two)
        spread(1, index, send_two, recv_two, far + near)

    def relay(index):
        return transfer(
            recv_two.at[part_of(index)], relayed.at[part_of(index)], -shift, 0,
            relay_send.at[index], relay_recv.at[index],
        )

    def levels_of(source, index, comp):
        low, high = chunks[index]
        modes = jnp.concatenate([source[g * comps + comp] for g in range(low, high)], axis=0)
        kind = comp // 2
        span = slice(low * count, high * count)
        value = shared(halves(modes.T), (vert_v[kind, 0, span], vert_v[kind, 1, span]))
        return value.reshape(depth, width, lanes)

    for index in range(len(chunks)):
        gathered(1, index, recv_two)

        @pl.when(row >= shift)
        def _():
            relay(index)[0].start()

        for comp in range(comps):
            value = levels_of(recv_two, index, comp)
            fringe[comp] = value if index == 0 else fringe[comp] + value

    @pl.when(row >= shift)
    def _():
        send_tile(fringe, 1, -shift)


    @pl.when(row < filled)
    def _():
        for index in range(len(chunks)):
            part = relayed.at[part_of(index)]
            pltpu.make_async_copy(part, part, relay_recv.at[index]).wait()
            for comp in range(comps):
                value = levels_of(relayed, index, comp)
                if index > 0:
                    value = value + stage_one[comp, 2 : depth + 2, :width]
                stage_one[comp, 2 : depth + 2, :width] = value

    inside = lax.broadcasted_iota(jnp.int32, (width, lanes), 1) < levels
    kept = lax.broadcasted_iota(jnp.int32, (width, lanes - base), 1) < tail

    def arrived(part, stage, place):
        pltpu.make_async_copy(part, part, halo_recv.at[stage, place]).wait()

    def lines_in(field, stage):
        arrived(field.at[:, pl.ds(2, depth), pl.ds(width + 6, 2)], stage, 8)
        arrived(field.at[:, pl.ds(2, depth), pl.ds(width, 2)], stage, 9)

    def side_in(field, stage, side):
        land = (depth + 2) * side
        ghost = 1 + (depth + 1) * side
        arrived(rows_in.at[stage, side], stage, side)
        arrived(field.at[:, ghost, pl.ds(width + 7, 1)], stage, 4 + 2 * side)
        arrived(field.at[:, ghost, pl.ds(width, 1)], stage, 5 + 2 * side)
        for comp in range(comps):
            for half in (0, 1):
                for block in range(base // 128):
                    field[comp, land + half, :width, block * 128 : block * 128 + 128] = rows_in[
                        stage, side, comp, half * (base // 128) + block
                    ]
            packed = rows_in[stage, side, comp, 2 * (base // 128)]
            field[comp, land, :width, base:] = jnp.where(kept, packed, 0.0)
            packed = pltpu.roll(packed, 128 - tail, 1)
            field[comp, land + 1, :width, base:] = jnp.where(kept, packed, 0.0)

    def drag(field):
        cells = field[0, 2 : depth + 2, :width].reshape(area, lanes)
        head, rest = halves(cells)
        table = where_lev[...]
        picked = (dot(head, table) + dot(rest, table)) * where_row[...]
        values = jnp.sum(picked, axis=0, keepdims=True) + WIND
        turbs = where_turb[...]
        sums = jnp.sum(turbs * values, axis=1, keepdims=True)
        counts = jnp.sum(turbs, axis=1, keepdims=True)
        mean = sums / jnp.maximum(counts, 1.0)
        thrust = (-0.5 * THRUST * STEP) * mean * jnp.abs(mean)
        per_slot = jnp.sum(turbs * thrust, axis=0, keepdims=True)
        head, rest = halves(where_row[...] * per_slot)
        last = ((1,), (1,))
        force[...] = (dot(head, table, last) + dot(rest, table, last)).reshape(depth, width, lanes)

    def ahead(value, axis):
        return pltpu.roll(value, value.shape[axis] - 1, axis)

    def behind(value, axis):
        return pltpu.roll(value, 1, axis)

    def eddy_slab(field, j, size):
        along, across_y, up = [], [], []
        for comp in range(comps):
            value = field[comp, j]
            along.append((ahead(value, 0) - behind(value, 0))[:size])
            across_y.append(field[comp, j + 1, :size] - field[comp, j - 1, :size])
            up.append(ahead(value[:size], 1) - behind(value[:size], 1))
        shear = 0.0
        for pair in (along[1] + across_y[0], along[2] + up[0], across_y[2] + up[1]):
            shear = shear + pair * pair
        square = along[0] * along[0] + across_y[1] * across_y[1] + up[2] * up[2] + 0.5 * shear
        eddy[j - 1, :size] = (0.5 * STEP * SMAG * math.sqrt(0.5)) * jnp.sqrt(square)

    def factors(speed, viscous):
        return speed + viscous, speed - viscous

    def flux(pair, low_f, high_f):
        return pair[0] * low_f + pair[1] * high_f

    quarter = 0.25 * STEP

    def span_flux(field, j):
        speed = quarter * (field[1, j, :width] + field[1, j + 1, :width])
        pair = factors(speed, eddy[j - 1, :width] + eddy[j, :width])
        return tuple(
            flux(pair, field[comp, j, :width], field[comp, j + 1, :width]) for comp in range(comps)
        )

    def rates(field, start, size, store):
        def slab(step, below):
            j = start + step
            above = span_flux(field, j)
            viscous = eddy[j - 1]
            whole = field[0, j]
            next_u = ahead(whole, 0)
            along = factors(
                quarter * (whole + next_u) + (2.0 * quarter * WIND), viscous + ahead(viscous, 0)
            )
            inner_h = viscous[:width]
            lift = field[2, j, :width]
            next_w = ahead(lift, 1)
            rising = factors(quarter * (lift + next_w), inner_h + ahead(inner_h, 1))
            for comp in range(comps):
                value = field[comp, j]
                face = flux(along, value, next_u if comp == 0 else ahead(value, 0))
                total = (face - behind(face, 0))[:width] + (above[comp] - below[comp])
                mid = value[:width]
                face = flux(rising, mid, next_w if comp == 2 else ahead(mid, 1))
                total = total + (face - behind(face, 1))
                change = force[j - 2] - total if comp == 0 else -total
                store(comp, j, mid + change)
            return above

        lax.fori_loop(0, size, slab, span_flux(field, start - 1), unroll=2)

    first = 1 - column % 2

    def section(stage, field, store, leave, settled=lambda: None):
        drag(field)
        lines_in(field, stage)

        @pl.loop(3, depth + 1, unroll=2)
        def _(j):
            eddy_slab(field, j, width + 8)

        rates(field, 4, depth - 4, store)
        settled()

        @pl.loop(0, 2)
        def _(turn):
            side = (turn + first) % 2
            side_in(field, stage, side)

            eddy_slab(field, 1 + (depth + 1) * side, width)
            eddy_slab(field, 2 + (depth - 1) * side, width + 8)

            rates(field, 2 + (depth - 2) * side, 2, store)
            leave(side)

    def to_next(target, share):
        def store(comp, j, value):
            if share < 1.0:
                value = (1.0 - share) * stage_one[comp, j, :width] + share * value
            target[comp, j, :width] = jnp.where(inside, value, 0.0)
        return store

    def to_output(comp, j, value):
        value = stage_one[comp, j, :width] * (1.0 / 3.0) + (2.0 / 3.0) * value
        farm_v[comp, j - 2] = value[:, :levels]

    section(0, stage_one, to_next(stage_two, 1.0), lambda side: send_side(stage_two, 2, 1, 2, stage_two, 0, 1 - side))
    send_lines(stage_two, 2, 1, 2, stage_two, 0)
    outs = []
    for comp in range(comps):
        farm_v[comp] = fringe[comp][:, :, :levels]
    for y in range(depth):
        outs.append(pltpu.make_async_copy(farm_v.at[:, y], pre_new.at[:, :, y], out_sem.at[0, y]))
        outs[-1].start()
    section(1, stage_two, to_next(stage_three, 0.25), lambda side: send_side(stage_three, 2, 2, 3, stage_three, 0, 1 - side))
    send_lines(stage_three, 2, 2, 3, stage_three, 0)

    def result(y):
        return pltpu.make_async_copy(farm_v.at[:, y], farm_new.at[:, :, y], out_sem.at[1, y])

    def inner_rows():
        for y in range(2, depth - 2):
            result(y).start()

    def outer_rows(side):
        for half in (0, 1):
            result((depth - 2) * side + half).start()

    for copy in outs:
        copy.wait()
    section(2, stage_three, to_output, outer_rows, inner_rows)
    for index in range(len(chunks)):
        sent(0, index, send)
        sent(1, index, send_two)
    for stage, field in ((1, stage_two), (2, stage_three)):
        copies = line_copies(field, 2, stage, stage + 1, field, 0)
        for side in (0, 1):
            copies += side_copies(field, 2, stage, stage + 1, field, 0, side)
        for copy, remote in copies:
            if remote:
                copy.wait_send()

    @pl.when(row >= shift)
    def _():
        tile_sent(fringe, 1, -shift)
        for index in range(len(chunks)):
            copy, remote = relay(index)
            if remote:
                copy.wait_send()

    @pl.when(row >= filled)
    def _():
        tile_sent(own, 0, 0)

    for y in range(depth):
        result(y).wait()


def write_out(farm, pre, farm_new, pre_new, hold, in_sem, out_sem):
    pieces = []
    for place, (source, target) in enumerate(((pre, pre_new), (farm, farm_new))):
        for comp in range(source.shape[0]):
            seat = hold.at[place, comp]
            pieces.append((
                pltpu.make_async_copy(source.at[comp], seat, in_sem.at[place, comp]),
                pltpu.make_async_copy(seat, target.at[comp], out_sem.at[place, comp]),
            ))
    for copy, _ in pieces:
        copy.start()
    for copy, onward in pieces:
        copy.wait()
        onward.start()
    for _, onward in pieces:
        onward.wait()


def shards(across, spanwise, farm, pre, turb_cell, turb_slot, disk_mask):
    comps, width, depth, levels = pre.shape
    count = across * spanwise
    area = width * depth
    slots = turb_cell.shape[-1]
    lanes = -(-(levels + 2) // 128) * 128
    groups = -(-levels // count)
    tables = [jnp.asarray(t) for t in spectral_tables(across, spanwise, width, depth, levels, lanes)]
    anywhere = pl.BlockSpec(memory_space=pl.ANY)
    f32 = jnp.float32

    def vmem(*shape, dtype=f32):
        return pltpu.VMEM(shape, dtype)

    def sems(*shape):
        return pltpu.SemaphoreType.DMA(shape)

    modes = vmem(groups * comps, count, area)
    cells = vmem(comps, depth, width, lanes)
    padded = vmem(comps, depth + 4, width + 8, lanes)
    results = [jax.ShapeDtypeStruct(farm.shape, f32), jax.ShapeDtypeStruct(pre.shape, f32)]
    farm_new, pre_new = pl.pallas_call(
        functools.partial(step_body, across, spanwise),
        out_shape=results,
        in_specs=[anywhere] * (5 + len(tables)),
        out_specs=[anywhere] * 2,
        scratch_shapes=[
            vmem(comps, area, levels),
            vmem(comps, depth, width, levels),
            vmem(3, 1, slots, dtype=jnp.int32),
            *[vmem(*t.shape, dtype=t.dtype) for t in tables[:-1]],
            vmem(*tables[-1].shape[1:]),
            modes, modes, modes, modes, modes,
            cells, cells, padded, padded, padded,
            vmem(4, 2, comps, 2 * (lanes // 128) - 1, width, 128),
            vmem(3, 2, comps, 2 * (lanes // 128) - 1, width, 128),
            vmem(depth + 2, width + 8, lanes),
            vmem(depth, width, lanes),
            vmem(area, slots),
            vmem(lanes, slots, dtype=jnp.bfloat16),
            vmem(TURB, slots),
            sems(comps + 2 + 10 + depth),
            sems(2, len(SHARES)),
            sems(2, len(SHARES)),
            sems(len(SHARES)),
            sems(len(SHARES)),
            sems(4, 10),
            sems(3, 10),
            pltpu.SemaphoreType.REGULAR((2,)),
            sems(2, depth),
        ],
        compiler_params=pltpu.CompilerParams(collective_id=0, has_side_effects=True),
        name="step",
    )(
        pre.reshape(comps, area, levels), farm,
        turb_cell.reshape(1, slots), turb_slot.reshape(1, slots), disk_mask.reshape(1, slots),
        *tables,
    )
    return pl.pallas_call(
        write_out,
        out_shape=results,
        in_specs=[anywhere] * 2,
        out_specs=[anywhere] * 2,
        scratch_shapes=[vmem(2, comps, width, depth, levels), sems(2, comps), sems(2, comps)],
        name="write_out",
    )(farm_new, pre_new)


def solution(mesh):
    across, spanwise = mesh.shape["gx"], mesh.shape["gy"]
    return jax.shard_map(
        functools.partial(shards, across, spanwise),
        mesh=mesh,
        in_specs=(
            P(None, "gx", "gy", None),
            P(None, "gx", "gy", None),
            P("gx", "gy", None),
            P("gx", "gy", None),
            P("gx", "gy", None),
        ),
        out_specs=(P(None, "gx", "gy", None), P(None, "gx", "gy", None)),
        check_vma=False,
    )
```

```python
import functools
import math

import jax
import jax.numpy as jnp
import numpy as np
from jax import lax
from jax.experimental import pallas as pl
from jax.experimental.pallas import tpu as pltpu
from jax.sharding import PartitionSpec as P

NF = 48
TURB = 16
WIND = 3.0
STEP = 0.1
SMAG = 0.0289
THRUST = 1.33
DIFFUSE = 0.05
MESH = pl.DeviceIdType.MESH
UNROLL = 1
SHARES = (1 / 3, 1 / 6, 1 / 3, 1 / 6)


def split_pair(table):
    table = np.asarray(table, np.float32)
    head = table.astype(jnp.bfloat16)
    tail = (table - head.astype(np.float32)).astype(jnp.bfloat16)
    return np.stack([head, tail])


def shared(left, right):
    rows = left[0].shape[0]
    both = dot(jnp.concatenate(left, axis=0), right[0])
    return both[:rows] + (both[rows:] + dot(left[0], right[1]))


def stacked(table):
    head, tail = split_pair(table)
    return np.concatenate([head, tail, head], axis=1)


def spectral_tables(across, spanwise, width, depth, levels, lanes):
    count = across * spanwise
    total_x, total_y = across * width, spanwise * depth
    groups = -(-levels // count)
    order = np.arange(groups * count)[:, None]
    height = np.arange(levels)[None, :]
    inside = order < levels
    scale = np.where(order == 0, math.sqrt(1.0 / levels), math.sqrt(2.0 / levels)) * inside
    centre = scale * np.cos(math.pi / (2 * levels) * (order * (2 * height + 1) % (4 * levels)))
    face = (
        math.sqrt(2.0 / levels)
        * np.sin(math.pi / levels * (order * (height + 1) % (2 * levels)))
        * ((height < levels - 1) & (order > 0) & inside)
    )
    pad = ((0, 0), (0, 0), (0, lanes - levels))
    vertical = np.stack([np.pad(split_pair(centre), pad), np.pad(split_pair(face), pad)])
    rise = 2.0 * np.sin(np.minimum(order, levels)[:, 0] * (math.pi / (2 * levels)))
    rise = np.pad(rise.reshape(groups, count).T, ((0, 0), (0, -groups % 8)))
    rise = np.broadcast_to(rise[:, :, None], rise.shape + (128,))
    tile = np.arange(count)
    tile_x, tile_y = tile // spanwise, tile % spanwise
    turn = 2.0 * math.pi * (np.outer(tile_x, tile_x) / across + np.outer(tile_y, tile_y) / spanwise)
    outer = np.concatenate([np.cos(turn), -np.sin(turn)], axis=0)
    outer_back = np.concatenate([np.cos(turn), -np.sin(turn)], axis=1)
    lane = np.arange(width * depth)
    lane_x, lane_y = lane // depth, lane % depth
    back = (lane % width) * depth + lane // width
    angle = 2.0 * math.pi * (np.outer(tile_x, lane_x) / total_x + np.outer(tile_y, lane_y) / total_y)
    twist = np.stack([np.cos(angle), -np.sin(angle), np.cos(angle)[:, back], -np.sin(angle)[:, back]])
    turn = 2.0 * math.pi * (np.outer(lane_x, lane_x) / width + np.outer(lane_y, lane_y) / depth)
    real, imag = np.cos(turn), np.sin(turn)
    inner_forward = np.block([[real, -imag], [imag, real]])
    real, imag = real[:, back], imag[:, back]
    inner_back = np.block([[real, imag], [-imag, real]])
    k = tile_x[:, None] + across * lane_x[None, :]
    q = tile_y[:, None] + spanwise * lane_y[None, :]
    kx = 2.0 * math.pi / total_x * np.where(k < total_x // 2, k, k - total_x)
    ky = 2.0 * math.pi / total_y * np.where(q < total_y // 2, q, q - total_y)
    hor = kx * kx + ky * ky
    kept = (k != total_x // 2) & (q != total_y // 2)
    decay = np.exp(-DIFFUSE * hor) * kept / (total_x * total_y)
    waves = np.stack([kx, ky, hor, decay])
    return (
        vertical,
        stacked(outer),
        stacked(outer_back),
        split_pair(inner_forward),
        split_pair(inner_back),
        twist.astype(np.float32),
        waves.astype(np.float32),
        rise.astype(np.float32),
    )


def halves(value):
    head = value.astype(jnp.bfloat16)
    return head, (value - head.astype(jnp.float32)).astype(jnp.bfloat16)


def dot(left, right, dims=((1,), (0,))):
    return lax.dot_general(
        left, right, dimension_numbers=(dims, ((), ())), preferred_element_type=jnp.float32
    )


def product(left, right, dims=((1,), (0,))):
    return dot(left[0], right[0], dims) + (dot(left[0], right[1], dims) + dot(left[1], right[0], dims))


def step_body(
    across, spanwise, pre, farm, cell, slot, live, vertical, outer, outer_back, inner_f, inner_b,
    twist, waves, rise, farm_new, pre_new,
    pre_v, farm_v, turb_v, vert_v, outer_v, outerb_v, innf_v, innb_v, twist_v, waves_v, rise_v,
    send, recv, send_two, recv_two, relayed, fringe, own, stage_one, stage_two, stage_three, rows_out,
    rows_in, eddy, force, where_row, where_lev, where_turb, load_sem, a2a_send, a2a_recv, relay_send,
    relay_recv, halo_send, halo_recv, known, out_sem,
):
    count = across * spanwise
    comps, width, depth, levels = farm.shape
    area = width * depth
    lanes = fringe.shape[-1]
    base = lanes - 128
    tail = levels - base
    groups = send.shape[0] // comps
    filled = NF // width
    shift = across - filled
    row, column = lax.axis_index("gx"), lax.axis_index("gy")
    position = row * spanwise + column
    barrier = pltpu.get_barrier_semaphore()

    chunks = []
    start = 0
    for share in SHARES:
        stop = min(groups, start + max(1, round(share * groups)))
        if start < stop:
            chunks.append((start, stop))
        start = stop
    chunks[-1] = (chunks[-1][0], groups)

    loads = []
    for comp in range(comps):
        loads.append(pltpu.make_async_copy(pre.at[comp], pre_v.at[comp], load_sem.at[comp]))
    cut = chunks[0][1] * count
    modes = groups * count
    loads.append(pltpu.make_async_copy(
        vertical.at[:, :, pl.ds(0, cut)], vert_v.at[:, :, pl.ds(0, cut)], load_sem.at[comps]
    ))
    early = len(loads)
    others = []
    if cut < modes:
        others.append(pltpu.make_async_copy(
            vertical.at[:, :, pl.ds(cut, modes - cut)], vert_v.at[:, :, pl.ds(cut, modes - cut)],
            load_sem.at[comps + 1],
        ))
    for copy in loads + others:
        copy.start()

    bands = 4 if spanwise % 4 == 0 else 1
    deep = spanwise // bands
    band = column // deep
    crowd = deep * across
    seat = lax.rem(column, deep)

    def each_in(delta, action):
        def all_of():
            cols = [(band + delta) * deep + lax.rem(seat + step, deep) for step in range(deep)]

            @pl.loop(1, across + (delta != 0), unroll=UNROLL)
            def _(step):
                peer_row = lax.rem(row + step, across)
                for col in cols:
                    action(peer_row, col)

            if delta == 0:
                for col in cols[1:]:
                    action(row, col)

        if delta == 0:
            all_of()
        elif delta > 0:
            pl.when(band < bands - delta)(all_of)
        else:
            pl.when(band >= -delta)(all_of)

    def greet(peer_row, peer_col):
        pl.semaphore_signal(barrier, inc=1, device_id=(peer_row, peer_col), device_id_type=MESH)

    def tell(semaphore, delta):
        pl.semaphore_signal(
            semaphore, inc=1, device_id=(row, column + delta * deep), device_id_type=MESH
        )

    near = (0,) if bands == 1 else (1, -1, 0)
    for delta in near[::-1]:
        each_in(delta, greet)

    for index, (source, target) in enumerate((
        (outer, outer_v), (outer_back, outerb_v), (inner_f, innf_v), (inner_b, innb_v),
        (twist, twist_v), (waves, waves_v), (rise.at[position], rise_v),
        (cell, turb_v.at[0]), (slot, turb_v.at[1]), (live, turb_v.at[2]),
    )):
        loads.append(pltpu.make_async_copy(source, target, load_sem.at[comps + 2 + index]))
    tables = len(loads)
    for y in range(depth):
        loads.append(pltpu.make_async_copy(farm.at[:, :, y], farm_v.at[:, y], load_sem.at[comps + 12 + y]))
    for copy in loads[early:]:
        copy.start()

    def part_of(index):
        low, high = chunks[index]
        return pl.ds(low * comps, (high - low) * comps)

    def spread(leg, index, source, target, deltas):
        part = part_of(index)

        def post(peer_row, peer_col):
            pltpu.make_async_remote_copy(
                src_ref=source.at[part, peer_row * spanwise + peer_col],
                dst_ref=target.at[part, position],
                send_sem=a2a_send.at[leg, index],
                recv_sem=a2a_recv.at[leg, index],
                device_id=(peer_row, peer_col),
                device_id_type=MESH,
            ).start()

        for delta in deltas:
            each_in(delta, post)

    def keep(leg, index, source, target):
        part = part_of(index)
        pltpu.make_async_copy(
            source.at[part, position], target.at[part, position], a2a_recv.at[leg, index]
        ).start()

    def gathered(leg, index, target):
        part = target.at[part_of(index)]
        pltpu.make_async_copy(part, part, a2a_recv.at[leg, index]).wait()

    def sent(leg, index, source):
        part = source.at[part_of(index), pl.ds(0, count - 1)]
        pltpu.make_async_copy(part, part, a2a_send.at[leg, index]).wait()

    for copy in loads[:early]:
        copy.wait()
    columns = [halves(pre_v[comp]) for comp in range(comps)]

    def transform(index):
        low, high = chunks[index]
        span = slice(low * count, high * count)
        for comp in range(comps):
            kind = comp // 2
            table = (vert_v[kind, 0, span][:, :levels], vert_v[kind, 1, span][:, :levels])
            modes = product(table, columns[comp], ((1,), (1,)))
            for group in range(low, high):
                send[group * comps + comp] = modes[(group - low) * count : (group - low + 1) * count]

    far = () if bands == 1 else (2, -2, 3, -3)
    middle = ((band + 1) // 2) % 2
    for index in range(len(chunks)):
        if index == 1:
            for copy in others:
                copy.wait()
        transform(index)
        if index == 0:
            if bands == 1:
                pl.semaphore_wait(barrier, count - 1)
            else:
                pl.semaphore_wait(barrier, (2 + middle) * crowd - 1)

                @pl.when(middle == 1)
                def _():
                    tell(known.at[0], 1)
                    tell(known.at[0], -1)

            spread(0, index, send, recv, near)
            if bands > 1:
                pl.semaphore_wait(known.at[0], 1)

                @pl.when(band == 1)
                def _():
                    tell(known.at[1], -1)

                @pl.when(band == 2)
                def _():
                    tell(known.at[1], 1)

                spread(0, index, send, recv, far[:2])

                @pl.when(middle == 0)
                def _():
                    pl.semaphore_wait(known.at[1], 1)

                spread(0, index, send, recv, far[2:])
        else:
            spread(0, index, send, recv, far + near)
        keep(0, index, send, recv)

    def transfer(source, target, step_row, step_col, send_sem, recv_sem):
        if isinstance(step_col, int) and step_row % across == 0 and step_col % spanwise == 0:
            return pltpu.make_async_copy(source, target, recv_sem), False
        copy = pltpu.make_async_remote_copy(
            src_ref=source, dst_ref=target, send_sem=send_sem, recv_sem=recv_sem,
            device_id=((row + step_row) % across, (column + step_col) % spanwise),
            device_id_type=MESH,
        )
        return copy, True

    def side_copies(source, at, stage, role, target, offset, side):
        step = 1 - 2 * side
        edge = at + (depth - 1) * (1 - side)
        ghost = 1 + (depth + 1) * side
        use = lambda place: (halo_send.at[role, place], halo_recv.at[stage, place])
        return [
            transfer(rows_out.at[role, side], rows_in.at[stage, side], offset, step, *use(side)),
            transfer(
                source.at[:, edge, pl.ds(width - 1, 1)], target.at[:, ghost, pl.ds(width + 7, 1)],
                offset + 1, step, *use(4 + 2 * side),
            ),
            transfer(
                source.at[:, edge, pl.ds(0, 1)], target.at[:, ghost, pl.ds(width, 1)],
                offset - 1, step, *use(5 + 2 * side),
            ),
        ]

    def line_copies(source, at, stage, role, target, offset):
        rows = pl.ds(at, depth)
        use = lambda place: (halo_send.at[role, place], halo_recv.at[stage, place])
        return [
            transfer(
                source.at[:, rows, pl.ds(width - 2, 2)], target.at[:, pl.ds(2, depth), pl.ds(width + 6, 2)],
                offset + 1, 0, *use(8),
            ),
            transfer(
                source.at[:, rows, pl.ds(0, 2)], target.at[:, pl.ds(2, depth), pl.ds(width, 2)],
                offset - 1, 0, *use(9),
            ),
        ]

    def pack(source, at, role, side):
        near = at + (depth - 2) * (1 - side)
        for comp in range(comps):
            for half in (0, 1):
                for block in range(base // 128):
                    rows_out[role, side, comp, half * (base // 128) + block] = source[
                        comp, near + half, :width, block * 128 : block * 128 + 128
                    ]
            rows_out[role, side, comp, 2 * (base // 128)] = source[comp, near, :width, base:] + pltpu.roll(
                source[comp, near + 1, :width, base:], tail, 1
            )

    def send_side(source, at, stage, role, target, offset, side):
        pack(source, at, role, side)
        copies = side_copies(source, at, stage, role, target, offset, side)
        for copy, _ in copies:
            copy.start()
        return copies

    def send_lines(source, at, stage, role, target, offset):
        copies = line_copies(source, at, stage, role, target, offset)
        for copy, _ in copies:
            copy.start()
        return copies

    def send_tile(source, role, offset):
        copies = send_lines(source, 0, 0, role, stage_one, offset)
        for side in (0, 1):
            copies += send_side(source, 0, 0, role, stage_one, offset, side)
        return copies

    def tile_sent(source, role, offset):
        copies = line_copies(source, 0, 0, role, stage_one, offset)
        for side in (0, 1):
            copies += side_copies(source, 0, 0, role, stage_one, offset, side)
        for copy, remote in copies:
            if remote:
                copy.wait_send()

    for copy in loads[tables:]:
        copy.wait()
    blank = jnp.zeros((width, lanes - base), jnp.float32)

    @pl.when(row >= filled)
    def _():
        for comp in range(comps):
            for y in range(depth):
                own[comp, y, :, base:] = blank
                own[comp, y, :, :levels] = farm_v[comp, y]
                stage_one[comp, 2 + y, :width] = own[comp, y]
        send_tile(own, 0, 0)

    for copy in loads[early:tables]:
        copy.wait()
    index = turb_v[0].astype(jnp.float32)
    line = jnp.floor((index + 0.5) * (1.0 / levels))
    level = index - levels * line
    at_x = jnp.floor((line + 0.5) * (1.0 / depth))
    line = (line - depth * at_x) * width + at_x
    slots = index.shape[-1]

    def hot(size, value):
        steps = lax.broadcasted_iota(jnp.int32, (size, slots), 0).astype(jnp.float32)
        return jnp.where(steps == value, 1.0, 0.0)

    where_row[...] = hot(area, line)
    where_lev[...] = hot(lanes, level).astype(jnp.bfloat16)
    turbine = jnp.where(turb_v[2] == 1, turb_v[1], TURB).astype(jnp.float32)
    where_turb[...] = hot(TURB, turbine)

    kx, ky, hor, decay = waves_v[0], waves_v[1], waves_v[2], waves_v[3]

    def project(chunk):
        low, high = chunk
        table = outer_v[...]
        cos, sin = twist_v[0], twist_v[1]
        blocks = []
        for place in range(low * comps, high * comps):
            head, rest = halves(recv[place])
            spun = dot(table, jnp.concatenate([head, head, rest], axis=0))
            real, imag = spun[:count], spun[count:]
            blocks.append(jnp.concatenate([real * cos - imag * sin, real * sin + imag * cos], axis=1))
        spec = shared(halves(jnp.concatenate(blocks, axis=0)), (innf_v[0], innf_v[1]))
        blocks = []
        for group in range(low, high):
            lift = rise_v[pl.ds(group, 1), :area]
            real, imag = [], []
            for comp in range(comps):
                start = ((group - low) * comps + comp) * count
                real.append(spec[start : start + count, :area])
                imag.append(spec[start : start + count, area:])
            bound = hor + lift * lift
            inverse = jnp.where(bound > 0.0, -1.0 / jnp.where(bound > 0.0, bound, 1.0), 0.0)
            press_re = (lift * real[2] - kx * imag[0] - ky * imag[1]) * inverse
            press_im = (kx * real[0] + ky * real[1] + lift * imag[2]) * inverse
            new_re = [real[0] + kx * press_im, real[1] + ky * press_im, real[2] + lift * press_re]
            new_im = [imag[0] - kx * press_re, imag[1] - ky * press_re, imag[2] + lift * press_im]
            for comp in range(comps):
                blocks.append(jnp.concatenate([new_re[comp] * decay, new_im[comp] * decay], axis=1))
        lines = shared(halves(jnp.concatenate(blocks, axis=0)), (innb_v[0], innb_v[1]))
        table = outerb_v[...]
        cos, sin = twist_v[2], twist_v[3]
        for place in range((high - low) * comps):
            real = lines[place * count : (place + 1) * count, :area]
            imag = lines[place * count : (place + 1) * count, area:]
            spun = jnp.concatenate([real * cos + imag * sin, imag * cos - real * sin], axis=0)
            head, rest = halves(spun)
            send_two[low * comps + place] = dot(table, jnp.concatenate([head, head, rest], axis=0))

    for index, chunk in enumerate(chunks):
        gathered(0, index, recv)
        project(chunk)
        keep(1, index, send_two, recv_two)
        spread(1, index, send_two, recv_two, far[2:] + far[:2] + near)

    def relay(index):
        return transfer(
            recv_two.at[part_of(index)], relayed.at[part_of(index)], -shift, 0,
            relay_send.at[index], relay_recv.at[index],
        )

    def levels_of(source, index, comp):
        low, high = chunks[index]
        modes = jnp.concatenate([source[g * comps + comp] for g in range(low, high)], axis=0)
        kind = comp // 2
        span = slice(low * count, high * count)
        value = shared(halves(modes.T), (vert_v[kind, 0, span], vert_v[kind, 1, span]))
        return value.reshape(depth, width, lanes)

    for index in range(len(chunks)):
        gathered(1, index, recv_two)

        @pl.when(row >= shift)
        def _():
            relay(index)[0].start()

        for comp in range(comps):
            value = levels_of(recv_two, index, comp)
            fringe[comp] = value if index == 0 else fringe[comp] + value

    @pl.when(row >= shift)
    def _():
        send_tile(fringe, 1, -shift)


    @pl.when(row < filled)
    def _():
        for index in range(len(chunks)):
            part = relayed.at[part_of(index)]
            pltpu.make_async_copy(part, part, relay_recv.at[index]).wait()
            for comp in range(comps):
                value = levels_of(relayed, index, comp)
                if index > 0:
                    value = value + stage_one[comp, 2 : depth + 2, :width]
                stage_one[comp, 2 : depth + 2, :width] = value

    inside = lax.broadcasted_iota(jnp.int32, (width, lanes), 1) < levels
    kept = lax.broadcasted_iota(jnp.int32, (width, lanes - base), 1) < tail

    def arrived(part, stage, place):
        pltpu.make_async_copy(part, part, halo_recv.at[stage, place]).wait()

    def lines_in(field, stage):
        arrived(field.at[:, pl.ds(2, depth), pl.ds(width + 6, 2)], stage, 8)
        arrived(field.at[:, pl.ds(2, depth), pl.ds(width, 2)], stage, 9)

    def side_in(field, stage, side):
        land = (depth + 2) * side
        ghost = 1 + (depth + 1) * side
        arrived(rows_in.at[stage, side], stage, side)
        arrived(field.at[:, ghost, pl.ds(width + 7, 1)], stage, 4 + 2 * side)
        arrived(field.at[:, ghost, pl.ds(width, 1)], stage, 5 + 2 * side)
        for comp in range(comps):
            for half in (0, 1):
                for block in range(base // 128):
                    field[comp, land + half, :width, block * 128 : block * 128 + 128] = rows_in[
                        stage, side, comp, half * (base // 128) + block
                    ]
            packed = rows_in[stage, side, comp, 2 * (base // 128)]
            field[comp, land, :width, base:] = jnp.where(kept, packed, 0.0)
            packed = pltpu.roll(packed, 128 - tail, 1)
            field[comp, land + 1, :width, base:] = jnp.where(kept, packed, 0.0)

    def drag(field):
        cells = field[0, 2 : depth + 2, :width].reshape(area, lanes)
        head, rest = halves(cells)
        table = where_lev[...]
        picked = (dot(head, table) + dot(rest, table)) * where_row[...]
        values = jnp.sum(picked, axis=0, keepdims=True) + WIND
        turbs = where_turb[...]
        sums = jnp.sum(turbs * values, axis=1, keepdims=True)
        counts = jnp.sum(turbs, axis=1, keepdims=True)
        mean = sums / jnp.maximum(counts, 1.0)
        thrust = (-0.5 * THRUST * STEP) * mean * jnp.abs(mean)
        per_slot = jnp.sum(turbs * thrust, axis=0, keepdims=True)
        head, rest = halves(where_row[...] * per_slot)
        last = ((1,), (1,))
        force[...] = (dot(head, table, last) + dot(rest, table, last)).reshape(depth, width, lanes)

    def ahead(value, axis):
        return pltpu.roll(value, value.shape[axis] - 1, axis)

    def behind(value, axis):
        return pltpu.roll(value, 1, axis)

    def eddy_slab(field, j, size):
        along, across_y, up = [], [], []
        for comp in range(comps):
            value = field[comp, j]
            along.append((ahead(value, 0) - behind(value, 0))[:size])
            across_y.append(field[comp, j + 1, :size] - field[comp, j - 1, :size])
            up.append(ahead(value[:size], 1) - behind(value[:size], 1))
        shear = 0.0
        for pair in (along[1] + across_y[0], along[2] + up[0], across_y[2] + up[1]):
            shear = shear + pair * pair
        square = along[0] * along[0] + across_y[1] * across_y[1] + up[2] * up[2] + 0.5 * shear
        eddy[j - 1, :size] = (0.5 * STEP * SMAG * math.sqrt(0.5)) * jnp.sqrt(square)

    def factors(speed, viscous):
        return speed + viscous, speed - viscous

    def flux(pair, low_f, high_f):
        return pair[0] * low_f + pair[1] * high_f

    quarter = 0.25 * STEP

    def span_flux(field, j):
        speed = quarter * (field[1, j, :width] + field[1, j + 1, :width])
        pair = factors(speed, eddy[j - 1, :width] + eddy[j, :width])
        return tuple(
            flux(pair, field[comp, j, :width], field[comp, j + 1, :width]) for comp in range(comps)
        )

    def rates(field, start, size, store):
        def slab(step, below):
            j = start + step
            above = span_flux(field, j)
            viscous = eddy[j - 1]
            whole = field[0, j]
            next_u = ahead(whole, 0)
            along = factors(
                quarter * (whole + next_u) + (2.0 * quarter * WIND), viscous + ahead(viscous, 0)
            )
            inner_h = viscous[:width]
            lift = field[2, j, :width]
            next_w = ahead(lift, 1)
            rising = factors(quarter * (lift + next_w), inner_h + ahead(inner_h, 1))
            for comp in range(comps):
                value = field[comp, j]
                face = flux(along, value, next_u if comp == 0 else ahead(value, 0))
                total = (face - behind(face, 0))[:width] + (above[comp] - below[comp])
                mid = value[:width]
                face = flux(rising, mid, next_w if comp == 2 else ahead(mid, 1))
                total = total + (face - behind(face, 1))
                change = force[j - 2] - total if comp == 0 else -total
                store(comp, j, mid + change)
            return above

        lax.fori_loop(0, size, slab, span_flux(field, start - 1), unroll=2)

    first = 1 - column % 2

    def section(stage, field, store, leave, settled=lambda: None):
        drag(field)
        lines_in(field, stage)

        @pl.loop(3, depth + 1, unroll=2)
        def _(j):
            eddy_slab(field, j, width + 8)

        rates(field, 4, depth - 4, store)
        settled()

        @pl.loop(0, 2)
        def _(turn):
            side = (turn + first) % 2
            side_in(field, stage, side)

            eddy_slab(field, 1 + (depth + 1) * side, width)
            eddy_slab(field, 2 + (depth - 1) * side, width + 8)

            rates(field, 2 + (depth - 2) * side, 2, store)
            leave(side)

    def to_next(target, share):
        def store(comp, j, value):
            if share < 1.0:
                value = (1.0 - share) * stage_one[comp, j, :width] + share * value
            target[comp, j, :width] = jnp.where(inside, value, 0.0)
        return store

    def to_output(comp, j, value):
        value = stage_one[comp, j, :width] * (1.0 / 3.0) + (2.0 / 3.0) * value
        farm_v[comp, j - 2] = value[:, :levels]

    section(0, stage_one, to_next(stage_two, 1.0), lambda side: send_side(stage_two, 2, 1, 2, stage_two, 0, 1 - side))
    send_lines(stage_two, 2, 1, 2, stage_two, 0)
    outs = []
    for comp in range(comps):
        farm_v[comp] = fringe[comp][:, :, :levels]
    for y in range(depth):
        outs.append(pltpu.make_async_copy(farm_v.at[:, y], pre_new.at[:, :, y], out_sem.at[0, y]))
        outs[-1].start()
    section(1, stage_two, to_next(stage_three, 0.25), lambda side: send_side(stage_three, 2, 2, 3, stage_three, 0, 1 - side))
    send_lines(stage_three, 2, 2, 3, stage_three, 0)

    def result(y):
        return pltpu.make_async_copy(farm_v.at[:, y], farm_new.at[:, :, y], out_sem.at[1, y])

    def inner_rows():
        for y in range(2, depth - 2):
            result(y).start()

    def outer_rows(side):
        for half in (0, 1):
            result((depth - 2) * side + half).start()

    for copy in outs:
        copy.wait()
    section(2, stage_three, to_output, outer_rows, inner_rows)
    for index in range(len(chunks)):
        sent(0, index, send)
        sent(1, index, send_two)
    for stage, field in ((1, stage_two), (2, stage_three)):
        copies = line_copies(field, 2, stage, stage + 1, field, 0)
        for side in (0, 1):
            copies += side_copies(field, 2, stage, stage + 1, field, 0, side)
        for copy, remote in copies:
            if remote:
                copy.wait_send()

    @pl.when(row >= shift)
    def _():
        tile_sent(fringe, 1, -shift)
        for index in range(len(chunks)):
            copy, remote = relay(index)
            if remote:
                copy.wait_send()

    @pl.when(row >= filled)
    def _():
        tile_sent(own, 0, 0)

    for y in range(depth):
        result(y).wait()


def write_out(farm, pre, farm_new, pre_new, hold, in_sem, out_sem):
    pieces = []
    for place, (source, target) in enumerate(((pre, pre_new), (farm, farm_new))):
        for comp in range(source.shape[0]):
            seat = hold.at[place, comp]
            pieces.append((
                pltpu.make_async_copy(source.at[comp], seat, in_sem.at[place, comp]),
                pltpu.make_async_copy(seat, target.at[comp], out_sem.at[place, comp]),
            ))
    for copy, _ in pieces:
        copy.start()
    for copy, onward in pieces:
        copy.wait()
        onward.start()
    for _, onward in pieces:
        onward.wait()


def shards(across, spanwise, farm, pre, turb_cell, turb_slot, disk_mask):
    comps, width, depth, levels = pre.shape
    count = across * spanwise
    area = width * depth
    slots = turb_cell.shape[-1]
    lanes = -(-(levels + 2) // 128) * 128
    groups = -(-levels // count)
    tables = [jnp.asarray(t) for t in spectral_tables(across, spanwise, width, depth, levels, lanes)]
    anywhere = pl.BlockSpec(memory_space=pl.ANY)
    f32 = jnp.float32

    def vmem(*shape, dtype=f32):
        return pltpu.VMEM(shape, dtype)

    def sems(*shape):
        return pltpu.SemaphoreType.DMA(shape)

    modes = vmem(groups * comps, count, area)
    cells = vmem(comps, depth, width, lanes)
    padded = vmem(comps, depth + 4, width + 8, lanes)
    results = [jax.ShapeDtypeStruct(farm.shape, f32), jax.ShapeDtypeStruct(pre.shape, f32)]
    farm_new, pre_new = pl.pallas_call(
        functools.partial(step_body, across, spanwise),
        out_shape=results,
        in_specs=[anywhere] * (5 + len(tables)),
        out_specs=[anywhere] * 2,
        scratch_shapes=[
            vmem(comps, area, levels),
            vmem(comps, depth, width, levels),
            vmem(3, 1, slots, dtype=jnp.int32),
            *[vmem(*t.shape, dtype=t.dtype) for t in tables[:-1]],
            vmem(*tables[-1].shape[1:]),
            modes, modes, modes, modes, modes,
            cells, cells, padded, padded, padded,
            vmem(4, 2, comps, 2 * (lanes // 128) - 1, width, 128),
            vmem(3, 2, comps, 2 * (lanes // 128) - 1, width, 128),
            vmem(depth + 2, width + 8, lanes),
            vmem(depth, width, lanes),
            vmem(area, slots),
            vmem(lanes, slots, dtype=jnp.bfloat16),
            vmem(TURB, slots),
            sems(comps + 2 + 10 + depth),
            sems(2, len(SHARES)),
            sems(2, len(SHARES)),
            sems(len(SHARES)),
            sems(len(SHARES)),
            sems(4, 10),
            sems(3, 10),
            pltpu.SemaphoreType.REGULAR((2,)),
            sems(2, depth),
        ],
        compiler_params=pltpu.CompilerParams(collective_id=0, has_side_effects=True),
        name="step",
    )(
        pre.reshape(comps, area, levels), farm,
        turb_cell.reshape(1, slots), turb_slot.reshape(1, slots), disk_mask.reshape(1, slots),
        *tables,
    )
    return pl.pallas_call(
        write_out,
        out_shape=results,
        in_specs=[anywhere] * 2,
        out_specs=[anywhere] * 2,
        scratch_shapes=[vmem(2, comps, width, depth, levels), sems(2, comps), sems(2, comps)],
        name="write_out",
    )(farm_new, pre_new)


def solution(mesh):
    across, spanwise = mesh.shape["gx"], mesh.shape["gy"]
    return jax.shard_map(
        functools.partial(shards, across, spanwise),
        mesh=mesh,
        in_specs=(
            P(None, "gx", "gy", None),
            P(None, "gx", "gy", None),
            P("gx", "gy", None),
            P("gx", "gy", None),
            P("gx", "gy", None),
        ),
        out_specs=(P(None, "gx", "gy", None), P(None, "gx", "gy", None)),
        check_vma=False,
    )
```
